32 devices in a mesh: fsdp: 4 (over y, x), ctx: 4 (over z), tp: 2 (over core).
Axes of the slice: x: 2, y: 2, z: 4, core: 2. Of those that a mesh axis runs over, the one named last changes fastest.
Arguments:
- inputs: bfloat16 [4, 1024, 2048], P('fsdp', 'ctx'), may hold values from -6 to 6
- positions: int32 [4, 1024], P('fsdp', 'ctx'), may hold values from 0 to 1535, as said below
- blocks: int32 [4, 1024], P('fsdp', 'ctx'), may hold values from 0 to 7, never falling along the last dimension, each value on 1 to 256 neighbouring positions
- cotangent: bfloat16 [4, 1024, 2048], P('fsdp', 'ctx'), may hold values from -6 to 6
- attn_gain: bfloat16 [2048], P('fsdp'), may hold values from 0.099609375 to 1.8984375
- w_query: bfloat16 [2048, 2048], P('fsdp', 'tp'), may hold values from -0.125 to 0.125
- w_key: bfloat16 [2048, 256], P('fsdp', 'tp'), may hold values from -0.125 to 0.125
- w_value: bfloat16 [2048, 256], P('fsdp', 'tp'), may hold values from -0.125 to 0.125
- w_out: bfloat16 [2048, 2048], P('tp', 'fsdp'), may hold values from -1 to 1
- mlp_gain: bfloat16 [2048], P('fsdp'), may hold values from 0.099609375 to 1.8984375
- w_gate: bfloat16 [2048, 5632], P('fsdp', 'tp'), may hold values from -0.125 to 0.125
- w_up: bfloat16 [2048, 5632], P('fsdp', 'tp'), may hold values from -0.125 to 0.125
- w_down: bfloat16 [5632, 2048], P('tp', 'fsdp'), may hold values from -0.078125 to 0.078125
Outputs:
- output: bfloat16 [4, 1024, 2048], P('fsdp', 'ctx')
- input_grad: float32 [4, 1024, 2048], P('fsdp', 'ctx')
- attn_gain_grad: float32 [2048], P('fsdp')
- query_grad: float32 [2048, 2048], P('fsdp', 'tp')
- key_grad: float32 [2048, 256], P('fsdp', 'tp')
- value_grad: float32 [2048, 256], P('fsdp', 'tp')
- out_grad: float32 [2048, 2048], P('tp', 'fsdp')
- mlp_gain_grad: float32 [2048], P('fsdp')
- gate_grad: float32 [2048, 5632], P('fsdp', 'tp')
- up_grad: float32 [2048, 5632], P('fsdp', 'tp')
- down_grad: float32 [5632, 2048], P('tp', 'fsdp')
The draws below stay inside these ranges and needn't reach their ends.
Inputs may be any that keep to these rules, and one draw needn't show every extreme that they name: `positions`: positions start at 0 and rise by 1 or 2 from each token to the next along a sequence; in every sequence exactly 512 of these steps are 2. `blocks`: block ids never fall along a sequence; every block holds 1 to 256 tokens.
All inputs are finite; a program needn't handle non-finite values.
Results may differ from the reference program's by a relative error of at most 0.023.
Values may be sent and summed in bfloat16 or wider, within the bound.
A program may use at most 320 MiB of HBM per device.

```python
import math
import jax
import jax.numpy as jnp
import numpy as np
from jax import lax

D = 2048
H = 32
KV = 4
HD = 64
FF = 5632
BLOCK = 256
SEQS = 4
LEN = 1024


def draw_positions(key, part):
    row_keys = jax.random.split(key, SEQS)

    def one_row(row_key):
        order = jax.random.permutation(row_key, LEN - 1)
        steps_drawn = 1 + (order < LEN // 2).astype(jnp.int32)
        return jnp.concatenate([jnp.zeros((1,), jnp.int32), jnp.cumsum(steps_drawn).astype(jnp.int32)])
    return jax.vmap(one_row)(row_keys).astype(jnp.int32)


def levels(own_key, shape, shards, low, high):
    def one(dim, blocks):
        steps = jax.random.uniform(jax.random.fold_in(jax.random.fold_in(own_key, 6), dim), (blocks,), jnp.float32, low / len(shards), high / len(shards))
        return jnp.repeat(jnp.exp(steps), shape[dim] // blocks).reshape((-1,) + (1,) * (len(shape) - dim - 1))

    factor_of = one(*shards[0])
    for cut in shards[1:]:
        factor_of = factor_of * one(*cut)
    return factor_of


def length_profile(number_of, total, most, lean):
    weights = [(1 << 20) // math.isqrt(grade ** lean) + 1 for grade in range(2, number_of + 1)]
    surplus, given = total - most - (number_of - 1), [1] * (number_of - 1)
    while surplus > 0:
        free = [i for i in range(number_of - 1) if given[i] < most]
        whole, remaining = sum([weights[i] for i in free]), surplus
        for i in free:
            addition = min(most - given[i], max(1, remaining * weights[i] // whole), surplus)
            given[i] = given[i] + addition
            surplus = surplus - addition
    return np.array([most] + given)


def uneven(key, count, total, most, skew):
    if count == 2:
        one = jax.random.randint(key, (), max(1, total - most), min(most, total - 1) + 1)
        return jnp.stack([one, total - one])
    sizes = jnp.asarray(length_profile(count, total, most, skew), jnp.int32)
    couples = (count - 1) // 2
    donor, sink = sizes[1:1 + 2 * couples:2], sizes[2:2 + 2 * couples:2]
    margin = jnp.minimum(donor - 1, most - sink)
    passed = jax.random.randint(jax.random.fold_in(key, 1), (couples,), 0, 1 << 20) % (margin + 1)
    sizes = sizes.at[1:1 + 2 * couples:2].set(donor - passed).at[2:2 + 2 * couples:2].set(sink + passed)
    return sizes[jax.random.permutation(jax.random.fold_in(key, 2), count)]


def centred(stream_key, shape, width, limit, cuts=(), kind=jnp.bfloat16):
    array = width * jax.random.normal(stream_key, shape, jnp.float32)
    if cuts:
        array = array * levels(stream_key, shape, cuts, -0.22, 0.18)
    return jnp.clip(array, -limit, limit).astype(kind)


def setup_inputs(seed: int = 0) -> dict:
    streams_of = jax.random.split(jax.random.key(seed), 14)
    return {
        "inputs": centred(streams_of[0], (SEQS, LEN, D), 1.0, 6.0, ((0, 4), (1, 4))),
        "positions": draw_positions(jax.random.fold_in(streams_of[13], 71), 0),
        "blocks": jax.vmap(lambda own: jnp.searchsorted(jnp.cumsum(uneven(own, 2 * LEN // BLOCK, LEN, BLOCK, 1)), jnp.arange(LEN), side="right"))(jax.random.split(streams_of[2], SEQS)).reshape((SEQS, LEN)).astype(jnp.int32),
        "cotangent": centred(streams_of[3], (SEQS, LEN, D), 1.0, 6.0, ((0, 4), (1, 4))),
        "attn_gain": jnp.clip(1.0 + 0.18 * jax.random.normal(streams_of[4], (D,), jnp.float32), 0.099609375, 1.8984375).astype(jnp.bfloat16),
        "w_query": centred(streams_of[5], (D, H * HD), D ** -0.5, 0.125, ((0, 4), (1, 2))),
        "w_key": centred(streams_of[6], (D, KV * HD), D ** -0.5, 0.125, ((0, 4), (1, 2))),
        "w_value": centred(streams_of[7], (D, KV * HD), D ** -0.5, 0.125, ((0, 4), (1, 2))),
        "w_out": centred(streams_of[8], (H * HD, D), (max(1, H * HD * 16 // LEN)) ** -0.5, 1.0, ((0, 2), (1, 4))),
        "mlp_gain": jnp.clip(1.0 + 0.18 * jax.random.normal(streams_of[9], (D,), jnp.float32), 0.099609375, 1.8984375).astype(jnp.bfloat16),
        "w_gate": centred(streams_of[10], (D, FF), D ** -0.5, 0.125, ((0, 4), (1, 2))),
        "w_up": centred(streams_of[11], (D, FF), D ** -0.5, 0.125, ((0, 4), (1, 2))),
        "w_down": centred(streams_of[12], (FF, D), FF ** -0.5, 0.078125, ((0, 2), (1, 4))),
    }


@jax.custom_vjp
def low(v):
    return lax.optimization_barrier(v.astype(jnp.bfloat16)).astype(jnp.float32)

@jax.custom_vjp
def low_back(v):
    return v

def low_keep(v):
    return (low(v), None)

def low_pass(kept, grad):
    return (grad,)

def back_keep(v):
    return (v, None)

def back_low(kept, grad):
    return (low(grad),)
low.defvjp(low_keep, low_pass)
low_back.defvjp(back_keep, back_low)
EPSILON = 1e-05
NEGATIVE = -1e+30
HIGHEST = lax.Precision.HIGHEST

def product(left, right):
    return jnp.dot(left, right, precision=HIGHEST, preferred_element_type=jnp.float32)

def rms_norm(values, gain):
    scale = lax.rsqrt(lax.optimization_barrier(jnp.mean(values * values, axis=-1, keepdims=True)) + EPSILON)
    return values * scale * gain

def angles(positions):
    half_size = HD // 2
    frequency = jnp.exp(jnp.arange(half_size, dtype=jnp.float32) * (-2.0 * math.log(10000.0) / HD))
    turned = positions.astype(jnp.float32)[:, None] * frequency[None, :]
    return (jnp.cos(turned)[:, None, :], jnp.sin(turned)[:, None, :])

def rotate(values, cosine, sine_turn):
    half_size = values.shape[-1] // 2
    first_half = values[..., :half_size]
    second_half = values[..., half_size:]
    return jnp.concatenate([first_half * cosine - second_half * sine_turn, second_half * cosine + first_half * sine_turn], axis=-1)

def attention(query_rot, key_rot, value_low, block_ids):
    length = query_rot.shape[0]
    rows_block = math.gcd(length, 512)
    blocks_count = length // rows_block
    factor = 1.0 / math.sqrt(HD)

    def one_block(pieces):
        query_part, ids_part = pieces
        query_four = query_part.reshape(rows_block, KV, H // KV, HD)
        scores = jnp.einsum('tkgd,skd->kgts', query_four, key_rot, precision=HIGHEST) * factor
        scores = low_back(scores)
        allowed = block_ids[None, :] <= ids_part[:, None]
        scores = jnp.where(allowed, scores, NEGATIVE)
        weights = low(jax.nn.softmax(scores, axis=-1))
        mixed = jnp.einsum('kgts,skd->tkgd', weights, value_low, precision=HIGHEST)
        return mixed.reshape(rows_block, H * HD)
    parts = lax.map(jax.checkpoint(one_block), (query_rot.reshape(blocks_count, rows_block, H, HD), block_ids.reshape(blocks_count, rows_block)))
    return parts.reshape(length, H * HD)

def layer(inputs_row, attn_gain, w_query, w_key, w_value, w_out, mlp_gain, w_gate, w_up, w_down, positions, block_ids):
    length = inputs_row.shape[0]
    normed_one = low(rms_norm(inputs_row, attn_gain))
    query_pre = low_back(product(normed_one, w_query)).reshape(length, H, HD)
    key_pre = low_back(product(normed_one, w_key)).reshape(length, KV, HD)
    value_low = low(low_back(product(normed_one, w_value))).reshape(length, KV, HD)
    cosine, sine_turn = angles(positions)
    query_rot = low(rotate(query_pre, cosine, sine_turn))
    key_rot = low(rotate(key_pre, cosine, sine_turn))
    mixed = low(low_back(attention(query_rot, key_rot, value_low, block_ids)))
    hidden = inputs_row + low_back(product(mixed, w_out))
    normed_two = low(rms_norm(hidden, mlp_gain))
    gate = low_back(product(normed_two, w_gate))
    up_proj = low_back(product(normed_two, w_up))
    activation = low(jax.nn.silu(gate) * up_proj)
    return hidden + low_back(product(activation, w_down))

def reference(inputs, positions, blocks, cotangent, attn_gain, w_query, w_key, w_value, w_out, mlp_gain, w_gate, w_up, w_down):
    weights = tuple((weight.astype(jnp.float32) for weight in (attn_gain, w_query, w_key, w_value, w_out, mlp_gain, w_gate, w_up, w_down)))

    def one_sequence(totals, pieces):
        inputs_row, place_row, ids_row, back_row = pieces

        def forward(row_values, *params):
            return layer(row_values, *params, place_row, ids_row)
        result, pullback = jax.vjp(forward, inputs_row.astype(jnp.float32), *weights)
        grads = pullback(back_row.astype(jnp.float32))
        totals = tuple((left + right for left, right in zip(totals, grads[1:])))
        return (totals, (result.astype(jnp.bfloat16), grads[0]))
    start = tuple((jnp.zeros(weight.shape, jnp.float32) for weight in weights))
    totals, (outputs, input_grads) = lax.scan(one_sequence, start, (inputs, positions, blocks, cotangent))
    return (outputs, input_grads, totals[0], totals[1], totals[2], totals[3], totals[4], totals[5], totals[6], totals[7], totals[8])
```

```python
import functools
import math

import jax
import jax.numpy as jnp
from jax import lax
from jax.experimental import pallas as pl
from jax.experimental.pallas import tpu as pltpu
from jax.sharding import PartitionSpec as P

HD = 64
EPSILON = 1e-05
NEGATIVE = -1e30
BF = jnp.bfloat16
F32 = jnp.float32


def dot(a, b, ca, cb):
    return lax.dot_general(a, b, (((ca,), (cb,)), ((), ())), preferred_element_type=F32)


def angles(positions):
    half = HD // 2
    frequency = jnp.exp(jnp.arange(half, dtype=F32) * (-2.0 * math.log(10000.0) / HD))
    turned = positions.astype(F32)[:, None] * frequency[None, :]
    return jnp.cos(turned)[:, None, :], jnp.sin(turned)[:, None, :]


def rotate(values, cosine, sine):
    half = HD // 2
    a, b = values[..., :half], values[..., half:]
    return jnp.concatenate([a * cosine - b * sine, b * cosine + a * sine], axis=-1)


def gated(values, after):
    return lax.optimization_barrier((values, after))[0]


def local(n, m, inputs, positions, blocks, cotangent, attn_gain, w_query, w_key, w_value, w_out, mlp_gain, w_gate, w_up, w_down):
    f = lax.axis_index("fsdp")
    z = lax.axis_index("ctx")
    t = lax.axis_index("tp")
    tokens, width = inputs.shape[1:]
    half = width // 2
    peers = range(1, n)

    def plane(x, k):
        return x if k == 0 else lax.ppermute(x, "fsdp", [(i, i ^ k) for i in range(n)])

    def column(x, k):
        return x if k == 0 else lax.ppermute(x, "ctx", [(i, i ^ k) for i in range(m)])

    def swap(x):
        return lax.ppermute(x, "tp", [(0, 1), (1, 0)])

    def part(x, index, axis):
        size = x.shape[axis] // n
        return lax.dynamic_slice_in_dim(x, index * size, size, axis)

    def mine(x, which):
        return lax.dynamic_slice_in_dim(x, which * half, half, x.ndim - 1)

    def place(pieces, axis):
        size = pieces[0].shape[axis]
        shape = list(pieces[0].shape)
        shape[axis] = size * n
        whole = jnp.zeros(shape, pieces[0].dtype)
        for k in range(n):
            whole = lax.dynamic_update_slice_in_dim(whole, pieces[k], (f ^ k) * size, axis)
        return whole

    def join(own, other):
        return jnp.where(t == 0, jnp.concatenate([own, other], -1), jnp.concatenate([other, own], -1))

    def gather(x):
        rows = jnp.concatenate([plane(x, k) for k in range(n)], 0)
        return join(rows, swap(rows))

    def scatter(partial):
        own = mine(partial, t) + swap(mine(partial.astype(BF), 1 - t)).astype(F32)
        low = own.astype(BF)
        total = own[:tokens]
        for k in peers:
            total = total + plane(low[k * tokens : (k + 1) * tokens], k).astype(F32)
        return total

    def row_mean(own):
        own = jnp.sum(own, -1)
        return ((own + swap(own)) / width)[:, None]

    x = inputs[0].astype(F32)
    gains = jnp.stack([attn_gain, mlp_gain])
    gains = place([plane(gains, k) for k in range(n)], 1).astype(F32)
    marks = jnp.stack([positions[0], blocks[0]])
    marks = [plane(marks, k) for k in range(n)]
    place_rows = jnp.concatenate([mk[0] for mk in marks])
    query_ids = jnp.stack([mk[1] for mk in marks])
    scale_one = lax.rsqrt(jnp.mean(x * x, axis=-1, keepdims=True) + EPSILON)
    x_half = mine(x, t)
    hat_one = x_half * scale_one
    gain_one, gain_two = mine(gains[0:1], t), mine(gains[1:2], t)
    xn_one = gather((hat_one * gain_one).astype(BF))

    heads = w_query.shape[1] // HD // n
    cols = heads * HD
    kv_pair = jnp.concatenate([w_key, w_value], 1)
    kv_heads = w_key.shape[1] // HD
    w_qkv = place([plane(jnp.concatenate([part(w_query, f ^ k, 1), kv_pair], 1), k) for k in range(n)], 0)
    wo = gated(w_out, xn_one)
    wo = place([plane(part(wo, f ^ k, 0), k) for k in range(n)], 1)
    gate_up = gated((w_gate, w_up), xn_one)
    gate_up = [plane(jnp.stack([part(gate_up[0], f ^ k, 1), part(gate_up[1], f ^ k, 1)]), k) for k in range(n)]
    wg = place([g[0] for g in gate_up], 0)
    wu = place([g[1] for g in gate_up], 0)

    qkv = dot(xn_one, w_qkv, 1, 0)
    cosine, sine = angles(place_rows)
    kv_here = (heads * f) // ((w_query.shape[1] // HD) // kv_heads)

    def pick(both):
        out = both[:, :HD]
        for g in range(1, kv_heads):
            out = jnp.where(kv_here == g, both[:, g * HD : (g + 1) * HD], out)
        return out

    kw = kv_heads * HD
    query = rotate(qkv[:, :cols].reshape(-1, heads, HD), cosine, sine).astype(BF)
    key = rotate(pick(qkv[:, cols : cols + kw])[:, None, :], cosine, sine)[:, 0, :].astype(BF)
    value = pick(qkv[:, cols + kw :]).astype(BF)
    key_value = jnp.concatenate([key, value], 1).reshape(n, tokens, 2 * HD)
    kv_all = jnp.concatenate([column(key_value, k) for k in range(m)], 1)
    ids_all = jnp.concatenate([column(query_ids, k) for k in range(m)], 1)
    keys, values = kv_all[..., :HD], kv_all[..., HD:]
    factor = 1.0 / math.sqrt(HD)
    query = query.reshape(n, tokens, heads, HD)
    allowed = (ids_all[:, None, :] <= query_ids[:, :, None])[:, None]
    scores = jnp.einsum("nthd,nsd->nhts", query, keys, preferred_element_type=F32) * factor
    scores = jnp.where(allowed, scores, NEGATIVE)
    top = jnp.max(scores, -1, keepdims=True)
    raw = jnp.where(allowed, jnp.exp(scores - top), 0.0)
    weights = raw / jnp.sum(raw, -1, keepdims=True)
    weights_low = weights.astype(BF)
    attended = jnp.einsum("nhts,nsd->nthd", weights_low, values, preferred_element_type=F32)
    attended_low = attended.astype(BF).reshape(n * tokens, cols)

    hidden = x_half + scatter(dot(attended_low, wo, 1, 0))
    scale_two = lax.rsqrt(row_mean(hidden * hidden) + EPSILON)
    hat_two = hidden * scale_two
    xn_two = gather((hat_two * gain_two).astype(BF))
    cot = gather(gated(mine(cotangent[0], t), wg))
    wd = gated(w_down, wg)
    wd = place([plane(part(wd, f ^ k, 0), k) for k in range(n)], 1)
    gate = dot(xn_two, wg, 1, 0)
    up = dot(xn_two, wu, 1, 0)
    sigma = jax.nn.sigmoid(gate)
    silu = gate * sigma
    act = (silu * up).astype(BF)
    dact = dot(cot, wd, 1, 1)
    dgate = (dact * up * sigma * (1.0 + gate * (1.0 - sigma))).astype(BF)
    dup = (dact * silu).astype(BF)

    def reduce(piece):
        if m != 4:
            return lax.psum(piece, "ctx")
        one = (piece.astype(F32) + lax.ppermute(piece, "ctx", [(0, 1), (3, 2)]).astype(F32)).astype(BF)
        two = (one.astype(F32) + lax.ppermute(one, "ctx", [(1, 2), (2, 1)]).astype(F32)).astype(BF)
        three = lax.ppermute(two, "ctx", [(1, 0), (2, 3)])
        return jnp.where((z == 0) | (z == 3), three, two)

    def share(grad, axis):
        low = grad.astype(BF)
        return [plane(part(low, f ^ k, axis), k) for k in range(n)]

    down_parts = [reduce(p) for p in share(dot(act, cot, 0, 0), 1)]
    gate_parts = [reduce(p) for p in share(dot(xn_two, dgate, 0, 0), 0)]
    up_parts = [reduce(p) for p in share(dot(xn_two, dup, 0, 0), 0)]
    d_two = scatter(dot(dgate, wg, 1, 1) + dot(dup, wu, 1, 1))
    out_half = (hidden + scatter(dot(act, wd, 1, 0))).astype(BF)
    output = join(out_half, swap(out_half))
    gain_two_grad = jnp.sum(d_two * hat_two, 0)
    e_two = d_two * gain_two
    d_hidden = mine(cotangent[0], t).astype(F32) + scale_two * (e_two - hat_two * row_mean(e_two * hat_two))
    dhb = gather(d_hidden.astype(BF))
    out_parts = [reduce(p) for p in share(dot(attended_low, dhb, 0, 0), 1)]

    d_att = dot(dhb, wo, 1, 1).astype(BF).reshape(n, tokens, heads, HD)
    delta = jnp.einsum("nthd,nthd->nht", d_att.astype(F32), attended)
    d_weights = jnp.einsum("nthd,nsd->nhts", d_att, values, preferred_element_type=F32)
    d_scores = (weights * (d_weights - delta[..., None])).astype(BF)
    dv = jnp.einsum("nhts,nthd->nsd", weights_low, d_att, preferred_element_type=F32)
    dk = jnp.einsum("nhts,nthd->nsd", d_scores, query, preferred_element_type=F32) * factor
    dq = jnp.einsum("nhts,nsd->nthd", d_scores, keys, preferred_element_type=F32) * factor
    d_kv = jnp.concatenate([dk, dv], -1).reshape(n, m, tokens, 2 * HD)
    d_low = d_kv.astype(BF)
    d_kv_own = d_kv[:, 0]
    for k in range(1, m):
        d_kv_own = d_kv_own + column(d_low[:, k], k).astype(F32)
    d_kv_own = d_kv_own.reshape(n * tokens, 2 * HD)
    dq = rotate(dq.reshape(n * tokens, heads, HD), cosine, -sine).reshape(n * tokens, cols)
    dk = rotate(d_kv_own[:, None, :HD], cosine, -sine)[:, 0, :]
    d_qkv = jnp.concatenate([dq, dk, d_kv_own[:, HD:]], 1).astype(BF)
    w_here = jnp.concatenate([w_qkv[:, :cols], pick(w_qkv[:, cols : cols + kw]), pick(w_qkv[:, cols + kw :])], 1)
    d_one = scatter(dot(d_qkv, w_here, 1, 1))
    qkv_parts = share(dot(xn_one, d_qkv, 0, 0), 0)
    key_parts, value_parts = [0.0] * kv_heads, [0.0] * kv_heads
    for k in range(n):
        owner = (heads * (f ^ k)) // ((w_query.shape[1] // HD) // kv_heads)
        piece = qkv_parts[k].astype(F32)
        for g in range(kv_heads):
            key_parts[g] = key_parts[g] + jnp.where(owner == g, piece[:, cols : cols + HD], 0.0)
            value_parts[g] = value_parts[g] + jnp.where(owner == g, piece[:, cols + HD :], 0.0)
    small = reduce(jnp.concatenate(key_parts + value_parts, 1).astype(BF)).astype(F32)
    query_parts = [reduce(p[:, :cols]) for p in qkv_parts]
    gain_one_grad = jnp.sum(d_one * hat_one, 0)
    e_one = d_one * gain_one
    in_half = d_hidden + scale_one * (e_one - hat_one * row_mean(e_one * hat_one))
    input_grad = join(in_half, swap(in_half))
    gain_grads = jnp.stack([gain_one_grad, gain_two_grad])
    nothing = jnp.zeros_like(gain_grads)
    gain_grads = jnp.where(t == 0, jnp.concatenate([gain_grads, nothing], 1), jnp.concatenate([nothing, gain_grads], 1))
    gain_grads = part(lax.psum(gain_grads, ("fsdp", "ctx", "tp")), f, 1)

    def settle(pieces, axis):
        return place(pieces, axis).astype(F32)

    return (
        output[None],
        input_grad[None],
        gain_grads[0],
        settle(query_parts, 1),
        small[:, :kw],
        small[:, kw:],
        settle(out_parts, 0),
        gain_grads[1],
        settle(gate_parts, 1),
        settle(up_parts, 1),
        settle(down_parts, 0),
    )


T, W, H, TILE = 256, 2048, 1024, 128
MAIN, WIN = 640, 768
GRADS = (("d", 2816, 512), ("g", 512, 2816), ("u", 512, 2816), ("o", 1024, 512), ("q", 512, 1024), ("k", 512, 256))
CHUNKS = [
    (name, r, c, min(512, rows - r), min(512, cols - c))
    for name, rows, cols in GRADS
    for r in range(0, rows, 512)
    for c in range(0, cols, 512)
]
MESH = pl.DeviceIdType.MESH


def nn(a, b):
    return lax.dot_general(a, b, (((1,), (0,)), ((), ())), preferred_element_type=F32)


def nt(a, b):
    return lax.dot_general(a, b, (((1,), (1,)), ((), ())), preferred_element_type=F32)


def tn(a, b):
    return lax.dot_general(a, b, (((0,), (0,)), ((), ())), preferred_element_type=F32)


def flip(a, k):
    return (a % 2 + k % 2) % 2 + 2 * ((a // 2 + k // 2) % 2)


def layer_kernel(*refs):
    names = iter(refs)

    def take(count):
        return [next(names) for _ in range(count)]

    x_in, table_in, gains_in, cot_in, wq, wk, wv, wo, wg, wu, wd = take(11)
    out_ref, in_grad_ref, gain_ref = take(3)
    first, left, cross, total = ({name: next(names) for name, _, _ in GRADS} for _ in range(4))
    (x1, x2, ct, dh, w_qkv, w_o, w_g, w_u, w_d, act, dg, du, q_buf, kv_all, ob) = take(15)
    (ps, pr, rr, yo, hid, d_hid, xv, tb, ga, ids, r1s, r2s, ss_own, ss_other, lse, bias) = take(16)
    (gs_d, kv_g, la, lb, ring, tt, d_kv, d_kv_recv, out_s, g_sum, g_plane, g_column, g_whole) = take(13)
    send_sem, recv_sem, local_sem, credit = take(4)
    f, z, t = lax.axis_index("fsdp"), lax.axis_index("ctx"), lax.axis_index("tp")
    sems = iter(range(10**6))
    drains = []

    def al(v, by):
        return pl.multiple_of(v, by)

    def plane(k):
        return (flip(f, k), z, t)

    def column(k):
        return (f, flip(z, k), t)

    core = (f, z, 1 - t)
    rows_f = pl.ds(al(f * T, T), T)
    half = pl.ds(al(t * H, H), H)
    rest = pl.ds(al((1 - t) * H, H), H)

    def rows_of(b):
        return pl.ds(al(b * T, T), T)

    def remote(src, dst, s, device):
        return pltpu.make_async_remote_copy(src_ref=src, dst_ref=dst, send_sem=send_sem.at[s], recv_sem=recv_sem.at[s], device_id=device, device_id_type=MESH)

    def here(src, dst, s):
        return pltpu.make_async_copy(src, dst, local_sem.at[s])

    local_count = iter(range(10**6))

    lx = here(x_in.at[0], xv, next(local_count))
    lx.start()
    lc = here(cot_in.at[0], ct.at[rows_f, :], next(local_count))
    lc.start()
    lh = here(cot_in.at[0, :, half], out_s, next(local_count))
    lh.start()
    lt = here(table_in, tb.at[f], next(local_count))
    lt.start()
    lg = here(gains_in, ga.at[:, pl.ds(al(f * 512, 512), 512)], next(local_count))
    lg.start()

    def starts(r):
        return (11 * r + 1) // 2

    def weight_moves(k, s0, wait_side):
        r = flip(f, k)
        mine = f if not wait_side else r
        rows = pl.ds(al(mine * 512, 512), 512)
        begin = al(starts(r) * TILE, TILE) if not wait_side else al(starts(f) * TILE, TILE)
        tail = al(begin + MAIN, TILE)
        col = al((r if not wait_side else f) * T, T)
        return {
            "qkv": [(wq.at[:, pl.ds(col, T)], w_qkv.at[rows, pl.ds(0, T)]), (wk, w_qkv.at[rows, pl.ds(T, TILE)]), (wv, w_qkv.at[rows, pl.ds(T + TILE, TILE)])],
            "o": [(wo.at[pl.ds(col, T), :], w_o.at[:, rows])],
            "gu": [(wg.at[:, pl.ds(begin, MAIN)], w_g.at[rows, pl.ds(0, MAIN)]), (wu.at[:, pl.ds(begin, MAIN)], w_u.at[rows, pl.ds(0, MAIN)])],
            "d": [(wd.at[pl.ds(begin, MAIN), :], w_d.at[pl.ds(0, MAIN), rows])],
            "gu_tail": [(wg.at[:, pl.ds(tail, TILE)], w_g.at[rows, pl.ds(MAIN, TILE)]), (wu.at[:, pl.ds(tail, TILE)], w_u.at[rows, pl.ds(MAIN, TILE)])],
            "d_tail": [(wd.at[pl.ds(tail, TILE), :], w_d.at[pl.ds(MAIN, TILE), rows])],
        }

    w_sem = {(key, k, i): next(sems) for key, c in (("qkv", 3), ("o", 1), ("gu", 2), ("d", 1), ("gu_tail", 2), ("d_tail", 1)) for k in (1, 2, 3) for i in range(c)}
    w_local = {(key, i): next(local_count) for key, c in (("qkv", 3), ("o", 1), ("gu", 2), ("d", 1), ("gu_tail", 2), ("d_tail", 1)) for i in range(c)}

    def weights_start(key):
        for k in (1, 2, 3):
            for i, (src, dst) in enumerate(weight_moves(k, 0, False)[key]):
                remote(src, dst, w_sem[key, k, i], plane(k)).start()
            if key in ("gu", "d"):

                @pl.when(flip(f, k) % 2 == 0)
                def _():
                    for i, (src, dst) in enumerate(weight_moves(k, 0, False)[key + "_tail"]):
                        remote(src, dst, w_sem[key + "_tail", k, i], plane(k)).start()

    def weights_own(wait):
        moves = weight_moves(0, 0, False)
        for key in ("qkv", "o", "gu", "d"):
            for i, (src, dst) in enumerate(moves[key]):
                cp = here(src, dst, w_local[key, i])
                cp.wait() if wait else cp.start()

        @pl.when(f % 2 == 0)
        def _():
            for key in ("gu_tail", "d_tail"):
                for i, (src, dst) in enumerate(moves[key]):
                    cp = here(src, dst, w_local[key, i])
                    cp.wait() if wait else cp.start()

    def weights_wait(key):
        for k in (1, 2, 3):
            for i, (src, dst) in enumerate(weight_moves(k, 0, True)[key]):
                remote(src, dst, w_sem[key, k, i], plane(k)).wait_recv()
            if key in ("gu", "d"):

                @pl.when(f % 2 == 0)
                def _():
                    for i, (src, dst) in enumerate(weight_moves(k, 0, True)[key + "_tail"]):
                        remote(src, dst, w_sem[key + "_tail", k, i], plane(k)).wait_recv()

    def weights_drain():
        for key in ("qkv", "o", "gu", "d"):
            for k in (1, 2, 3):
                for i, (src, dst) in enumerate(weight_moves(k, 0, False)[key]):
                    remote(src, dst, w_sem[key, k, i], plane(k)).wait_send()
                if key in ("gu", "d"):

                    @pl.when(flip(f, k) % 2 == 0)
                    def _():
                        for i, (src, dst) in enumerate(weight_moves(k, 0, False)[key + "_tail"]):
                            remote(src, dst, w_sem[key + "_tail", k, i], plane(k)).wait_send()

    g_sem = [[next(sems) for _ in range(3)] for _ in range(4)]
    f_sem = [[next(sems) for _ in range(4)] for _ in range(4)]

    def gather_start(g, buf, with_own, src=None):
        block = buf.at[rows_f, half]
        for k in (1, 2, 3):
            remote(block if src is None else src, block, g_sem[g][k - 1], plane(k)).start()
        if with_own:
            remote(block, block, f_sem[g][3], core).start()

    def gather_forward(g, buf):
        for k in (1, 2, 3):
            block = buf.at[rows_of(flip(f, k)), half]
            remote(block, block, g_sem[g][k - 1], plane(k)).wait_recv()
            remote(block, block, f_sem[g][k - 1], core).start()

    def gather_take(g, buf, k):
        if k == 0:
            block = buf.at[rows_f, rest]
            remote(block, block, f_sem[g][3], core).wait_recv()
        else:
            block = buf.at[rows_of(flip(f, k)), rest]
            remote(block, block, f_sem[g][k - 1], core).wait_recv()

    def gather_drain(g, buf, with_own, src=None):
        block = buf.at[rows_f, half]
        for k in (1, 2, 3):
            remote(block if src is None else src, block, g_sem[g][k - 1], plane(k)).wait_send()
            other = buf.at[rows_of(flip(f, k)), half]
            remote(other, other, f_sem[g][k - 1], core).wait_send()
        if with_own:
            remote(block, block, f_sem[g][3], core).wait_send()

    t_sem = [next(sems) for _ in range(3)]
    a_sem = [next(sems) for _ in range(3)]
    own_gain = ga.at[:, pl.ds(al(f * 512, 512), 512)]

    barrier = pltpu.get_barrier_semaphore()
    for k in (1, 2, 3):
        pl.semaphore_signal(barrier, inc=1, device_id=plane(k), device_id_type=MESH)
        pl.semaphore_signal(barrier, inc=1, device_id=column(k), device_id_type=MESH)
    pl.semaphore_signal(barrier, inc=1, device_id=core, device_id_type=MESH)
    pl.semaphore_wait(barrier, 7)

    lt.wait()
    lg.wait()
    for k in (1, 2, 3):
        remote(own_gain, own_gain, a_sem[k - 1], plane(k)).start()
        remote(tb.at[f], tb.at[f], t_sem[k - 1], plane(k)).start()
    weights_start("qkv")
    weights_own(False)

    @pl.when(f % 2 == 1)
    def _():
        w_g[:, MAIN:WIN] = jnp.zeros((W, TILE), BF)
        w_u[:, MAIN:WIN] = jnp.zeros((W, TILE), BF)
        w_d[MAIN:WIN, :] = jnp.zeros((TILE, W), BF)

    lx.wait()
    for k in (1, 2, 3):
        dst = ga.at[:, pl.ds(al(flip(f, k) * 512, 512), 512)]
        remote(dst, dst, a_sem[k - 1], plane(k)).wait_recv()

    STEP = 32

    def sub(i):
        return pl.ds(al(i * STEP, STEP), STEP)

    @pl.loop(0, T // STEP)
    def _(i):
        xs = xv[sub(i), :].astype(F32)
        scale = lax.rsqrt(jnp.mean(xs * xs, axis=-1, keepdims=True) + EPSILON)
        r1s[sub(i), :] = jnp.broadcast_to(scale, (STEP, TILE))
        x1[pl.ds(al(f * T + i * STEP, STEP), STEP), :] = (xs * scale * ga[0:1, :]).astype(BF)

    gather_start(0, x1, False)
    weights_start("o")
    for k in (1, 2, 3):
        dst = tb.at[flip(f, k)]
        remote(dst, dst, t_sem[k - 1], plane(k)).wait_recv()
    weights_own(True)
    weights_wait("qkv")
    weights_start("gu")

    lane = lax.broadcasted_iota(jnp.int32, (T, TILE), 1)
    low_lane = lane < HD
    first_half = lane % HD < HD // 2
    kv_head = f // 2

    def turns(b):
        cosine, sine = tb[b, 0:32, :], tb[b, 32:64, :]
        return (
            jnp.transpose(jnp.concatenate([cosine] * 4, 0)),
            jnp.transpose(jnp.concatenate([-sine, sine, -sine, sine], 0)),
        )

    def turn(v, c, s):
        swapped = jnp.where(first_half, pltpu.roll(v, TILE - 32, 1), pltpu.roll(v, 32, 1))
        return v * c + swapped * s

    def qkv_block(k):
        b = flip(f, k)
        qkv = nn(x1[rows_of(b), :], w_qkv[...])
        c, s = turns(b)
        for i in range(2):
            q = turn(qkv[:, i * TILE : (i + 1) * TILE], c, s) * 0.125
            q_buf[rows_of(b), i * TILE : (i + 1) * TILE] = q.astype(BF)
        key = turn(qkv[:, 2 * TILE : 3 * TILE], c, s)
        value = qkv[:, 3 * TILE :]
        key = jnp.where(kv_head == 0, key, pltpu.roll(key, HD, 1))
        value = jnp.where(kv_head == 1, value, pltpu.roll(value, HD, 1))
        kv_all[z, b, :, :] = jnp.where(low_lane, key, value).astype(BF)
        ids[z, pl.ds(b, 1), :] = tb[b, 64:65, :]

    qkv_block(0)
    gather_forward(0, x1)
    for k in (1, 2, 3):
        gather_take(0, x1, k)

    @pl.loop(1, 4)
    def _(k):
        qkv_block(k)

    z_sem = [[next(sems) for _ in range(2)] for _ in range(3)]
    for k in (1, 2, 3):
        remote(kv_all.at[z], kv_all.at[z], z_sem[k - 1][0], column(k)).start()
        remote(ids.at[z], ids.at[z], z_sem[k - 1][1], column(k)).start()
    gather_start(1, ct, False, cot_in.at[0, :, half])
    for k in (1, 2, 3):
        zz = flip(z, k)
        remote(kv_all.at[zz], kv_all.at[zz], z_sem[k - 1][0], column(k)).wait_recv()
        remote(ids.at[zz], ids.at[zz], z_sem[k - 1][1], column(k)).wait_recv()
    lc.wait()

    low_keys = lax.broadcasted_iota(jnp.int32, (4 * T, TILE), 1) < HD

    def bias_of(s):
        query_id = ids[z, pl.ds(s, 1), :]
        for j in range(4):
            key_id = jnp.transpose(jnp.broadcast_to(ids[j, pl.ds(s, 1), :], (8, T)))[:, 0:1]
            bias[j * T : (j + 1) * T, :] = jnp.where(key_id <= query_id, 0.0, NEGATIVE).astype(BF)

    def kv_of(s):
        kv = jnp.concatenate([kv_all[j, s, :, :] for j in range(4)], 0).astype(F32)
        turned = pltpu.roll(kv, HD, 1)
        keys = jnp.where(low_keys, kv, turned).astype(BF)
        values = jnp.where(low_keys, turned, kv).astype(BF)
        return kv, keys, values

    def only(v, parity):
        return jnp.where(low_lane if parity == 0 else ~low_lane, v.astype(F32), 0.0).astype(BF)

    @pl.loop(0, 4)
    def _(s):
        bias_of(s)
        kv, keys, _ = kv_of(s)
        values_t = jnp.transpose(kv)[HD:, :].astype(BF)

        for i in range(2):
            mixed = []
            for parity in range(2):
                q = only(q_buf[rows_of(s), i * TILE : (i + 1) * TILE], parity)
                scores = nt(keys, q) + bias[...].astype(F32)
                top = jnp.max(scores, axis=0, keepdims=True)
                raw = jnp.exp(scores - top)
                norm = jnp.sum(raw, axis=0, keepdims=True)
                lse[s, 2 * i + parity : 2 * i + parity + 1, :] = top + jnp.log(norm)
                weights = (raw * (1.0 / norm)).astype(BF)
                mixed.append(nn(values_t, weights))
            ob[rows_of(s), i * TILE : (i + 1) * TILE] = jnp.transpose(jnp.concatenate(mixed, 0)).astype(BF)

    p_sem = [[next(sems) for _ in range(4)] for _ in range(4)]
    s_sem = [[next(sems) for _ in range(3)] for _ in range(4)]
    COLS = 256

    def scatter_start(u, product):
        p0, s0 = p_sem[u][0], s_sem[u][0]

        @pl.loop(0, 4)
        def _(i):
            k = (i + 1) % 4
            b = flip(f, k)

            @pl.loop(0, H // COLS)
            def _(j):
                ps[k, :, pl.ds(al(j * COLS, COLS), COLS)] = product(b, (1 - t) * H + j * COLS).astype(BF)

            remote(ps.at[k], pr.at[k], p0 + k, core).start()

        def own(k, j):
            b = flip(f, k)
            cols = pl.ds(al(j * COLS, COLS), COLS)
            return product(b, t * H + j * COLS) + pr[k, :, cols].astype(F32)

        @pl.loop(1, 4)
        def _(k):
            remote(ps.at[k], pr.at[k], p0 + k, core).wait()

            @pl.loop(0, H // COLS)
            def _(j):
                ps[k, :, pl.ds(al(j * COLS, COLS), COLS)] = own(k, j).astype(BF)

            remote(ps.at[k], rr.at[k - 1], s0 + k - 1, plane(k)).start()

        remote(ps.at[0], pr.at[0], p0, core).wait()

        @pl.loop(0, H // COLS)
        def _(j):
            yo[:, pl.ds(al(j * COLS, COLS), COLS)] = own(0, j)

    def scatter_wait(u):
        for k in (1, 2, 3):
            remote(ps.at[k], rr.at[k - 1], s_sem[u][k - 1], plane(k)).wait()

    def scattered(i):
        return yo[sub(i), :] + rr[0, sub(i), :].astype(F32) + rr[1, sub(i), :].astype(F32) + rr[2, sub(i), :].astype(F32)

    n_sem = [next(sems) for _ in range(3)]

    def core_sums(u):
        remote(ss_own.at[u], ss_other.at[u], n_sem[u], core).start()
        remote(ss_own.at[u], ss_other.at[u], n_sem[u], core).wait()

    weights_wait("o")
    weights_wait("gu")
    weights_start("d")
    scatter_start(0, lambda b, c: nn(ob[rows_of(b), :], w_o[:, pl.ds(al(c, COLS), COLS)]))
    scatter_wait(0)

    @pl.loop(0, T // STEP)
    def _(i):
        rows = xv[sub(i), half].astype(F32) + scattered(i)
        hid[sub(i), :] = rows
        ss_own[0, sub(i), :] = jnp.broadcast_to(jnp.sum(rows * rows, axis=-1, keepdims=True), (STEP, TILE))

    core_sums(0)
    gain_one, gain_two = ga[0:1, half], ga[1:2, half]

    @pl.loop(0, T // STEP)
    def _(i):
        scale = lax.rsqrt((ss_own[0, sub(i), 0:1] + ss_other[0, sub(i), 0:1]) * (1.0 / W) + EPSILON)
        r2s[sub(i), :] = jnp.broadcast_to(scale, (STEP, TILE))
        x2[pl.ds(al(f * T + i * STEP, STEP), STEP), half] = (hid[sub(i), :] * scale * gain_two).astype(BF)

    gather_start(2, x2, True)
    gather_forward(1, ct)
    for k in (1, 2, 3):
        gather_take(1, ct, k)
    weights_wait("d")
    gather_forward(2, x2)
    gather_take(2, x2, 0)

    UNITS = 256

    def feed_block(k):
        b = flip(f, k)

        @pl.loop(0, WIN // UNITS)
        def _(j):
            cols = pl.ds(al(j * UNITS, UNITS), UNITS)
            gate = nn(x2[rows_of(b), :], w_g[:, cols])
            up = nn(x2[rows_of(b), :], w_u[:, cols])
            back = nt(ct[rows_of(b), :], w_d[cols, :])
            sigma = jax.nn.sigmoid(gate)
            silu = gate * sigma
            act[rows_of(b), cols] = (silu * up).astype(BF)
            dg[rows_of(b), cols] = (back * up * sigma * (1.0 + gate * (1.0 - sigma))).astype(BF)
            du[rows_of(b), cols] = (back * silu).astype(BF)

    feed_block(0)
    for k in (1, 2, 3):
        gather_take(2, x2, k)

    @pl.loop(1, 4)
    def _(k):
        feed_block(k)

    e_sem = {(name, k, i): next(sems) for name in "dguoqk" for k in (1, 2, 3) for i in range(2)}
    e_local = {(name, i): next(local_count) for name in "dguoqk" for i in range(2)}
    mine = al(starts(f) * TILE, TILE)

    def stage(name, k):
        if name == "d":
            return gs_d.at[pl.ds(k * WIN, WIN), :]
        if name in "gu":
            return ct.at[pl.ds((k // 2) * 512, 512), pl.ds((k % 2) * H, WIN)]
        if name == "o":
            return gs_d.at[pl.ds(k * WIN, T), :]
        return x2.at[pl.ds((k // 2) * 512, 512), pl.ds((k % 2) * 512 + (0 if name == "q" else T), T)]

    def grad_moves(name, k, sender):
        buf, begin = stage(name, k), al(starts(sender) * TILE, TILE)
        tail = al(begin + MAIN, TILE)
        if name == "d":
            return [(buf.at[pl.ds(0, MAIN), :], first["d"].at[pl.ds(begin, MAIN), :]), (buf.at[pl.ds(MAIN, TILE), :], first["d"].at[pl.ds(tail, TILE), :])]
        if name in "gu":
            return [(buf.at[:, pl.ds(0, MAIN)], first[name].at[:, pl.ds(begin, MAIN)]), (buf.at[:, pl.ds(MAIN, TILE)], first[name].at[:, pl.ds(tail, TILE)])]
        if name == "o":
            return [(buf, first["o"].at[rows_of(sender), :])]
        if name == "q":
            return [(buf, first["q"].at[:, rows_of(sender)])]
        return [(buf, kv_g.at[k - 1])]

    def grad_send(name, k, act_on, only_wait=False):
        for i, (src, dst) in enumerate(grad_moves(name, k, f)):

            def run(i=i, src=src, dst=dst):
                if k == 0:
                    cp = here(src, dst, e_local[name, i])
                    cp.wait() if act_on == "wait" else cp.start()
                else:
                    cp = remote(src, dst, e_sem[name, k, i], plane(k))
                    cp.wait_send() if act_on == "wait" else cp.start()

            if i == 0:
                run()
            else:
                pl.when(f % 2 == 0)(run)

    def grad_take(name):
        for k in (1, 2, 3):
            sender = flip(f, k)
            for i, (src, dst) in enumerate(grad_moves(name, k, sender)):

                def run(i=i, src=src, dst=dst):
                    remote(src, dst, e_sem[name, k, i], plane(k)).wait_recv()

                if i == 0:
                    run()
                else:
                    pl.when(sender % 2 == 0)(run)

    def block_cols(k):
        return pl.ds(al(flip(f, k) * 512, 512), 512)

    for k in (1, 2, 3, 0):

        @pl.loop(0, WIN // UNITS)
        def _(j):
            cols = pl.ds(al(j * UNITS, UNITS), UNITS)
            gs_d[pl.ds(al(k * WIN + j * UNITS, UNITS), UNITS), :] = tn(act[:, cols], ct[:, block_cols(k)]).astype(BF)

        grad_send("d", k, "start")

    scatter_start(1, lambda b, c: nt(dg[rows_of(b), :], w_g[pl.ds(al(c, COLS), COLS), :]) + nt(du[rows_of(b), :], w_u[pl.ds(al(c, COLS), COLS), :]))

    gather_drain(1, ct, False, cot_in.at[0, :, half])
    def feed_grads(name, right):
        for k in (1, 2, 3, 0):

            @pl.loop(0, 2)
            def _(i):
                xs = x2[:, pl.ds(al(flip(f, k) * 512 + i * T, T), T)]
                stage(name, k)[pl.ds(al(i * T, T), T), :] = tn(xs, right[...]).astype(BF)

            grad_send(name, k, "start")

    feed_grads("g", dg)

    end = (z == 0) | (z == 3)
    middle = (z == 1) | (z == 2)
    next_in = (f, jnp.where(z < 2, 1, 2), t)
    next_out = (f, jnp.where(z < 2, 0, 3), t)
    facing = (f, 3 - z, t)
    l_sem = [[next(sems) for _ in range(3)] for _ in CHUNKS]
    v_sem = [next(local_count) for _ in range(2)]
    o_sem = [next(local_count) for _ in CHUNKS]
    DEPTH = 2

    def window(arrays, i):
        name, r, c, rows, cols = CHUNKS[i]
        return arrays[name].at[pl.ds(r, rows), pl.ds(c, cols)]

    def line_send(name):
        @pl.when(end)
        def _():
            for i, chunk in enumerate(CHUNKS):
                if chunk[0] == name:
                    remote(window(first, i), window(left, i), l_sem[i][0], next_in).start()

    def add_into(dst, a, b, rows, cols):
        @pl.loop(0, rows // STEP)
        def _(i):
            at = sub(i)
            dst[at, pl.ds(0, cols)] = (a[at, pl.ds(0, cols)].astype(F32) + b[at, pl.ds(0, cols)].astype(F32)).astype(BF)

    def line_one(i):
        name, r, c, rows, cols = CHUNKS[i]
        part = (pl.ds(0, rows), pl.ds(0, cols))
        a, b, keep = la.at[part], lb.at[part], ring.at[i % DEPTH]

        @pl.when(middle)
        def _():
            get_a = here(window(first, i), a, v_sem[0])
            get_a.start()
            remote(window(first, i), window(left, i), l_sem[i][0], next_in).wait_recv()
            get_b = here(window(left, i), b, v_sem[1])
            get_b.start()
            get_a.wait()
            get_b.wait()
            add_into(keep, la, lb, rows, cols)
            remote(keep.at[part], window(cross, i), l_sem[i][1], facing).start()

    def line_two(i):
        name, r, c, rows, cols = CHUNKS[i]
        part = (pl.ds(0, rows), pl.ds(0, cols))
        keep, done = ring.at[i % DEPTH], tt.at[i % 2]

        @pl.when(middle)
        def _():
            remote(keep.at[part], window(cross, i), l_sem[i][1], facing).wait()
            get = here(window(cross, i), lb.at[part], v_sem[1])
            get.start()
            if i >= 2:
                line_out(i - 2)
            get.wait()
            add_into(done, keep, lb, rows, cols)
            remote(done.at[part], window(total, i), l_sem[i][2], next_out).start()
            here(done.at[part], window(total, i), o_sem[i]).start()

    def line_out(i):
        name, r, c, rows, cols = CHUNKS[i]
        done = tt.at[i % 2].at[pl.ds(0, rows), pl.ds(0, cols)]
        remote(done, window(total, i), l_sem[i][2], next_out).wait_send()
        here(done, window(total, i), o_sem[i]).wait()

    pumped = [0]

    def pump(name):
        while pumped[0] < len(CHUNKS) and CHUNKS[pumped[0]][0] == name:
            i = pumped[0]
            line_one(i)
            if i >= 1:
                line_two(i - 1)
            pumped[0] += 1

    def grad_ready(name):
        grad_take(name)
        grad_send(name, 0, "wait")
        line_send(name)

    grad_ready("d")
    scatter_wait(1)

    lh.wait()

    def norm_two_back(i, carry):
        rows = scattered(i)
        yo[sub(i), :] = rows
        hat = hid[sub(i), :] * r2s[sub(i), 0:1]
        ss_own[1, sub(i), :] = jnp.broadcast_to(jnp.sum(rows * gain_two * hat, axis=-1, keepdims=True), (STEP, TILE))
        return carry + jnp.sum(rows * hat, axis=0, keepdims=True)

    g_sum[...] = jnp.zeros((8, H), F32)
    g_sum[1:2, :] = lax.fori_loop(0, T // STEP, norm_two_back, jnp.zeros((1, H), F32))
    core_sums(1)

    @pl.loop(0, T // STEP)
    def _(i):
        scale = r2s[sub(i), 0:1]
        hat = hid[sub(i), :] * scale
        mean = (ss_own[1, sub(i), 0:1] + ss_other[1, sub(i), 0:1]) * (1.0 / W)
        rows = out_s[sub(i), :].astype(F32) + scale * (yo[sub(i), :] * gain_two - hat * mean)
        d_hid[sub(i), :] = rows
        dh[pl.ds(al(f * T + i * STEP, STEP), STEP), half] = rows.astype(BF)

    gather_start(3, dh, True)
    grad_ready("g")
    gather_forward(3, dh)
    pump("d")
    for k in range(4):
        gather_take(3, dh, k)
    for k in (1, 2, 3):
        grad_send("g", k, "wait")
    feed_grads("u", du)

    for k in (1, 2, 3):
        grad_send("d", k, "wait")
    for k in (1, 2, 3, 0):
        gs_d[k * WIN : k * WIN + T, :] = tn(ob[...], dh[:, block_cols(k)]).astype(BF)
        grad_send("o", k, "start")

    @pl.loop(0, 4)
    def _(b):
        ob[rows_of(b), :] = nt(dh[rows_of(b), :], w_o[...]).astype(BF)

    d_ob, d_qkv = ob, dg
    scatter_start(2, lambda b, c: nn(act[rows_of(b), :], w_d[:, pl.ds(al(c, COLS), COLS)]))

    gather_drain(2, x2, True)

    def attend_back(s):
        bias_of(s)
        kv, keys, values = kv_of(s)
        keys_t = jnp.transpose(kv)[:HD, :].astype(BF)
        c, sn = turns(s)
        d_key = jnp.zeros((4 * T, TILE), F32)
        d_value = jnp.zeros((4 * T, TILE), F32)
        for i in range(2):
            d_query = []
            for parity in range(2):
                q = only(q_buf[rows_of(s), i * TILE : (i + 1) * TILE], parity)
                do = only(d_ob[rows_of(s), i * TILE : (i + 1) * TILE], parity)
                weights = jnp.exp(nt(keys, q) + bias[...].astype(F32) - lse[s, 2 * i + parity : 2 * i + parity + 1, :])
                d_weights = nt(values, do)
                delta = jnp.sum(weights * d_weights, axis=0, keepdims=True)
                d_scores = (weights * (d_weights - delta)).astype(BF)
                d_value = d_value + nn(weights.astype(BF), do)
                d_key = d_key + nn(d_scores, q)
                d_query.append(nn(keys_t, d_scores))
            d_query = jnp.transpose(jnp.concatenate(d_query, 0)) * 0.125
            d_qkv[rows_of(s), i * TILE : (i + 1) * TILE] = turn(d_query, c, -sn).astype(BF)
        d_key = d_key + pltpu.roll(d_key, HD, 1)
        d_value = d_value + pltpu.roll(d_value, HD, 1)
        both = jnp.where(low_keys, d_key, d_value)
        own = both[0:T, :]
        for j in range(1, 4):
            own = jnp.where(z == j, both[j * T : (j + 1) * T, :], own)
        d_kv[s, :, :] = own
        for j in range(4):
            x2[rows_of(s), H + j * TILE : H + (j + 1) * TILE] = both[j * T : (j + 1) * T, :].astype(BF)

    @pl.loop(0, 2)
    def _(s):
        attend_back(s)

    grad_ready("u")
    pump("g")
    scatter_wait(2)

    @pl.loop(0, T // STEP)
    def _(i):
        out_s[sub(i), :] = (hid[sub(i), :] + scattered(i)).astype(BF)

    for k in (1, 2, 3):
        pl.semaphore_signal(credit, inc=1, device_id=plane(k), device_id_type=MESH)
    pl.semaphore_signal(credit, inc=1, device_id=core, device_id_type=MESH)
    out_local = here(out_s, out_ref.at[:, half], next(local_count))
    out_local.start()
    out_remote = remote(out_s, out_ref.at[:, half], next(sems), core)
    out_remote.start()

    @pl.loop(2, 4)
    def _(s):
        attend_back(s)

    k_sem = [next(sems) for _ in range(3)]
    for k in (1, 2, 3):
        remote(x2.at[:, pl.ds(al(H + flip(z, k) * TILE, TILE), TILE)], d_kv_recv.at[k - 1], k_sem[k - 1], column(k)).start()
    grad_ready("o")
    pump("u")
    for k in (1, 2, 3):
        remote(x2.at[:, pl.ds(al(H + flip(z, k) * TILE, TILE), TILE)], d_kv_recv.at[k - 1], k_sem[k - 1], column(k)).wait()

    here_half = low_lane if False else (lane // HD) == kv_head

    @pl.loop(0, 4)
    def _(s):
        c, sn = turns(s)
        whole = d_kv[s, :, :]
        for k in range(3):
            whole = whole + d_kv_recv[k, rows_of(s), :].astype(F32)
        turned = pltpu.roll(whole, HD, 1)
        d_key = turn(jnp.where(low_lane, whole, turned), c, -sn)
        d_value = jnp.where(low_lane, turned, whole)
        d_qkv[rows_of(s), 2 * TILE : 3 * TILE] = jnp.where(here_half, d_key, 0.0).astype(BF)
        d_qkv[rows_of(s), 3 * TILE : 4 * TILE] = jnp.where(here_half, d_value, 0.0).astype(BF)

    for k in (1, 2, 3, 0):

        @pl.loop(0, 2)
        def _(i):
            xs = x1[:, pl.ds(al(flip(f, k) * 512 + i * T, T), T)]
            x2[pl.ds(al((k // 2) * 512 + i * T, T), T), (k % 2) * 512 : (k % 2) * 512 + 512] = tn(xs, d_qkv[:, 0:512]).astype(BF)

        grad_send("q", k, "start")
        if k:
            grad_send("k", k, "start")
    pl.semaphore_wait(credit, 4)
    scatter_start(3, lambda b, c: nt(d_qkv[rows_of(b), 0:512], w_qkv[pl.ds(al(c, COLS), COLS), :]))
    pump("o")
    grad_ready("q")
    grad_take("k")

    @pl.loop(0, 512 // STEP)
    def _(i):
        rows = x2[sub(i), T : 2 * T].astype(F32)
        for k in (1, 2, 3):
            rows = rows + kv_g[k - 1, sub(i), :].astype(F32)
        la[sub(i), 0:T] = rows.astype(BF)

    kv_copy = here(la.at[:, pl.ds(0, T)], first["k"], next(local_count))
    kv_copy.start()
    kv_copy.wait()
    line_send("k")
    pump("q")
    scatter_wait(3)

    def norm_one_back(i, carry):
        rows = scattered(i)
        yo[sub(i), :] = rows
        hat = xv[sub(i), half].astype(F32) * r1s[sub(i), 0:1]
        ss_own[2, sub(i), :] = jnp.broadcast_to(jnp.sum(rows * gain_one * hat, axis=-1, keepdims=True), (STEP, TILE))
        return carry + jnp.sum(rows * hat, axis=0, keepdims=True)

    g_sum[0:1, :] = lax.fori_loop(0, T // STEP, norm_one_back, jnp.zeros((1, H), F32))
    core_sums(2)

    q_sem = [[next(sems) for _ in range(3)] for _ in range(2)]
    g_plane[f, :, :] = g_sum[...]
    for k in (1, 2, 3):
        remote(g_sum, g_plane.at[f], q_sem[0][k - 1], plane(k)).start()

    @pl.loop(0, T // STEP)
    def _(i):
        scale = r1s[sub(i), 0:1]
        hat = xv[sub(i), half].astype(F32) * scale
        mean = (ss_own[2, sub(i), 0:1] + ss_other[2, sub(i), 0:1]) * (1.0 / W)
        yo[sub(i), :] = d_hid[sub(i), :] + scale * (yo[sub(i), :] * gain_one - hat * mean)

    in_local = here(yo, in_grad_ref.at[:, half], next(local_count))
    in_local.start()
    in_remote = remote(yo, in_grad_ref.at[:, half], next(sems), core)
    in_remote.start()
    for k in (1, 2, 3):
        remote(g_sum, g_plane.at[flip(f, k)], q_sem[0][k - 1], plane(k)).wait_recv()
    g_column[z, :, :] = ((g_plane[0, :, :] + g_plane[1, :, :]) + g_plane[2, :, :]) + g_plane[3, :, :]
    for k in (1, 2, 3):
        remote(g_column.at[z], g_column.at[z], q_sem[1][k - 1], column(k)).start()
    pump("k")
    line_two(len(CHUNKS) - 1)
    for k in (1, 2, 3):
        remote(g_column.at[z], g_column.at[flip(z, k)], q_sem[1][k - 1], column(k)).wait_recv()
    g_whole[:, half] = ((g_column[0, :, :] + g_column[1, :, :]) + g_column[2, :, :]) + g_column[3, :, :]
    w_move = remote(g_whole.at[:, half], g_whole.at[:, half], next(sems), core)
    w_move.start()
    w_move.wait()
    gain_move = here(g_whole.at[:, pl.ds(al(f * 512, 512), 512)], gain_ref, next(local_count))
    gain_move.start()

    @pl.when(middle)
    def _():
        line_out(len(CHUNKS) - 2)
        line_out(len(CHUNKS) - 1)

    @pl.when(end)
    def _():
        for i in range(len(CHUNKS)):
            remote(window(first, i), window(left, i), l_sem[i][0], next_in).wait_send()
            remote(window(total, i), window(total, i), l_sem[i][2], next_in).wait_recv()

    gain_move.wait()
    out_local.wait()
    out_remote.wait()
    in_local.wait()
    in_remote.wait()
    weights_drain()
    gather_drain(0, x1, False)
    gather_drain(3, dh, True)
    for k in (1, 2, 3):
        remote(own_gain, own_gain, a_sem[k - 1], plane(k)).wait_send()
        remote(tb.at[f], tb.at[f], t_sem[k - 1], plane(k)).wait_send()
        remote(kv_all.at[z], kv_all.at[z], z_sem[k - 1][0], column(k)).wait_send()
        remote(ids.at[z], ids.at[z], z_sem[k - 1][1], column(k)).wait_send()
        remote(g_sum, g_plane.at[f], q_sem[0][k - 1], plane(k)).wait_send()
        remote(g_column.at[z], g_column.at[z], q_sem[1][k - 1], column(k)).wait_send()
        for name in "uoqk":
            grad_send(name, k, "wait")
    assert next(sems) <= REMOTE_SEMS and next(local_count) <= LOCAL_SEMS


REMOTE_SEMS, LOCAL_SEMS = 400, 96


def layer_call(inputs, positions, blocks, cotangent, attn_gain, w_query, w_key, w_value, w_out, mlp_gain, w_gate, w_up, w_down):
    frequency = jnp.exp(jnp.arange(HD // 2, dtype=F32) * (-2.0 * math.log(10000.0) / HD))
    turned = frequency[:, None] * positions.astype(F32)
    table = jnp.concatenate([jnp.cos(turned), jnp.sin(turned), jnp.broadcast_to(blocks.astype(F32), (8, T))], 0)
    gains = jnp.concatenate([attn_gain[None], mlp_gain[None], jnp.zeros((6, 512), BF)], 0).astype(F32)
    shape = jax.ShapeDtypeStruct
    grads = [shape((rows, cols), BF) for _, rows, cols in GRADS]
    any_spec = pl.BlockSpec(memory_space=pl.ANY)
    v = pltpu.VMEM
    results = pl.pallas_call(
        layer_kernel,
        out_shape=[shape((T, W), BF), shape((T, W), F32), shape((8, 512), F32)] + grads * 4,
        in_specs=[any_spec] * 11,
        out_specs=[any_spec] * 27,
        scratch_shapes=[
            v((4 * T, W), BF), v((4 * T, W), BF), v((4 * T, W), BF), v((4 * T, W), BF),
            v((W, 512), BF), v((T, W), BF), v((W, WIN), BF), v((W, WIN), BF), v((WIN, W), BF),
            v((4 * T, WIN), BF), v((4 * T, WIN), BF), v((4 * T, WIN), BF),
            v((4 * T, T), BF), v((4, 4, T, TILE), BF), v((4 * T, T), BF),
            v((4, T, H), BF), v((4, T, H), BF), v((3, T, H), BF), v((T, H), F32), v((T, H), F32), v((T, H), F32), v((T, W), BF),
            v((4, 72, T), F32), v((8, W), F32), v((4, 8, T), F32), v((T, TILE), F32), v((T, TILE), F32),
            v((3, T, TILE), F32), v((3, T, TILE), F32), v((4, 8, T), F32), v((4 * T, T), BF),
            v((4 * WIN, 512), BF), v((3, 512, T), BF), v((512, 512), BF), v((512, 512), BF),
            v((2, 512, 512), BF), v((2, 512, 512), BF), v((4, T, TILE), F32), v((3, 4 * T, TILE), BF),
            v((T, H), BF), v((8, H), F32), v((4, 8, H), F32), v((4, 8, H), F32), v((8, W), F32),
            pltpu.SemaphoreType.DMA((REMOTE_SEMS,)), pltpu.SemaphoreType.DMA((REMOTE_SEMS,)),
            pltpu.SemaphoreType.DMA((LOCAL_SEMS,)), pltpu.SemaphoreType.REGULAR,
        ],
        compiler_params=pltpu.CompilerParams(collective_id=0, has_side_effects=True, vmem_limit_bytes=62 << 20),
    )(inputs, table, gains, cotangent, w_query, w_key, w_value, w_out, w_gate, w_up, w_down)
    output, input_grad, gain_grads = results[:3]
    down, gate, up, out, query, kv = (r.astype(F32) for r in results[-6:])
    return (output[None], input_grad[None], gain_grads[0], query, kv[:, :TILE], kv[:, TILE:], out, gain_grads[1], gate, up, down)


def solution(mesh):
    n, m = mesh.shape["fsdp"], mesh.shape["ctx"]

    def step(*args):
        return layer_call(*args) if n == m == 4 else local(n, m, *args)

    return jax.shard_map(
        step,
        mesh=mesh,
        in_specs=(
            P("fsdp", "ctx", None),
            P("fsdp", "ctx"),
            P("fsdp", "ctx"),
            P("fsdp", "ctx", None),
            P("fsdp"),
            P("fsdp", "tp"),
            P("fsdp", "tp"),
            P("fsdp", "tp"),
            P("tp", "fsdp"),
            P("fsdp"),
            P("fsdp", "tp"),
            P("fsdp", "tp"),
            P("tp", "fsdp"),
        ),
        out_specs=(
            P("fsdp", "ctx", None),
            P("fsdp", "ctx", None),
            P("fsdp"),
            P("fsdp", "tp"),
            P("fsdp", "tp"),
            P("fsdp", "tp"),
            P("tp", "fsdp"),
            P("fsdp"),
            P("fsdp", "tp"),
            P("fsdp", "tp"),
            P("tp", "fsdp"),
        ),
        check_vma=False,
    )
```

```python
import functools
import math

import jax
import jax.numpy as jnp
from jax import lax
from jax.experimental import pallas as pl
from jax.experimental.pallas import tpu as pltpu
from jax.sharding import PartitionSpec as P

HD = 64
EPSILON = 1e-05
NEGATIVE = -1e30
BF = jnp.bfloat16
F32 = jnp.float32


def dot(a, b, ca, cb):
    return lax.dot_general(a, b, (((ca,), (cb,)), ((), ())), preferred_element_type=F32)


def angles(positions):
    half = HD // 2
    frequency = jnp.exp(jnp.arange(half, dtype=F32) * (-2.0 * math.log(10000.0) / HD))
    turned = positions.astype(F32)[:, None] * frequency[None, :]
    return jnp.cos(turned)[:, None, :], jnp.sin(turned)[:, None, :]


def rotate(values, cosine, sine):
    half = HD // 2
    a, b = values[..., :half], values[..., half:]
    return jnp.concatenate([a * cosine - b * sine, b * cosine + a * sine], axis=-1)


def gated(values, after):
    return lax.optimization_barrier((values, after))[0]


def local(n, m, inputs, positions, blocks, cotangent, attn_gain, w_query, w_key, w_value, w_out, mlp_gain, w_gate, w_up, w_down):
    f = lax.axis_index("fsdp")
    z = lax.axis_index("ctx")
    t = lax.axis_index("tp")
    tokens, width = inputs.shape[1:]
    half = width // 2
    peers = range(1, n)

    def plane(x, k):
        return x if k == 0 else lax.ppermute(x, "fsdp", [(i, i ^ k) for i in range(n)])

    def column(x, k):
        return x if k == 0 else lax.ppermute(x, "ctx", [(i, i ^ k) for i in range(m)])

    def swap(x):
        return lax.ppermute(x, "tp", [(0, 1), (1, 0)])

    def part(x, index, axis):
        size = x.shape[axis] // n
        return lax.dynamic_slice_in_dim(x, index * size, size, axis)

    def mine(x, which):
        return lax.dynamic_slice_in_dim(x, which * half, half, x.ndim - 1)

    def place(pieces, axis):
        size = pieces[0].shape[axis]
        shape = list(pieces[0].shape)
        shape[axis] = size * n
        whole = jnp.zeros(shape, pieces[0].dtype)
        for k in range(n):
            whole = lax.dynamic_update_slice_in_dim(whole, pieces[k], (f ^ k) * size, axis)
        return whole

    def join(own, other):
        return jnp.where(t == 0, jnp.concatenate([own, other], -1), jnp.concatenate([other, own], -1))

    def gather(x):
        rows = jnp.concatenate([plane(x, k) for k in range(n)], 0)
        return join(rows, swap(rows))

    def scatter(partial):
        own = mine(partial, t) + swap(mine(partial.astype(BF), 1 - t)).astype(F32)
        low = own.astype(BF)
        total = own[:tokens]
        for k in peers:
            total = total + plane(low[k * tokens : (k + 1) * tokens], k).astype(F32)
        return total

    def row_mean(own):
        own = jnp.sum(own, -1)
        return ((own + swap(own)) / width)[:, None]

    x = inputs[0].astype(F32)
    gains = jnp.stack([attn_gain, mlp_gain])
    gains = place([plane(gains, k) for k in range(n)], 1).astype(F32)
    marks = jnp.stack([positions[0], blocks[0]])
    marks = [plane(marks, k) for k in range(n)]
    place_rows = jnp.concatenate([mk[0] for mk in marks])
    query_ids = jnp.stack([mk[1] for mk in marks])
    scale_one = lax.rsqrt(jnp.mean(x * x, axis=-1, keepdims=True) + EPSILON)
    x_half = mine(x, t)
    hat_one = x_half * scale_one
    gain_one, gain_two = mine(gains[0:1], t), mine(gains[1:2], t)
    xn_one = gather((hat_one * gain_one).astype(BF))

    heads = w_query.shape[1] // HD // n
    cols = heads * HD
    kv_pair = jnp.concatenate([w_key, w_value], 1)
    kv_heads = w_key.shape[1] // HD
    w_qkv = place([plane(jnp.concatenate([part(w_query, f ^ k, 1), kv_pair], 1), k) for k in range(n)], 0)
    wo = gated(w_out, xn_one)
    wo = place([plane(part(wo, f ^ k, 0), k) for k in range(n)], 1)
    gate_up = gated((w_gate, w_up), xn_one)
    gate_up = [plane(jnp.stack([part(gate_up[0], f ^ k, 1), part(gate_up[1], f ^ k, 1)]), k) for k in range(n)]
    wg = place([g[0] for g in gate_up], 0)
    wu = place([g[1] for g in gate_up], 0)

    qkv = dot(xn_one, w_qkv, 1, 0)
    cosine, sine = angles(place_rows)
    kv_here = (heads * f) // ((w_query.shape[1] // HD) // kv_heads)

    def pick(both):
        out = both[:, :HD]
        for g in range(1, kv_heads):
            out = jnp.where(kv_here == g, both[:, g * HD : (g + 1) * HD], out)
        return out

    kw = kv_heads * HD
    query = rotate(qkv[:, :cols].reshape(-1, heads, HD), cosine, sine).astype(BF)
    key = rotate(pick(qkv[:, cols : cols + kw])[:, None, :], cosine, sine)[:, 0, :].astype(BF)
    value = pick(qkv[:, cols + kw :]).astype(BF)
    key_value = jnp.concatenate([key, value], 1).reshape(n, tokens, 2 * HD)
    kv_all = jnp.concatenate([column(key_value, k) for k in range(m)], 1)
    ids_all = jnp.concatenate([column(query_ids, k) for k in range(m)], 1)
    keys, values = kv_all[..., :HD], kv_all[..., HD:]
    factor = 1.0 / math.sqrt(HD)
    query = query.reshape(n, tokens, heads, HD)
    allowed = (ids_all[:, None, :] <= query_ids[:, :, None])[:, None]
    scores = jnp.einsum("nthd,nsd->nhts", query, keys, preferred_element_type=F32) * factor
    scores = jnp.where(allowed, scores, NEGATIVE)
    top = jnp.max(scores, -1, keepdims=True)
    raw = jnp.where(allowed, jnp.exp(scores - top), 0.0)
    weights = raw / jnp.sum(raw, -1, keepdims=True)
    weights_low = weights.astype(BF)
    attended = jnp.einsum("nhts,nsd->nthd", weights_low, values, preferred_element_type=F32)
    attended_low = attended.astype(BF).reshape(n * tokens, cols)

    hidden = x_half + scatter(dot(attended_low, wo, 1, 0))
    scale_two = lax.rsqrt(row_mean(hidden * hidden) + EPSILON)
    hat_two = hidden * scale_two
    xn_two = gather((hat_two * gain_two).astype(BF))
    cot = gather(gated(mine(cotangent[0], t), wg))
    wd = gated(w_down, wg)
    wd = place([plane(part(wd, f ^ k, 0), k) for k in range(n)], 1)
    gate = dot(xn_two, wg, 1, 0)
    up = dot(xn_two, wu, 1, 0)
    sigma = jax.nn.sigmoid(gate)
    silu = gate * sigma
    act = (silu * up).astype(BF)
    dact = dot(cot, wd, 1, 1)
    dgate = (dact * up * sigma * (1.0 + gate * (1.0 - sigma))).astype(BF)
    dup = (dact * silu).astype(BF)

    def reduce(piece):
        if m != 4:
            return lax.psum(piece, "ctx")
        one = (piece.astype(F32) + lax.ppermute(piece, "ctx", [(0, 1), (3, 2)]).astype(F32)).astype(BF)
        two = (one.astype(F32) + lax.ppermute(one, "ctx", [(1, 2), (2, 1)]).astype(F32)).astype(BF)
        three = lax.ppermute(two, "ctx", [(1, 0), (2, 3)])
        return jnp.where((z == 0) | (z == 3), three, two)

    def share(grad, axis):
        low = grad.astype(BF)
        return [plane(part(low, f ^ k, axis), k) for k in range(n)]

    down_parts = [reduce(p) for p in share(dot(act, cot, 0, 0), 1)]
    gate_parts = [reduce(p) for p in share(dot(xn_two, dgate, 0, 0), 0)]
    up_parts = [reduce(p) for p in share(dot(xn_two, dup, 0, 0), 0)]
    d_two = scatter(dot(dgate, wg, 1, 1) + dot(dup, wu, 1, 1))
    out_half = (hidden + scatter(dot(act, wd, 1, 0))).astype(BF)
    output = join(out_half, swap(out_half))
    gain_two_grad = jnp.sum(d_two * hat_two, 0)
    e_two = d_two * gain_two
    d_hidden = mine(cotangent[0], t).astype(F32) + scale_two * (e_two - hat_two * row_mean(e_two * hat_two))
    dhb = gather(d_hidden.astype(BF))
    out_parts = [reduce(p) for p in share(dot(attended_low, dhb, 0, 0), 1)]

    d_att = dot(dhb, wo, 1, 1).astype(BF).reshape(n, tokens, heads, HD)
    delta = jnp.einsum("nthd,nthd->nht", d_att.astype(F32), attended)
    d_weights = jnp.einsum("nthd,nsd->nhts", d_att, values, preferred_element_type=F32)
    d_scores = (weights * (d_weights - delta[..., None])).astype(BF)
    dv = jnp.einsum("nhts,nthd->nsd", weights_low, d_att, preferred_element_type=F32)
    dk = jnp.einsum("nhts,nthd->nsd", d_scores, query, preferred_element_type=F32) * factor
    dq = jnp.einsum("nhts,nsd->nthd", d_scores, keys, preferred_element_type=F32) * factor
    d_kv = jnp.concatenate([dk, dv], -1).reshape(n, m, tokens, 2 * HD)
    d_low = d_kv.astype(BF)
    d_kv_own = d_kv[:, 0]
    for k in range(1, m):
        d_kv_own = d_kv_own + column(d_low[:, k], k).astype(F32)
    d_kv_own = d_kv_own.reshape(n * tokens, 2 * HD)
    dq = rotate(dq.reshape(n * tokens, heads, HD), cosine, -sine).reshape(n * tokens, cols)
    dk = rotate(d_kv_own[:, None, :HD], cosine, -sine)[:, 0, :]
    d_qkv = jnp.concatenate([dq, dk, d_kv_own[:, HD:]], 1).astype(BF)
    w_here = jnp.concatenate([w_qkv[:, :cols], pick(w_qkv[:, cols : cols + kw]), pick(w_qkv[:, cols + kw :])], 1)
    d_one = scatter(dot(d_qkv, w_here, 1, 1))
    qkv_parts = share(dot(xn_one, d_qkv, 0, 0), 0)
    key_parts, value_parts = [0.0] * kv_heads, [0.0] * kv_heads
    for k in range(n):
        owner = (heads * (f ^ k)) // ((w_query.shape[1] // HD) // kv_heads)
        piece = qkv_parts[k].astype(F32)
        for g in range(kv_heads):
            key_parts[g] = key_parts[g] + jnp.where(owner == g, piece[:, cols : cols + HD], 0.0)
            value_parts[g] = value_parts[g] + jnp.where(owner == g, piece[:, cols + HD :], 0.0)
    small = reduce(jnp.concatenate(key_parts + value_parts, 1).astype(BF)).astype(F32)
    query_parts = [reduce(p[:, :cols]) for p in qkv_parts]
    gain_one_grad = jnp.sum(d_one * hat_one, 0)
    e_one = d_one * gain_one
    in_half = d_hidden + scale_one * (e_one - hat_one * row_mean(e_one * hat_one))
    input_grad = join(in_half, swap(in_half))
    gain_grads = jnp.stack([gain_one_grad, gain_two_grad])
    nothing = jnp.zeros_like(gain_grads)
    gain_grads = jnp.where(t == 0, jnp.concatenate([gain_grads, nothing], 1), jnp.concatenate([nothing, gain_grads], 1))
    gain_grads = part(lax.psum(gain_grads, ("fsdp", "ctx", "tp")), f, 1)

    def settle(pieces, axis):
        return place(pieces, axis).astype(F32)

    return (
        output[None],
        input_grad[None],
        gain_grads[0],
        settle(query_parts, 1),
        small[:, :kw],
        small[:, kw:],
        settle(out_parts, 0),
        gain_grads[1],
        settle(gate_parts, 1),
        settle(up_parts, 1),
        settle(down_parts, 0),
    )


T, W, H, TILE = 256, 2048, 1024, 128
MAIN, WIN = 640, 768
GRADS = (("d", 2816, 512), ("g", 512, 2816), ("u", 512, 2816), ("o", 1024, 512), ("q", 512, 1024), ("k", 512, 256))
PART = 384


def chunk_list():
    chunks = []
    for name in "dgu":
        for which in "AB":
            for j in range(4):
                begin = (11 * j + 1) // 2 * TILE
                size = (11 * j + 12) // 2 * TILE - begin
                at, size = (begin, PART) if which == "A" else (begin + PART, size - PART)
                chunks.append((name + which, name) + ((at, 0, size, 512) if name == "d" else (0, at, 512, size)))
    chunks += [("o", "o", r, 0, 512, 512) for r in (0, 512)]
    chunks += [("q", "q", 0, c, 512, 512) for c in (0, 512)]
    return chunks + [("k", "k", 0, 0, 512, 256)]


CHUNKS = chunk_list()
MESH = pl.DeviceIdType.MESH


def nn(a, b):
    return lax.dot_general(a, b, (((1,), (0,)), ((), ())), preferred_element_type=F32)


def nt(a, b):
    return lax.dot_general(a, b, (((1,), (1,)), ((), ())), preferred_element_type=F32)


def tn(a, b):
    return lax.dot_general(a, b, (((0,), (0,)), ((), ())), preferred_element_type=F32)


def flip(a, k):
    return (a % 2 + k % 2) % 2 + 2 * ((a // 2 + k // 2) % 2)


def layer_kernel(*refs):
    names = iter(refs)

    def take(count):
        return [next(names) for _ in range(count)]

    x_in, table_in, gains_in, cot_in, wq, wk, wv, wo, wg, wu, wd = take(11)
    out_ref, in_grad_ref, gain_ref = take(3)
    first, left, cross, total = ({name: next(names) for name, _, _ in GRADS} for _ in range(4))
    (x1, x2, ct, dh, w_qkv, w_o, w_g, w_u, w_d, act, dg, du, q_buf, kv_all, ob) = take(15)
    (ps, pr, rr, yo, hid, d_hid, xv, tb, ga, ids, r1s, r2s, ss_own, ss_other, lse, bias) = take(16)
    (gs_d, kv_g, d_kv, d_kv_recv, out_s, g_sum, g_plane, g_column, g_whole) = take(9)
    send_sem, recv_sem, local_sem, credit = take(4)
    f, z, t = lax.axis_index("fsdp"), lax.axis_index("ctx"), lax.axis_index("tp")
    sems = iter(range(10**6))
    drains = []

    def al(v, by):
        return pl.multiple_of(v, by)

    def plane(k):
        return (flip(f, k), z, t)

    def column(k):
        return (f, flip(z, k), t)

    core = (f, z, 1 - t)
    rows_f = pl.ds(al(f * T, T), T)
    half = pl.ds(al(t * H, H), H)
    rest = pl.ds(al((1 - t) * H, H), H)

    def rows_of(b):
        return pl.ds(al(b * T, T), T)

    def remote(src, dst, s, device):
        return pltpu.make_async_remote_copy(src_ref=src, dst_ref=dst, send_sem=send_sem.at[s], recv_sem=recv_sem.at[s], device_id=device, device_id_type=MESH)

    def here(src, dst, s):
        return pltpu.make_async_copy(src, dst, local_sem.at[s])

    local_count = iter(range(10**6))

    lx = here(x_in.at[0], xv, next(local_count))
    lx.start()
    lc = here(cot_in.at[0], ct.at[rows_f, :], next(local_count))
    lc.start()
    lh = here(cot_in.at[0, :, half], out_s, next(local_count))
    lh.start()
    lt = here(table_in, tb.at[f], next(local_count))
    lt.start()
    lg = here(gains_in, ga.at[:, pl.ds(al(f * 512, 512), 512)], next(local_count))
    lg.start()

    def starts(r):
        return (11 * r + 1) // 2

    def weight_moves(k, taking):
        r = flip(f, k)
        sender, taker = (r, f) if taking else (f, r)
        rows = pl.ds(al(sender * 512, 512), 512)
        row_part = pl.ds(al(sender * 512 + z * TILE, TILE), TILE)
        own_part = pl.ds(al(z * TILE, TILE), TILE)
        begin = al(starts(taker) * TILE, TILE)
        tail = al(begin + MAIN, TILE)
        col = al(taker * T, T)
        moves = {
            "o": [(wo.at[pl.ds(col, T), :], w_o.at[:, rows])],
            "g": [(wg.at[:, pl.ds(begin, MAIN)], w_g.at[rows, pl.ds(0, MAIN)])],
            "g+": [(wg.at[:, pl.ds(tail, TILE)], w_g.at[rows, pl.ds(MAIN, TILE)])],
        }
        from_rows, to_rows = (pl.ds(0, 512), rows) if k == 0 else (own_part, row_part)
        moves["qkv"] = [
            (wq.at[from_rows, pl.ds(col, T)], w_qkv.at[to_rows, pl.ds(0, T)]),
            (wk.at[from_rows, :], w_qkv.at[to_rows, pl.ds(T, TILE)]),
            (wv.at[from_rows, :], w_qkv.at[to_rows, pl.ds(T + TILE, TILE)]),
        ]
        if k == 0:
            moves["u"] = [(wu.at[:, pl.ds(begin, MAIN)], w_u.at[rows, pl.ds(0, MAIN)])]
            moves["u+"] = [(wu.at[:, pl.ds(tail, TILE)], w_u.at[rows, pl.ds(MAIN, TILE)])]
            moves["d"] = [(wd.at[pl.ds(begin, MAIN), :], w_d.at[pl.ds(0, MAIN), rows])]
            moves["d+"] = [(wd.at[pl.ds(tail, TILE), :], w_d.at[pl.ds(MAIN, TILE), rows])]
        else:
            moves["u"] = [(wu.at[own_part, pl.ds(begin, MAIN)], w_u.at[row_part, pl.ds(0, MAIN)])]
            moves["u+"] = [(wu.at[own_part, pl.ds(tail, TILE)], w_u.at[row_part, pl.ds(MAIN, TILE)])]
            moves["d"] = [(wd.at[pl.ds(begin, MAIN), own_part], w_d.at[pl.ds(0, MAIN), row_part])]
            moves["d+"] = [(wd.at[pl.ds(tail, TILE), own_part], w_d.at[pl.ds(MAIN, TILE), row_part])]
        return moves

    w_counts = (("qkv", 3), ("o", 1), ("g", 1), ("g+", 1), ("u", 1), ("u+", 1), ("d", 1), ("d+", 1))
    w_sem = {(key, k, i): next(sems) for key, c in w_counts for k in (1, 2, 3) for i in range(c)}
    w_local = {(key, i): next(local_count) for key, c in w_counts for i in range(c)}

    def weights_each(key, taking, run):
        for k in (1, 2, 3):
            moves = weight_moves(k, taking)
            for i, (src, dst) in enumerate(moves[key]):
                run(remote(src, dst, w_sem[key, k, i], plane(k)))
            if key + "+" in moves:

                @pl.when((f if taking else flip(f, k)) % 2 == 0)
                def _():
                    (src, dst), = moves[key + "+"]
                    run(remote(src, dst, w_sem[key + "+", k, 0], plane(k)))

    def weights_start(key):
        weights_each(key, False, lambda cp: cp.start())

    def weights_wait(key):
        weights_each(key, True, lambda cp: cp.wait_recv())

    def weights_drain():
        for key in ("qkv", "o", "g", "u", "d"):
            weights_each(key, False, lambda cp: cp.wait_send())

    def weights_own(wait):
        moves = weight_moves(0, False)

        def run(key):
            for i, (src, dst) in enumerate(moves[key]):
                cp = here(src, dst, w_local[key, i])
                cp.wait() if wait else cp.start()

        for key in ("qkv", "o", "g", "u", "d"):
            run(key)

        @pl.when(f % 2 == 0)
        def _():
            for key in ("g+", "u+", "d+"):
                run(key)

    y_sem = {(key, k, j): next(sems) for key in ("qkv", "u", "d") for k in (1, 2, 3) for j in (1, 2, 3)}

    def column_each(key, taking, run):
        for k in (1, 2, 3):
            for j in (1, 2, 3):
                from_z = flip(z, j) if taking else z
                part = pl.ds(al(flip(f, k) * 512 + from_z * TILE, TILE), TILE)

                def move(size):
                    ref = w_u.at[part, pl.ds(0, size)] if key == "u" else w_d.at[pl.ds(0, size), part]
                    run(remote(ref, ref, y_sem[key, k, j], column(j)))

                if key == "qkv":
                    ref = w_qkv.at[part, :]
                    run(remote(ref, ref, y_sem[key, k, j], column(j)))
                    continue
                pl.when(f % 2 == 0)(functools.partial(move, WIN))
                pl.when(f % 2 == 1)(functools.partial(move, MAIN))

    g_sem = [[next(sems) for _ in range(3)] for _ in range(4)]
    f_sem = [[next(sems) for _ in range(4)] for _ in range(4)]

    def gather_start(g, buf, with_own, src=None):
        block = buf.at[rows_f, half]
        for k in (1, 2, 3):
            remote(block if src is None else src, block, g_sem[g][k - 1], plane(k)).start()
        if with_own:
            remote(block, block, f_sem[g][3], core).start()

    def gather_forward(g, buf):
        for k in (1, 2, 3):
            block = buf.at[rows_of(flip(f, k)), half]
            remote(block, block, g_sem[g][k - 1], plane(k)).wait_recv()
            remote(block, block, f_sem[g][k - 1], core).start()

    def gather_take(g, buf, k):
        if k == 0:
            block = buf.at[rows_f, rest]
            remote(block, block, f_sem[g][3], core).wait_recv()
        else:
            block = buf.at[rows_of(flip(f, k)), rest]
            remote(block, block, f_sem[g][k - 1], core).wait_recv()

    def gather_drain(g, buf, with_own, src=None):
        block = buf.at[rows_f, half]
        for k in (1, 2, 3):
            remote(block if src is None else src, block, g_sem[g][k - 1], plane(k)).wait_send()
            other = buf.at[rows_of(flip(f, k)), half]
            remote(other, other, f_sem[g][k - 1], core).wait_send()
        if with_own:
            remote(block, block, f_sem[g][3], core).wait_send()

    t_sem = [next(sems) for _ in range(3)]
    a_sem = [next(sems) for _ in range(3)]
    own_gain = ga.at[:, pl.ds(al(f * 512, 512), 512)]

    barrier = pltpu.get_barrier_semaphore()
    for k in (1, 2, 3):
        pl.semaphore_signal(barrier, inc=1, device_id=plane(k), device_id_type=MESH)
        pl.semaphore_signal(barrier, inc=1, device_id=column(k), device_id_type=MESH)
    pl.semaphore_signal(barrier, inc=1, device_id=core, device_id_type=MESH)
    pl.semaphore_wait(barrier, 7)

    lt.wait()
    lg.wait()
    for k in (1, 2, 3):
        remote(own_gain, own_gain, a_sem[k - 1], plane(k)).start()
        remote(tb.at[f], tb.at[f], t_sem[k - 1], plane(k)).start()
    weights_start("qkv")
    weights_own(False)

    @pl.when(f % 2 == 1)
    def _():
        w_g[:, MAIN:WIN] = jnp.zeros((W, TILE), BF)
        w_u[:, MAIN:WIN] = jnp.zeros((W, TILE), BF)
        w_d[MAIN:WIN, :] = jnp.zeros((TILE, W), BF)

    lx.wait()
    for k in (1, 2, 3):
        dst = ga.at[:, pl.ds(al(flip(f, k) * 512, 512), 512)]
        remote(dst, dst, a_sem[k - 1], plane(k)).wait_recv()

    STEP = 32

    def sub(i):
        return pl.ds(al(i * STEP, STEP), STEP)

    @pl.loop(0, T // STEP)
    def _(i):
        xs = xv[sub(i), :].astype(F32)
        scale = lax.rsqrt(jnp.mean(xs * xs, axis=-1, keepdims=True) + EPSILON)
        r1s[sub(i), :] = jnp.broadcast_to(scale, (STEP, TILE))
        x1[pl.ds(al(f * T + i * STEP, STEP), STEP), :] = (xs * scale * ga[0:1, :]).astype(BF)

    gather_start(0, x1, False)
    weights_wait("qkv")
    column_each("qkv", False, lambda cp: cp.start())
    for key in "oudg":
        weights_start(key)
    for k in (1, 2, 3):
        dst = tb.at[flip(f, k)]
        remote(dst, dst, t_sem[k - 1], plane(k)).wait_recv()
    weights_own(True)
    column_each("qkv", True, lambda cp: cp.wait_recv())

    lane = lax.broadcasted_iota(jnp.int32, (T, TILE), 1)
    low_lane = lane < HD
    first_half = lane % HD < HD // 2
    kv_head = f // 2

    def turns(b):
        cosine, sine = tb[b, 0:32, :], tb[b, 32:64, :]
        return (
            jnp.transpose(jnp.concatenate([cosine] * 4, 0)),
            jnp.transpose(jnp.concatenate([-sine, sine, -sine, sine], 0)),
        )

    def turn(v, c, s):
        swapped = jnp.where(first_half, pltpu.roll(v, TILE - 32, 1), pltpu.roll(v, 32, 1))
        return v * c + swapped * s

    def qkv_block(k):
        b = flip(f, k)
        qkv = nn(x1[rows_of(b), :], w_qkv[...])
        c, s = turns(b)
        for i in range(2):
            q = turn(qkv[:, i * TILE : (i + 1) * TILE], c, s) * 0.125
            q_buf[rows_of(b), i * TILE : (i + 1) * TILE] = q.astype(BF)
        key = turn(qkv[:, 2 * TILE : 3 * TILE], c, s)
        value = qkv[:, 3 * TILE :]
        key = jnp.where(kv_head == 0, key, pltpu.roll(key, HD, 1))
        value = jnp.where(kv_head == 1, value, pltpu.roll(value, HD, 1))
        kv_all[z, b, :, :] = jnp.where(low_lane, key, value).astype(BF)
        ids[z, pl.ds(b, 1), :] = tb[b, 64:65, :]

    qkv_block(0)
    gather_forward(0, x1)
    for k in (1, 2, 3):
        gather_take(0, x1, k)

    @pl.loop(1, 4)
    def _(k):
        qkv_block(k)

    z_sem = [[next(sems) for _ in range(2)] for _ in range(3)]
    for k in (1, 2, 3):
        remote(kv_all.at[z], kv_all.at[z], z_sem[k - 1][0], column(k)).start()
        remote(ids.at[z], ids.at[z], z_sem[k - 1][1], column(k)).start()
    for k in (1, 2, 3):
        zz = flip(z, k)
        remote(kv_all.at[zz], kv_all.at[zz], z_sem[k - 1][0], column(k)).wait_recv()
        remote(ids.at[zz], ids.at[zz], z_sem[k - 1][1], column(k)).wait_recv()
    lc.wait()
    weights_wait("u")
    column_each("u", False, lambda cp: cp.start())

    low_keys = lax.broadcasted_iota(jnp.int32, (4 * T, TILE), 1) < HD

    def bias_of(s):
        query_id = ids[z, pl.ds(s, 1), :]
        for j in range(4):
            key_id = jnp.transpose(jnp.broadcast_to(ids[j, pl.ds(s, 1), :], (8, T)))[:, 0:1]
            bias[j * T : (j + 1) * T, :] = jnp.where(key_id <= query_id, 0.0, NEGATIVE).astype(BF)

    def kv_of(s):
        kv = jnp.concatenate([kv_all[j, s, :, :] for j in range(4)], 0).astype(F32)
        turned = pltpu.roll(kv, HD, 1)
        keys = jnp.where(low_keys, kv, turned).astype(BF)
        values = jnp.where(low_keys, turned, kv).astype(BF)
        return kv, keys, values

    def only(v, parity):
        return jnp.where(low_lane if parity == 0 else ~low_lane, v.astype(F32), 0.0).astype(BF)

    @pl.loop(0, 4)
    def _(s):
        bias_of(s)
        kv, keys, _ = kv_of(s)
        values_t = jnp.transpose(kv)[HD:, :].astype(BF)

        for i in range(2):
            mixed = []
            for parity in range(2):
                q = only(q_buf[rows_of(s), i * TILE : (i + 1) * TILE], parity)
                scores = nt(keys, q) + bias[...].astype(F32)
                top = jnp.max(scores, axis=0, keepdims=True)
                raw = jnp.exp(scores - top)
                norm = jnp.sum(raw, axis=0, keepdims=True)
                lse[s, 2 * i + parity : 2 * i + parity + 1, :] = top + jnp.log(norm)
                weights = (raw * (1.0 / norm)).astype(BF)
                mixed.append(nn(values_t, weights))
            ob[rows_of(s), i * TILE : (i + 1) * TILE] = jnp.transpose(jnp.concatenate(mixed, 0)).astype(BF)

    p_sem = [[next(sems) for _ in range(4)]] * 4
    s_sem = [[next(sems) for _ in range(3)]] * 4
    COLS = 256

    def scatter_start(u, product):
        p0, s0 = p_sem[u][0], s_sem[u][0]

        @pl.loop(0, 4)
        def _(i):
            k = (i + 1) % 4
            b = flip(f, k)

            @pl.loop(0, H // COLS)
            def _(j):
                ps[k, :, pl.ds(al(j * COLS, COLS), COLS)] = product(b, (1 - t) * H + j * COLS).astype(BF)

            remote(ps.at[k], pr.at[k], p0 + k, core).start()

        def own(k, j):
            b = flip(f, k)
            cols = pl.ds(al(j * COLS, COLS), COLS)
            return product(b, t * H + j * COLS) + pr[k, :, cols].astype(F32)

        @pl.loop(1, 4)
        def _(k):
            remote(ps.at[k], pr.at[k], p0 + k, core).wait()

            @pl.loop(0, H // COLS)
            def _(j):
                ps[k, :, pl.ds(al(j * COLS, COLS), COLS)] = own(k, j).astype(BF)

            remote(ps.at[k], rr.at[k - 1], s0 + k - 1, plane(k)).start()

        remote(ps.at[0], pr.at[0], p0, core).wait()

        @pl.loop(0, H // COLS)
        def _(j):
            yo[:, pl.ds(al(j * COLS, COLS), COLS)] = own(0, j)

    def scatter_wait(u):
        for k in (1, 2, 3):
            remote(ps.at[k], rr.at[k - 1], s_sem[u][k - 1], plane(k)).wait()

    def scattered(i):
        return yo[sub(i), :] + rr[0, sub(i), :].astype(F32) + rr[1, sub(i), :].astype(F32) + rr[2, sub(i), :].astype(F32)

    n_sem = [next(sems) for _ in range(3)]

    def core_sums(u):
        remote(ss_own.at[u], ss_other.at[u], n_sem[u], core).start()
        remote(ss_own.at[u], ss_other.at[u], n_sem[u], core).wait()

    weights_wait("d")
    column_each("d", False, lambda cp: cp.start())
    weights_wait("o")
    scatter_start(0, lambda b, c: nn(ob[rows_of(b), :], w_o[:, pl.ds(al(c, COLS), COLS)]))
    scatter_wait(0)

    @pl.loop(0, T // STEP)
    def _(i):
        rows = xv[sub(i), half].astype(F32) + scattered(i)
        hid[sub(i), :] = rows
        ss_own[0, sub(i), :] = jnp.broadcast_to(jnp.sum(rows * rows, axis=-1, keepdims=True), (STEP, TILE))

    core_sums(0)
    gain_one, gain_two = ga[0:1, half], ga[1:2, half]

    @pl.loop(0, T // STEP)
    def _(i):
        scale = lax.rsqrt((ss_own[0, sub(i), 0:1] + ss_other[0, sub(i), 0:1]) * (1.0 / W) + EPSILON)
        r2s[sub(i), :] = jnp.broadcast_to(scale, (STEP, TILE))
        x2[pl.ds(al(f * T + i * STEP, STEP), STEP), half] = (hid[sub(i), :] * scale * gain_two).astype(BF)

    gather_start(2, x2, True)
    gather_start(1, ct, False, cot_in.at[0, :, half])
    weights_wait("g")
    column_each("u", True, lambda cp: cp.wait_recv())
    gather_forward(2, x2)
    gather_take(2, x2, 0)

    UNITS = 256

    def feed_block(k):
        b = flip(f, k)

        @pl.loop(0, WIN // UNITS)
        def _(j):
            cols = pl.ds(al(j * UNITS, UNITS), UNITS)
            gate = nn(x2[rows_of(b), :], w_g[:, cols])
            up = nn(x2[rows_of(b), :], w_u[:, cols])
            sigma = jax.nn.sigmoid(gate)
            silu = gate * sigma
            act[rows_of(b), cols] = (silu * up).astype(BF)
            dg[rows_of(b), cols] = (up * sigma * (1.0 + gate * (1.0 - sigma))).astype(BF)
            du[rows_of(b), cols] = silu.astype(BF)

    feed_block(0)
    for k in (1, 2, 3):
        gather_take(2, x2, k)

    @pl.loop(1, 4)
    def _(k):
        feed_block(k)

    gather_forward(1, ct)
    for k in (1, 2, 3):
        gather_take(1, ct, k)

    GROUPS = ("dA", "dB", "gA", "gB", "uA", "uB", "o", "q", "k")
    e_sem = {(name, i): [next(sems) for _ in range(3)][0] for name in GROUPS for i in range(2 if name[-1] == "B" else 1)}
    e_local = {(name, i): next(local_count) for name in GROUPS for i in range(2 if name[-1] == "B" else 1)}

    def stage(name, k):
        if name == "d":
            return gs_d.at[pl.ds(al(k * WIN, WIN), WIN), :]
        if name in "gu":
            return ct.at[pl.ds(al((k // 2) * 512, 512), 512), pl.ds(al((k % 2) * H, H), WIN)]
        if name == "o":
            return gs_d.at[pl.ds(al(k * WIN, WIN), T), :]
        return x2.at[pl.ds(al((k // 2) * 512, 512), 512), pl.ds(al((k % 2) * 512 + (0 if name == "q" else T), T), T)]

    def grad_moves(group, k, sender):
        name = group[0]
        buf, begin = stage(name, k), al(starts(sender) * TILE, TILE)
        if name in "dgu":
            parts = [(0, PART)] if group[1] == "A" else [(PART, MAIN - PART), (MAIN, TILE)]
            if name == "d":
                return [(buf.at[pl.ds(c, size), :], first["d"].at[pl.ds(al(begin + c, TILE), size), :]) for c, size in parts]
            return [(buf.at[:, pl.ds(c, size)], first[name].at[:, pl.ds(al(begin + c, TILE), size)]) for c, size in parts]
        if name == "o":
            return [(buf, first["o"].at[rows_of(sender), :])]
        if name == "q":
            return [(buf, first["q"].at[:, rows_of(sender)])]
        return [(buf, kv_g.at[k - 1])]

    def grad_send(group, k, act_on):
        for i, (src, dst) in enumerate(grad_moves(group, k, f)):

            def run(i=i, src=src, dst=dst):
                if isinstance(k, int) and k == 0:
                    cp = here(src, dst, e_local[group, i])
                    cp.wait() if act_on == "wait" else cp.start()
                else:
                    cp = remote(src, dst, e_sem[group, i] + k - 1, plane(k))
                    cp.wait_send() if act_on == "wait" else cp.start()

            if i == 0:
                run()
            else:
                pl.when(f % 2 == 0)(run)

    def grad_take(group):
        for k in (1, 2, 3):
            sender = flip(f, k)
            for i, (src, dst) in enumerate(grad_moves(group, k, sender)):

                def run(i=i, src=src, dst=dst):
                    remote(src, dst, e_sem[group, i] + k - 1, plane(k)).wait_recv()

                if i == 0:
                    run()
                else:
                    pl.when(sender % 2 == 0)(run)

    def sent(*groups):
        for group in groups:
            for k in (1, 2, 3):
                grad_send(group, k, "wait")

    def block_cols(k):
        return pl.ds(al(flip(f, k) * 512, 512), 512)

    def each_owner(run):
        @pl.loop(1, 4)
        def _(k):
            run(k)

        run(0)

    def down_grads(which):
        c = 0 if which == "A" else PART

        def run(k):
            stage("d", k)[c : c + PART, :] = tn(act[:, c : c + PART], ct[:, block_cols(k)]).astype(BF)
            grad_send("d" + which, k, "start")

        each_owner(run)

    def feed_grads(name, which, right):
        c = 0 if which == "A" else PART

        def run(k):
            @pl.loop(0, 2)
            def _(i):
                xs = x2[:, pl.ds(al(flip(f, k) * 512 + i * T, T), T)]
                stage(name, k)[pl.ds(al(i * T, T), T), c : c + PART] = tn(xs, right[:, c : c + PART]).astype(BF)

            grad_send(name + which, k, "start")

        each_owner(run)

    down_grads("A")

    column_each("d", True, lambda cp: cp.wait_recv())

    @pl.loop(0, 4)
    def _(b):
        @pl.loop(0, WIN // UNITS)
        def _(j):
            cols = pl.ds(al(j * UNITS, UNITS), UNITS)
            back = nt(ct[rows_of(b), :], w_d[cols, :])
            dg[rows_of(b), cols] = (back * dg[rows_of(b), cols].astype(F32)).astype(BF)
            du[rows_of(b), cols] = (back * du[rows_of(b), cols].astype(F32)).astype(BF)

    scatter_start(1, lambda b, c: nt(dg[rows_of(b), :], w_g[pl.ds(al(c, COLS), COLS), :]) + nt(du[rows_of(b), :], w_u[pl.ds(al(c, COLS), COLS), :]))
    end = (z == 0) | (z == 3)
    middle = (z == 1) | (z == 2)
    next_in = (f, jnp.where(z < 2, 1, 2), t)
    next_out = (f, jnp.where(z < 2, 0, 3), t)
    facing = (f, 3 - z, t)
    across = [next(sems) for _ in range(6)]
    l_sem = [[next(sems), across[i % 6], next(sems)] for i in range(len(CHUNKS))]
    v_sem = [next(local_count) for _ in range(2)]
    o_sem = [next(local_count) for _ in range(4)]
    DEPTH, LAG = 3, 2

    def square(buf, i):
        return buf.at[pl.ds(i * 512, 512), pl.ds(0, 512)]

    ring, la = [square(w_u, i) for i in range(DEPTH)], square(w_u, 3)
    tt, lb = [square(w_g, i) for i in range(2)], square(w_g, 2)

    def d_kv_place(j):
        return w_g.at[pl.ds(al(j // 2 * 4 * T, T), 4 * T), pl.ds(al(512 + j % 2 * TILE, TILE), TILE)]


    def window(arrays, i):
        _, name, r, c, rows, cols = CHUNKS[i]
        return arrays[name].at[pl.ds(r, rows), pl.ds(c, cols)]

    def line_send(group):
        @pl.when(end)
        def _():
            for i, chunk in enumerate(CHUNKS):
                if chunk[0] == group:
                    remote(window(first, i), window(left, i), l_sem[i][0], next_in).start()

    def add_into(dst, a, b, rows, cols):
        @pl.loop(0, rows // STEP)
        def _(i):
            at = sub(i)
            dst[at, pl.ds(0, cols)] = (a[at, pl.ds(0, cols)].astype(F32) + b[at, pl.ds(0, cols)].astype(F32)).astype(BF)

    def line_one(i):
        _, name, r, c, rows, cols = CHUNKS[i]
        part = (pl.ds(0, rows), pl.ds(0, cols))
        a, b, keep = la.at[part], lb.at[part], ring[i % DEPTH]

        @pl.when(middle)
        def _():
            get_a = here(window(first, i), a, v_sem[0])
            get_a.start()
            remote(window(first, i), window(left, i), l_sem[i][0], next_in).wait_recv()
            get_b = here(window(left, i), b, v_sem[1])
            get_b.start()
            get_a.wait()
            get_b.wait()
            add_into(keep, la, lb, rows, cols)
            remote(keep.at[part], window(cross, i), l_sem[i][1], facing).start()

    def line_two(i):
        _, name, r, c, rows, cols = CHUNKS[i]
        part = (pl.ds(0, rows), pl.ds(0, cols))
        keep, done = ring[i % DEPTH], tt[i % 2]

        @pl.when(middle)
        def _():
            remote(keep.at[part], window(cross, i), l_sem[i][1], facing).wait()
            get = here(window(cross, i), lb.at[part], v_sem[1])
            get.start()
            if i >= 2:
                line_out(i - 2)
            get.wait()
            add_into(done, keep, lb, rows, cols)
            remote(done.at[part], window(total, i), l_sem[i][2], next_out).start()
            here(done.at[part], window(total, i), o_sem[i % 4]).start()

    def line_out(i):
        _, name, r, c, rows, cols = CHUNKS[i]
        done = tt[i % 2].at[pl.ds(0, rows), pl.ds(0, cols)]
        remote(done, window(total, i), l_sem[i][2], next_out).wait_send()
        here(done, window(total, i), o_sem[i % 4]).wait()

    pumped, ready = [0], set()

    def pump(count):
        for i in range(pumped[0], pumped[0] + count):
            if i < len(CHUNKS):
                assert CHUNKS[i][0] in ready
                line_one(i)
            if LAG <= i < len(CHUNKS) + LAG:
                line_two(i - LAG)
        pumped[0] += count

    def grad_ready(group):
        grad_take(group)
        grad_send(group, 0, "wait")
        line_send(group)
        ready.add(group)

    grad_ready("dA")
    down_grads("B")
    gather_drain(1, ct, False, cot_in.at[0, :, half])
    feed_grads("g", "A", dg)
    column_each("u", False, lambda cp: cp.wait_send())
    pump(2)
    scatter_wait(1)
    lh.wait()

    def norm_two_back(i, carry):
        rows = scattered(i)
        yo[sub(i), :] = rows
        hat = hid[sub(i), :] * r2s[sub(i), 0:1]
        ss_own[1, sub(i), :] = jnp.broadcast_to(jnp.sum(rows * gain_two * hat, axis=-1, keepdims=True), (STEP, TILE))
        return carry + jnp.sum(rows * hat, axis=0, keepdims=True)

    g_sum[...] = jnp.zeros((8, H), F32)
    g_sum[1:2, :] = lax.fori_loop(0, T // STEP, norm_two_back, jnp.zeros((1, H), F32))
    core_sums(1)

    @pl.loop(0, T // STEP)
    def _(i):
        scale = r2s[sub(i), 0:1]
        hat = hid[sub(i), :] * scale
        mean = (ss_own[1, sub(i), 0:1] + ss_other[1, sub(i), 0:1]) * (1.0 / W)
        rows = out_s[sub(i), :].astype(F32) + scale * (yo[sub(i), :] * gain_two - hat * mean)
        d_hid[sub(i), :] = rows
        dh[pl.ds(al(f * T + i * STEP, STEP), STEP), half] = rows.astype(BF)

    gather_start(3, dh, True)
    feed_grads("g", "B", dg)
    pump(1)
    grad_ready("dB")
    pump(2)
    grad_ready("gA")
    pump(4)
    gather_forward(3, dh)
    for k in range(4):
        gather_take(3, dh, k)
    pump(1)
    sent("dA", "dB")

    def out_grads(k):
        stage("o", k)[...] = tn(ob[...], dh[:, block_cols(k)]).astype(BF)
        grad_send("o", k, "start")

    each_owner(out_grads)

    @pl.loop(0, 4)
    def _(b):
        ob[rows_of(b), :] = nt(dh[rows_of(b), :], w_o[...]).astype(BF)

    d_ob, d_qkv = ob, dg
    gather_drain(2, x2, True)

    def attend_back(s):
        bias_of(s)
        kv, keys, values = kv_of(s)
        keys_t = jnp.transpose(kv)[:HD, :].astype(BF)
        c, sn = turns(s)
        d_key = jnp.zeros((4 * T, TILE), F32)
        d_value = jnp.zeros((4 * T, TILE), F32)
        for i in range(2):
            d_query = []
            for parity in range(2):
                q = only(q_buf[rows_of(s), i * TILE : (i + 1) * TILE], parity)
                do = only(d_ob[rows_of(s), i * TILE : (i + 1) * TILE], parity)
                weights = jnp.exp(nt(keys, q) + bias[...].astype(F32) - lse[s, 2 * i + parity : 2 * i + parity + 1, :])
                d_weights = nt(values, do)
                delta = jnp.sum(weights * d_weights, axis=0, keepdims=True)
                d_scores = (weights * (d_weights - delta)).astype(BF)
                d_value = d_value + nn(weights.astype(BF), do)
                d_key = d_key + nn(d_scores, q)
                d_query.append(nn(keys_t, d_scores))
            d_query = jnp.transpose(jnp.concatenate(d_query, 0)) * 0.125
            d_qkv[rows_of(s), i * TILE : (i + 1) * TILE] = turn(d_query, c, -sn).astype(BF)
        d_key = d_key + pltpu.roll(d_key, HD, 1)
        d_value = d_value + pltpu.roll(d_value, HD, 1)
        both = jnp.where(low_keys, d_key, d_value)
        own = both[0:T, :]
        for j in range(1, 4):
            own = jnp.where(z == j, both[j * T : (j + 1) * T, :], own)
        d_kv[s, :, :] = own
        for j in range(4):
            d_kv_place(j)[rows_of(s), :] = both[j * T : (j + 1) * T, :].astype(BF)

    attend_back(0)
    pump(1)
    attend_back(1)
    grad_ready("gB")
    pump(1)
    sent("gA", "gB")
    feed_grads("u", "A", du)
    attend_back(2)
    pump(1)
    attend_back(3)
    k_sem = [next(sems) for _ in range(3)]
    for k in (1, 2, 3):
        remote(d_kv_place(flip(z, k)), d_kv_recv.at[k - 1], k_sem[k - 1], column(k)).start()
    pump(1)
    feed_grads("u", "B", du)
    pump(1)
    grad_ready("o")
    grad_ready("uA")
    pump(3)
    for k in (1, 2, 3):
        remote(d_kv_place(flip(z, k)), d_kv_recv.at[k - 1], k_sem[k - 1], column(k)).wait()
    here_half = (lane // HD) == kv_head

    @pl.loop(0, 4)
    def _(s):
        c, sn = turns(s)
        whole = d_kv[s, :, :]
        for k in range(3):
            whole = whole + d_kv_recv[k, rows_of(s), :].astype(F32)
        turned = pltpu.roll(whole, HD, 1)
        d_key = turn(jnp.where(low_lane, whole, turned), c, -sn)
        d_value = jnp.where(low_lane, turned, whole)
        d_qkv[rows_of(s), 2 * TILE : 3 * TILE] = jnp.where(here_half, d_key, 0.0).astype(BF)
        d_qkv[rows_of(s), 3 * TILE : 4 * TILE] = jnp.where(here_half, d_value, 0.0).astype(BF)

    def qkv_grads(k):
        @pl.loop(0, 2)
        def _(i):
            xs = x1[:, pl.ds(al(flip(f, k) * 512 + i * T, T), T)]
            grads = tn(xs, d_qkv[:, 0:512]).astype(BF)
            stage("q", k)[pl.ds(al(i * T, T), T), :] = grads[:, 0:T]
            stage("k", k)[pl.ds(al(i * T, T), T), :] = grads[:, T:]

        grad_send("q", k, "start")
        if not (isinstance(k, int) and k == 0):
            grad_send("k", k, "start")

    each_owner(qkv_grads)
    pump(1)
    scatter_start(2, lambda b, c: nt(d_qkv[rows_of(b), 0:512], w_qkv[pl.ds(al(c, COLS), COLS), :]))
    grad_ready("uB")
    pump(2)
    grad_ready("q")
    grad_take("k")

    @pl.loop(0, 512 // STEP)
    def _(i):
        rows = x2[sub(i), T : 2 * T].astype(F32)
        for k in (1, 2, 3):
            rows = rows + kv_g[k - 1, sub(i), :].astype(F32)
        x2[sub(i), T : 2 * T] = rows.astype(BF)

    kv_copy = here(x2.at[pl.ds(0, 512), pl.ds(T, T)], first["k"], next(local_count))
    kv_copy.start()
    kv_copy.wait()
    line_send("k")
    ready.add("k")
    pump(4)
    scatter_wait(2)

    def norm_one_back(i, carry):
        rows = scattered(i)
        yo[sub(i), :] = rows
        hat = xv[sub(i), half].astype(F32) * r1s[sub(i), 0:1]
        ss_own[2, sub(i), :] = jnp.broadcast_to(jnp.sum(rows * gain_one * hat, axis=-1, keepdims=True), (STEP, TILE))
        return carry + jnp.sum(rows * hat, axis=0, keepdims=True)

    g_sum[0:1, :] = lax.fori_loop(0, T // STEP, norm_one_back, jnp.zeros((1, H), F32))
    for k in (1, 2, 3):
        pl.semaphore_signal(credit, inc=1, device_id=plane(k), device_id_type=MESH)
    pl.semaphore_signal(credit, inc=1, device_id=core, device_id_type=MESH)
    core_sums(2)

    q_sem = [[next(sems) for _ in range(3)] for _ in range(2)]
    g_plane[f, :, :] = g_sum[...]
    for k in (1, 2, 3):
        remote(g_sum, g_plane.at[f], q_sem[0][k - 1], plane(k)).start()

    @pl.loop(0, T // STEP)
    def _(i):
        scale = r1s[sub(i), 0:1]
        hat = xv[sub(i), half].astype(F32) * scale
        mean = (ss_own[2, sub(i), 0:1] + ss_other[2, sub(i), 0:1]) * (1.0 / W)
        d_hid[sub(i), :] = d_hid[sub(i), :] + scale * (yo[sub(i), :] * gain_one - hat * mean)

    in_local = here(d_hid, in_grad_ref.at[:, half], next(local_count))
    in_local.start()
    in_remote = remote(d_hid, in_grad_ref.at[:, half], next(sems), core)
    in_remote.start()
    pump(1)
    pl.semaphore_wait(credit, 4)
    scatter_start(3, lambda b, c: nn(act[rows_of(b), :], w_d[:, pl.ds(al(c, COLS), COLS)]))
    pump(2)
    for k in (1, 2, 3):
        remote(g_sum, g_plane.at[flip(f, k)], q_sem[0][k - 1], plane(k)).wait_recv()
    g_column[z, :, :] = ((g_plane[0, :, :] + g_plane[1, :, :]) + g_plane[2, :, :]) + g_plane[3, :, :]
    for k in (1, 2, 3):
        remote(g_column.at[z], g_column.at[z], q_sem[1][k - 1], column(k)).start()
    scatter_wait(3)

    @pl.loop(0, T // STEP)
    def _(i):
        out_s[sub(i), :] = (hid[sub(i), :] + scattered(i)).astype(BF)

    out_local = here(out_s, out_ref.at[:, half], next(local_count))
    out_local.start()
    out_remote = remote(out_s, out_ref.at[:, half], next(sems), core)
    out_remote.start()
    pump(2)
    for k in (1, 2, 3):
        remote(g_column.at[z], g_column.at[flip(z, k)], q_sem[1][k - 1], column(k)).wait_recv()
    g_whole[:, half] = ((g_column[0, :, :] + g_column[1, :, :]) + g_column[2, :, :]) + g_column[3, :, :]
    w_move = remote(g_whole.at[:, half], g_whole.at[:, half], next(sems), core)
    w_move.start()
    w_move.wait()
    gain_move = here(g_whole.at[:, pl.ds(al(f * 512, 512), 512)], gain_ref, next(local_count))
    gain_move.start()
    pump(len(CHUNKS) + LAG - pumped[0])

    @pl.when(middle)
    def _():
        line_out(len(CHUNKS) - 2)
        line_out(len(CHUNKS) - 1)

    @pl.when(end)
    def _():
        for i in range(len(CHUNKS)):
            remote(window(first, i), window(left, i), l_sem[i][0], next_in).wait_send()
            remote(window(total, i), window(total, i), l_sem[i][2], next_in).wait_recv()

    gain_move.wait()
    out_local.wait()
    out_remote.wait()
    in_local.wait()
    in_remote.wait()
    weights_drain()
    column_each("d", False, lambda cp: cp.wait_send())
    column_each("qkv", False, lambda cp: cp.wait_send())
    gather_drain(0, x1, False)
    gather_drain(3, dh, True)
    for k in (1, 2, 3):
        remote(own_gain, own_gain, a_sem[k - 1], plane(k)).wait_send()
        remote(tb.at[f], tb.at[f], t_sem[k - 1], plane(k)).wait_send()
        remote(kv_all.at[z], kv_all.at[z], z_sem[k - 1][0], column(k)).wait_send()
        remote(ids.at[z], ids.at[z], z_sem[k - 1][1], column(k)).wait_send()
        remote(g_sum, g_plane.at[f], q_sem[0][k - 1], plane(k)).wait_send()
        remote(g_column.at[z], g_column.at[z], q_sem[1][k - 1], column(k)).wait_send()
        for name in ("uA", "uB", "o", "q", "k"):
            grad_send(name, k, "wait")
    assert (next(sems), next(local_count)) == (REMOTE_SEMS, LOCAL_SEMS)


REMOTE_SEMS, LOCAL_SEMS = 219, 37


def layer_call(inputs, positions, blocks, cotangent, attn_gain, w_query, w_key, w_value, w_out, mlp_gain, w_gate, w_up, w_down):
    frequency = jnp.exp(jnp.arange(HD // 2, dtype=F32) * (-2.0 * math.log(10000.0) / HD))
    turned = frequency[:, None] * positions.astype(F32)
    table = jnp.concatenate([jnp.cos(turned), jnp.sin(turned), jnp.broadcast_to(blocks.astype(F32), (8, T))], 0)
    gains = jnp.concatenate([attn_gain[None], mlp_gain[None], jnp.zeros((6, 512), BF)], 0).astype(F32)
    shape = jax.ShapeDtypeStruct
    grads = [shape((rows, cols), BF) for _, rows, cols in GRADS]
    any_spec = pl.BlockSpec(memory_space=pl.ANY)
    v = pltpu.VMEM
    results = pl.pallas_call(
        layer_kernel,
        out_shape=[shape((T, W), BF), shape((T, W), F32), shape((8, 512), F32)] + grads * 4,
        in_specs=[any_spec] * 11,
        out_specs=[any_spec] * 27,
        scratch_shapes=[
            v((4 * T, W), BF), v((4 * T, W), BF), v((4 * T, W), BF), v((4 * T, W), BF),
            v((W, 512), BF), v((T, W), BF), v((W, WIN), BF), v((W, WIN), BF), v((WIN, W), BF),
            v((4 * T, WIN), BF), v((4 * T, WIN), BF), v((4 * T, WIN), BF),
            v((4 * T, T), BF), v((4, 4, T, TILE), BF), v((4 * T, T), BF),
            v((4, T, H), BF), v((4, T, H), BF), v((3, T, H), BF), v((T, H), F32), v((T, H), F32), v((T, H), F32), v((T, W), BF),
            v((4, 72, T), F32), v((8, W), F32), v((4, 8, T), F32), v((T, TILE), F32), v((T, TILE), F32),
            v((3, T, TILE), F32), v((3, T, TILE), F32), v((4, 8, T), F32), v((4 * T, T), BF),
            v((4 * WIN, 512), BF), v((3, 512, T), BF),
            v((4, T, TILE), F32), v((3, 4 * T, TILE), BF),
            v((T, H), BF), v((8, H), F32), v((4, 8, H), F32), v((4, 8, H), F32), v((8, W), F32),
            pltpu.SemaphoreType.DMA((REMOTE_SEMS,)), pltpu.SemaphoreType.DMA((REMOTE_SEMS,)),
            pltpu.SemaphoreType.DMA((LOCAL_SEMS,)), pltpu.SemaphoreType.REGULAR,
        ],
        compiler_params=pltpu.CompilerParams(collective_id=0, has_side_effects=True, vmem_limit_bytes=62 << 20),
    )(inputs, table, gains, cotangent, w_query, w_key, w_value, w_out, w_gate, w_up, w_down)
    output, input_grad, gain_grads = results[:3]
    down, gate, up, out, query, kv = (r.astype(F32) for r in results[-6:])
    return (output[None], input_grad[None], gain_grads[0], query, kv[:, :TILE], kv[:, TILE:], out, gain_grads[1], gate, up, down)


def solution(mesh):
    n, m = mesh.shape["fsdp"], mesh.shape["ctx"]

    def step(*args):
        return layer_call(*args) if n == m == 4 else local(n, m, *args)

    return jax.shard_map(
        step,
        mesh=mesh,
        in_specs=(
            P("fsdp", "ctx", None),
            P("fsdp", "ctx"),
            P("fsdp", "ctx"),
            P("fsdp", "ctx", None),
            P("fsdp"),
            P("fsdp", "tp"),
            P("fsdp", "tp"),
            P("fsdp", "tp"),
            P("tp", "fsdp"),
            P("fsdp"),
            P("fsdp", "tp"),
            P("fsdp", "tp"),
            P("tp", "fsdp"),
        ),
        out_specs=(
            P("fsdp", "ctx", None),
            P("fsdp", "ctx", None),
            P("fsdp"),
            P("fsdp", "tp"),
            P("fsdp", "tp"),
            P("fsdp", "tp"),
            P("tp", "fsdp"),
            P("fsdp"),
            P("fsdp", "tp"),
            P("fsdp", "tp"),
            P("tp", "fsdp"),
        ),
        check_vma=False,
    )
```

```python
import functools
import math

import jax
import jax.numpy as jnp
from jax import lax
from jax.experimental import pallas as pl
from jax.experimental.pallas import tpu as pltpu
from jax.sharding import PartitionSpec as P

HD = 64
EPSILON = 1e-05
NEGATIVE = -1e30
BF = jnp.bfloat16
F32 = jnp.float32


def dot(a, b, ca, cb):
    return lax.dot_general(a, b, (((ca,), (cb,)), ((), ())), preferred_element_type=F32)


def angles(positions):
    half = HD // 2
    frequency = jnp.exp(jnp.arange(half, dtype=F32) * (-2.0 * math.log(10000.0) / HD))
    turned = positions.astype(F32)[:, None] * frequency[None, :]
    return jnp.cos(turned)[:, None, :], jnp.sin(turned)[:, None, :]


def rotate(values, cosine, sine):
    half = HD // 2
    a, b = values[..., :half], values[..., half:]
    return jnp.concatenate([a * cosine - b * sine, b * cosine + a * sine], axis=-1)


def gated(values, after):
    return lax.optimization_barrier((values, after))[0]


def local(n, m, inputs, positions, blocks, cotangent, attn_gain, w_query, w_key, w_value, w_out, mlp_gain, w_gate, w_up, w_down):
    f = lax.axis_index("fsdp")
    z = lax.axis_index("ctx")
    t = lax.axis_index("tp")
    tokens, width = inputs.shape[1:]
    half = width // 2
    peers = range(1, n)

    def plane(x, k):
        return x if k == 0 else lax.ppermute(x, "fsdp", [(i, i ^ k) for i in range(n)])

    def column(x, k):
        return x if k == 0 else lax.ppermute(x, "ctx", [(i, i ^ k) for i in range(m)])

    def swap(x):
        return lax.ppermute(x, "tp", [(0, 1), (1, 0)])

    def part(x, index, axis):
        size = x.shape[axis] // n
        return lax.dynamic_slice_in_dim(x, index * size, size, axis)

    def mine(x, which):
        return lax.dynamic_slice_in_dim(x, which * half, half, x.ndim - 1)

    def place(pieces, axis):
        size = pieces[0].shape[axis]
        shape = list(pieces[0].shape)
        shape[axis] = size * n
        whole = jnp.zeros(shape, pieces[0].dtype)
        for k in range(n):
            whole = lax.dynamic_update_slice_in_dim(whole, pieces[k], (f ^ k) * size, axis)
        return whole

    def join(own, other):
        return jnp.where(t == 0, jnp.concatenate([own, other], -1), jnp.concatenate([other, own], -1))

    def gather(x):
        rows = jnp.concatenate([plane(x, k) for k in range(n)], 0)
        return join(rows, swap(rows))

    def scatter(partial):
        own = mine(partial, t) + swap(mine(partial.astype(BF), 1 - t)).astype(F32)
        low = own.astype(BF)
        total = own[:tokens]
        for k in peers:
            total = total + plane(low[k * tokens : (k + 1) * tokens], k).astype(F32)
        return total

    def row_mean(own):
        own = jnp.sum(own, -1)
        return ((own + swap(own)) / width)[:, None]

    x = inputs[0].astype(F32)
    gains = jnp.stack([attn_gain, mlp_gain])
    gains = place([plane(gains, k) for k in range(n)], 1).astype(F32)
    marks = jnp.stack([positions[0], blocks[0]])
    marks = [plane(marks, k) for k in range(n)]
    place_rows = jnp.concatenate([mk[0] for mk in marks])
    query_ids = jnp.stack([mk[1] for mk in marks])
    scale_one = lax.rsqrt(jnp.mean(x * x, axis=-1, keepdims=True) + EPSILON)
    x_half = mine(x, t)
    hat_one = x_half * scale_one
    gain_one, gain_two = mine(gains[0:1], t), mine(gains[1:2], t)
    xn_one = gather((hat_one * gain_one).astype(BF))

    heads = w_query.shape[1] // HD // n
    cols = heads * HD
    kv_pair = jnp.concatenate([w_key, w_value], 1)
    kv_heads = w_key.shape[1] // HD
    w_qkv = place([plane(jnp.concatenate([part(w_query, f ^ k, 1), kv_pair], 1), k) for k in range(n)], 0)
    wo = gated(w_out, xn_one)
    wo = place([plane(part(wo, f ^ k, 0), k) for k in range(n)], 1)
    gate_up = gated((w_gate, w_up), xn_one)
    gate_up = [plane(jnp.stack([part(gate_up[0], f ^ k, 1), part(gate_up[1], f ^ k, 1)]), k) for k in range(n)]
    wg = place([g[0] for g in gate_up], 0)
    wu = place([g[1] for g in gate_up], 0)

    qkv = dot(xn_one, w_qkv, 1, 0)
    cosine, sine = angles(place_rows)
    kv_here = (heads * f) // ((w_query.shape[1] // HD) // kv_heads)

    def pick(both):
        out = both[:, :HD]
        for g in range(1, kv_heads):
            out = jnp.where(kv_here == g, both[:, g * HD : (g + 1) * HD], out)
        return out

    kw = kv_heads * HD
    query = rotate(qkv[:, :cols].reshape(-1, heads, HD), cosine, sine).astype(BF)
    key = rotate(pick(qkv[:, cols : cols + kw])[:, None, :], cosine, sine)[:, 0, :].astype(BF)
    value = pick(qkv[:, cols + kw :]).astype(BF)
    key_value = jnp.concatenate([key, value], 1).reshape(n, tokens, 2 * HD)
    kv_all = jnp.concatenate([column(key_value, k) for k in range(m)], 1)
    ids_all = jnp.concatenate([column(query_ids, k) for k in range(m)], 1)
    keys, values = kv_all[..., :HD], kv_all[..., HD:]
    factor = 1.0 / math.sqrt(HD)
    query = query.reshape(n, tokens, heads, HD)
    allowed = (ids_all[:, None, :] <= query_ids[:, :, None])[:, None]
    scores = jnp.einsum("nthd,nsd->nhts", query, keys, preferred_element_type=F32) * factor
    scores = jnp.where(allowed, scores, NEGATIVE)
    top = jnp.max(scores, -1, keepdims=True)
    raw = jnp.where(allowed, jnp.exp(scores - top), 0.0)
    weights = raw / jnp.sum(raw, -1, keepdims=True)
    weights_low = weights.astype(BF)
    attended = jnp.einsum("nhts,nsd->nthd", weights_low, values, preferred_element_type=F32)
    attended_low = attended.astype(BF).reshape(n * tokens, cols)

    hidden = x_half + scatter(dot(attended_low, wo, 1, 0))
    scale_two = lax.rsqrt(row_mean(hidden * hidden) + EPSILON)
    hat_two = hidden * scale_two
    xn_two = gather((hat_two * gain_two).astype(BF))
    cot = gather(gated(mine(cotangent[0], t), wg))
    wd = gated(w_down, wg)
    wd = place([plane(part(wd, f ^ k, 0), k) for k in range(n)], 1)
    gate = dot(xn_two, wg, 1, 0)
    up = dot(xn_two, wu, 1, 0)
    sigma = jax.nn.sigmoid(gate)
    silu = gate * sigma
    act = (silu * up).astype(BF)
    dact = dot(cot, wd, 1, 1)
    dgate = (dact * up * sigma * (1.0 + gate * (1.0 - sigma))).astype(BF)
    dup = (dact * silu).astype(BF)

    def reduce(piece):
        if m != 4:
            return lax.psum(piece, "ctx")
        one = (piece.astype(F32) + lax.ppermute(piece, "ctx", [(0, 1), (3, 2)]).astype(F32)).astype(BF)
        two = (one.astype(F32) + lax.ppermute(one, "ctx", [(1, 2), (2, 1)]).astype(F32)).astype(BF)
        three = lax.ppermute(two, "ctx", [(1, 0), (2, 3)])
        return jnp.where((z == 0) | (z == 3), three, two)

    def share(grad, axis):
        low = grad.astype(BF)
        return [plane(part(low, f ^ k, axis), k) for k in range(n)]

    down_parts = [reduce(p) for p in share(dot(act, cot, 0, 0), 1)]
    gate_parts = [reduce(p) for p in share(dot(xn_two, dgate, 0, 0), 0)]
    up_parts = [reduce(p) for p in share(dot(xn_two, dup, 0, 0), 0)]
    d_two = scatter(dot(dgate, wg, 1, 1) + dot(dup, wu, 1, 1))
    out_half = (hidden + scatter(dot(act, wd, 1, 0))).astype(BF)
    output = join(out_half, swap(out_half))
    gain_two_grad = jnp.sum(d_two * hat_two, 0)
    e_two = d_two * gain_two
    d_hidden = mine(cotangent[0], t).astype(F32) + scale_two * (e_two - hat_two * row_mean(e_two * hat_two))
    dhb = gather(d_hidden.astype(BF))
    out_parts = [reduce(p) for p in share(dot(attended_low, dhb, 0, 0), 1)]

    d_att = dot(dhb, wo, 1, 1).astype(BF).reshape(n, tokens, heads, HD)
    delta = jnp.einsum("nthd,nthd->nht", d_att.astype(F32), attended)
    d_weights = jnp.einsum("nthd,nsd->nhts", d_att, values, preferred_element_type=F32)
    d_scores = (weights * (d_weights - delta[..., None])).astype(BF)
    dv = jnp.einsum("nhts,nthd->nsd", weights_low, d_att, preferred_element_type=F32)
    dk = jnp.einsum("nhts,nthd->nsd", d_scores, query, preferred_element_type=F32) * factor
    dq = jnp.einsum("nhts,nsd->nthd", d_scores, keys, preferred_element_type=F32) * factor
    d_kv = jnp.concatenate([dk, dv], -1).reshape(n, m, tokens, 2 * HD)
    d_low = d_kv.astype(BF)
    d_kv_own = d_kv[:, 0]
    for k in range(1, m):
        d_kv_own = d_kv_own + column(d_low[:, k], k).astype(F32)
    d_kv_own = d_kv_own.reshape(n * tokens, 2 * HD)
    dq = rotate(dq.reshape(n * tokens, heads, HD), cosine, -sine).reshape(n * tokens, cols)
    dk = rotate(d_kv_own[:, None, :HD], cosine, -sine)[:, 0, :]
    d_qkv = jnp.concatenate([dq, dk, d_kv_own[:, HD:]], 1).astype(BF)
    w_here = jnp.concatenate([w_qkv[:, :cols], pick(w_qkv[:, cols : cols + kw]), pick(w_qkv[:, cols + kw :])], 1)
    d_one = scatter(dot(d_qkv, w_here, 1, 1))
    qkv_parts = share(dot(xn_one, d_qkv, 0, 0), 0)
    key_parts, value_parts = [0.0] * kv_heads, [0.0] * kv_heads
    for k in range(n):
        owner = (heads * (f ^ k)) // ((w_query.shape[1] // HD) // kv_heads)
        piece = qkv_parts[k].astype(F32)
        for g in range(kv_heads):
            key_parts[g] = key_parts[g] + jnp.where(owner == g, piece[:, cols : cols + HD], 0.0)
            value_parts[g] = value_parts[g] + jnp.where(owner == g, piece[:, cols + HD :], 0.0)
    small = reduce(jnp.concatenate(key_parts + value_parts, 1).astype(BF)).astype(F32)
    query_parts = [reduce(p[:, :cols]) for p in qkv_parts]
    gain_one_grad = jnp.sum(d_one * hat_one, 0)
    e_one = d_one * gain_one
    in_half = d_hidden + scale_one * (e_one - hat_one * row_mean(e_one * hat_one))
    input_grad = join(in_half, swap(in_half))
    gain_grads = jnp.stack([gain_one_grad, gain_two_grad])
    nothing = jnp.zeros_like(gain_grads)
    gain_grads = jnp.where(t == 0, jnp.concatenate([gain_grads, nothing], 1), jnp.concatenate([nothing, gain_grads], 1))
    gain_grads = part(lax.psum(gain_grads, ("fsdp", "ctx", "tp")), f, 1)

    def settle(pieces, axis):
        return place(pieces, axis).astype(F32)

    return (
        output[None],
        input_grad[None],
        gain_grads[0],
        settle(query_parts, 1),
        small[:, :kw],
        small[:, kw:],
        settle(out_parts, 0),
        gain_grads[1],
        settle(gate_parts, 1),
        settle(up_parts, 1),
        settle(down_parts, 0),
    )


T, W, H, TILE = 256, 2048, 1024, 128
MAIN, WIN = 640, 768
GRADS = (("d", 2816, 512), ("g", 512, 2816), ("u", 512, 2816), ("o", 1024, 512), ("q", 512, 1024), ("k", 512, 256))
PART = 384


def chunk_list():
    chunks = []
    for name in "dgu":
        if name == "u":
            chunks += [("o", "o", r, 0, 256, 512) for r in range(0, 1024, 256)]
        for which in "AB":
            for j in range(4):
                size = PART if which == "A" or j % 2 == 0 else MAIN - PART
                chunks.append((name + which, name, j, j) + ((size, 512) if name == "d" else (512, size)))
    chunks += [("q", "q", 0, c, 512, 256) for c in range(0, 1024, 256)]
    return chunks + [("k", "k", 0, 0, 512, 256)]


CHUNKS = chunk_list()
DEPTH = 4
ORDER = (
    "+", "relay", "down_B", "gate_A", 1, "norm_two_back", 1, "gate_B", 1, "dB", 1, "gA", 1, 1, 1, 1, "dh_take",
    "out_grads", 1, "attend0", "attend1", 1, "gB", "up_A", 1, "attend2", 1, "attend3", "pair_send", "up_B", 1, "o", 1, 1, 1,
    "pair_sum", "uA", 1, 1, 1, "+", "d_kv_take", "qkv_grads", 1, "d1_begin", "+", 1, "uB", "q", 1, "relay", 1, "kv_ready", 1, "norm_one_back",
    1, "out_begin", 1, "relay", 1, 1, "gains_column", 1, 1, "out_end", "-", "-", "gains_end",
)
MESH = pl.DeviceIdType.MESH


def nn(a, b):
    return lax.dot_general(a, b, (((1,), (0,)), ((), ())), preferred_element_type=F32)


def nt(a, b):
    return lax.dot_general(a, b, (((1,), (1,)), ((), ())), preferred_element_type=F32)


def tn(a, b):
    return lax.dot_general(a, b, (((0,), (0,)), ((), ())), preferred_element_type=F32)


def flip(a, k):
    return (a % 2 + k % 2) % 2 + 2 * ((a // 2 + k // 2) % 2)


def layer_kernel(*refs):
    names = iter(refs)

    def take(count):
        return [next(names) for _ in range(count)]

    x_in, table_in, gains_in, cot_in, wq, wk, wv, wo, wg, wu, wd = take(11)
    out_ref, in_grad_ref, gain_ref = take(3)
    first, left, cross, total = ({name: next(names) for name, _, _ in GRADS} for _ in range(4))
    (x1, x2, ct, dh, w_qkv, w_o, w_g, w_u, w_d, act, dg, du, q_buf, kv_all, ob) = take(15)
    (ps, pr, rr, rd, yo, hid, d_hid, xv, tb, ga, ids, r1s, r2s, ss_own, ss_other, lse, bias) = take(17)
    (gs_d, kv_g, d_kv, d_kv_pair, d_kv_recv, out_s, g_sum, g_plane, g_column, g_whole) = take(10)
    send_sem, recv_sem, local_sem, credit = take(4)
    f, z, t = lax.axis_index("fsdp"), lax.axis_index("ctx"), lax.axis_index("tp")
    sems = iter(range(10**6))
    drains = []

    def al(v, by):
        return pl.multiple_of(v, by)

    def plane(k):
        return (flip(f, k), z, t)

    def column(k):
        return (f, flip(z, k), t)

    core = (f, z, 1 - t)
    rows_f = pl.ds(al(f * T, T), T)
    half = pl.ds(al(t * H, H), H)
    rest = pl.ds(al((1 - t) * H, H), H)

    def rows_of(b):
        return pl.ds(al(b * T, T), T)

    def remote(src, dst, s, device):
        return pltpu.make_async_remote_copy(src_ref=src, dst_ref=dst, send_sem=send_sem.at[s], recv_sem=recv_sem.at[s], device_id=device, device_id_type=MESH)

    def here(src, dst, s):
        return pltpu.make_async_copy(src, dst, local_sem.at[s])

    local_count = iter(range(10**6))

    lx = here(x_in.at[0], xv, next(local_count))
    lx.start()
    lc = here(cot_in.at[0], ct.at[rows_f, :], next(local_count))
    lc.start()
    lh = here(cot_in.at[0, :, half], out_s, next(local_count))
    lh.start()
    lt = here(table_in, tb.at[f], next(local_count))
    lt.start()
    lg = here(gains_in, ga.at[:, pl.ds(al(f * 512, 512), 512)], next(local_count))
    lg.start()

    def starts(r):
        return (11 * r + 1 - t) // 2

    def full(r):
        return (r + t) % 2 == 0

    def weight_moves(k, taking):
        r = flip(f, k)
        sender, taker = (r, f) if taking else (f, r)
        rows = pl.ds(al(sender * 512, 512), 512)
        row_part = pl.ds(al(sender * 512 + z * TILE, TILE), TILE)
        own_part = pl.ds(al(z * TILE, TILE), TILE)
        begin = al(starts(taker) * TILE, TILE)
        tail = al(begin + MAIN, TILE)
        col = al(taker * T, T)
        moves = {
            "o": [(wo.at[pl.ds(col, T), :], w_o.at[:, rows])],
            "g": [(wg.at[:, pl.ds(begin, MAIN)], w_g.at[rows, pl.ds(0, MAIN)])],
            "g+": [(wg.at[:, pl.ds(tail, TILE)], w_g.at[rows, pl.ds(MAIN, TILE)])],
        }
        from_rows, to_rows = pl.ds(0, 512), rows
        if k:
            from_rows, to_rows = pl.ds(al(z % 2 * T, T), T), pl.ds(al(sender * 512 + z % 2 * T, T), T)
        moves["qkv"] = [
            (wq.at[from_rows, pl.ds(col, T)], w_qkv.at[to_rows, pl.ds(0, T)]),
            (wk.at[from_rows, :], w_qkv.at[to_rows, pl.ds(T, TILE)]),
            (wv.at[from_rows, :], w_qkv.at[to_rows, pl.ds(T + TILE, TILE)]),
        ]
        if k == 0:
            moves["u"] = [(wu.at[:, pl.ds(begin, MAIN)], w_u.at[rows, pl.ds(0, MAIN)])]
            moves["u+"] = [(wu.at[:, pl.ds(tail, TILE)], w_u.at[rows, pl.ds(MAIN, TILE)])]
            moves["d"] = [(wd.at[pl.ds(begin, MAIN), :], w_d.at[pl.ds(0, MAIN), rows])]
            moves["d+"] = [(wd.at[pl.ds(tail, TILE), :], w_d.at[pl.ds(MAIN, TILE), rows])]
        else:
            moves["u"] = [(wu.at[own_part, pl.ds(begin, MAIN)], w_u.at[row_part, pl.ds(0, MAIN)])]
            moves["u+"] = [(wu.at[own_part, pl.ds(tail, TILE)], w_u.at[row_part, pl.ds(MAIN, TILE)])]
            moves["d"] = [(wd.at[pl.ds(begin, MAIN), own_part], w_d.at[pl.ds(0, MAIN), row_part])]
            moves["d+"] = [(wd.at[pl.ds(tail, TILE), own_part], w_d.at[pl.ds(MAIN, TILE), row_part])]
        return moves

    w_counts = (("qkv", 3), ("o", 1), ("g", 1), ("g+", 1), ("u", 1), ("u+", 1), ("d", 1), ("d+", 1))
    w_sem = {(key, k, i): next(sems) for key, c in w_counts for k in (1, 2, 3) for i in range(c)}
    w_local = {(key, i): next(local_count) for key, c in w_counts for i in range(c)}

    def weights_each(key, taking, run):
        for k in (1, 2, 3):
            moves = weight_moves(k, taking)
            for i, (src, dst) in enumerate(moves[key]):
                run(remote(src, dst, w_sem[key, k, i], plane(k)))
            if key + "+" in moves:

                @pl.when(full(f if taking else flip(f, k)))
                def _():
                    (src, dst), = moves[key + "+"]
                    run(remote(src, dst, w_sem[key + "+", k, 0], plane(k)))

    def weights_start(key):
        weights_each(key, False, lambda cp: cp.start())

    def weights_wait(key):
        weights_each(key, True, lambda cp: cp.wait_recv())

    def weights_drain():
        for key in ("qkv", "o", "g", "u", "d"):
            weights_each(key, False, lambda cp: cp.wait_send())

    def weights_own(wait):
        moves = weight_moves(0, False)

        def run(key):
            for i, (src, dst) in enumerate(moves[key]):
                cp = here(src, dst, w_local[key, i])
                cp.wait() if wait else cp.start()

        for key in ("qkv", "o", "g", "u", "d"):
            run(key)

        @pl.when(full(f))
        def _():
            for key in ("g+", "u+", "d+"):
                run(key)

    y_sem = {(key, k, j): next(sems) for key in ("qkv", "u", "d") for k in (1, 2, 3) for j in (1, 2, 3) if key != "qkv" or j == 1}

    def column_each(key, taking, run):
        for k in (1, 2, 3):
            for j in (1, 2, 3):
                from_z = flip(z, j) if taking else z
                part = pl.ds(al(flip(f, k) * 512 + from_z * TILE, TILE), TILE)

                def move(size):
                    ref = w_u.at[part, pl.ds(0, size)] if key == "u" else w_d.at[pl.ds(0, size), part]
                    run(remote(ref, ref, y_sem[key, k, j], column(j)))

                if key == "qkv":
                    if j == 1:
                        ref = w_qkv.at[pl.ds(al(flip(f, k) * 512 + from_z % 2 * T, T), T), :]
                        run(remote(ref, ref, y_sem[key, k, j], column(j)))
                    continue
                pl.when(full(f))(functools.partial(move, WIN))
                pl.when(full(f + 1))(functools.partial(move, MAIN))

    g_sem = [[next(sems) for _ in range(4)] for _ in range(4)]
    f_sem = [[next(sems) for _ in range(4)] for _ in range(4)]
    quarters = (pl.ds(al(t * H, 512), 512), pl.ds(al(t * H + 512, 512), 512))

    def gather_direct(g):
        return (1, 2, 3) if g == 3 else (1, 2)

    def gather_start(g, buf, with_own, src=None):
        block = buf.at[rows_f, half]
        for k in gather_direct(g):
            remote(block if src is None else src, block, g_sem[g][k - 1], plane(k)).start()
        if with_own:
            remote(block, block, f_sem[g][3], core).start()

    def gather_hand(g, buf, k):
        block = buf.at[rows_of(flip(f, k)), half]
        return remote(block, block, f_sem[g][k - 1], core)

    def gather_relay(g, buf, k):
        part = buf.at[rows_of(flip(f, k)), quarters[k - 1]]
        return remote(part, part, g_sem[g][4 - k], plane(3 - k))

    def gather_forward(g, buf):
        for k in gather_direct(g):
            block = buf.at[rows_of(flip(f, k)), half]
            remote(block, block, g_sem[g][k - 1], plane(k)).wait_recv()
            if g != 3:
                gather_relay(g, buf, k).start()
            gather_hand(g, buf, k).start()

    def gather_diagonal(g, buf):
        for k in (1, 2):
            part = buf.at[rows_of(flip(f, 3)), quarters[k - 1]]
            remote(part, part, g_sem[g][4 - k], plane(3 - k)).wait_recv()
        gather_hand(g, buf, 3).start()

    def gather_take(g, buf, k):
        if k == 0:
            block = buf.at[rows_f, rest]
            remote(block, block, f_sem[g][3], core).wait_recv()
        else:
            block = buf.at[rows_of(flip(f, k)), rest]
            remote(block, block, f_sem[g][k - 1], core).wait_recv()

    def gather_drain(g, buf, with_own, src=None):
        block = buf.at[rows_f, half]
        for k in gather_direct(g):
            remote(block if src is None else src, block, g_sem[g][k - 1], plane(k)).wait_send()
        for k in (1, 2, 3):
            gather_hand(g, buf, k).wait_send()
            if g != 3 and k != 3:
                gather_relay(g, buf, k).wait_send()
        if with_own:
            remote(block, block, f_sem[g][3], core).wait_send()

    t_sem = [next(sems) for _ in range(3)]
    a_sem = [next(sems) for _ in range(3)]
    own_gain = ga.at[:, pl.ds(al(f * 512, 512), 512)]

    barrier = pltpu.get_barrier_semaphore()
    for k in (1, 2, 3):
        pl.semaphore_signal(barrier, inc=1, device_id=plane(k), device_id_type=MESH)
        pl.semaphore_signal(barrier, inc=1, device_id=column(k), device_id_type=MESH)
    pl.semaphore_signal(barrier, inc=1, device_id=core, device_id_type=MESH)
    pl.semaphore_wait(barrier, 7)

    lt.wait()
    lg.wait()
    for k in (1, 2, 3):
        remote(own_gain, own_gain, a_sem[k - 1], plane(k)).start()
        remote(tb.at[f], tb.at[f], t_sem[k - 1], plane(k)).start()
    weights_start("qkv")
    weights_own(False)

    @pl.when(full(f + 1))
    def _():
        w_g[:, MAIN:WIN] = jnp.zeros((W, TILE), BF)
        w_u[:, MAIN:WIN] = jnp.zeros((W, TILE), BF)
        w_d[MAIN:WIN, :] = jnp.zeros((TILE, W), BF)

    lx.wait()
    for k in (1, 2, 3):
        dst = ga.at[:, pl.ds(al(flip(f, k) * 512, 512), 512)]
        remote(dst, dst, a_sem[k - 1], plane(k)).wait_recv()

    STEP = 32

    def sub(i):
        return pl.ds(al(i * STEP, STEP), STEP)

    @pl.loop(0, T // STEP)
    def _(i):
        xs = xv[sub(i), :].astype(F32)
        scale = lax.rsqrt(jnp.mean(xs * xs, axis=-1, keepdims=True) + EPSILON)
        r1s[sub(i), :] = jnp.broadcast_to(scale, (STEP, TILE))
        x1[pl.ds(al(f * T + i * STEP, STEP), STEP), :] = (xs * scale * ga[0:1, :]).astype(BF)

    gather_start(0, x1, False)
    weights_wait("qkv")
    column_each("qkv", False, lambda cp: cp.start())
    gather_forward(0, x1)
    for key in "oudg":
        weights_start(key)
    gather_diagonal(0, x1)
    for k in (1, 2, 3):
        dst = tb.at[flip(f, k)]
        remote(dst, dst, t_sem[k - 1], plane(k)).wait_recv()
    weights_own(True)
    column_each("qkv", True, lambda cp: cp.wait_recv())

    lane = lax.broadcasted_iota(jnp.int32, (T, TILE), 1)
    low_lane = lane < HD
    first_half = lane % HD < HD // 2
    kv_head = f // 2

    def turns(b):
        cosine, sine = tb[b, 0:32, :], tb[b, 32:64, :]
        return (
            jnp.transpose(jnp.concatenate([cosine] * 4, 0)),
            jnp.transpose(jnp.concatenate([-sine, sine, -sine, sine], 0)),
        )

    def turn(v, c, s):
        swapped = jnp.where(first_half, pltpu.roll(v, TILE - 32, 1), pltpu.roll(v, 32, 1))
        return v * c + swapped * s

    def qkv_block(k):
        b = flip(f, k)
        qkv = nn(x1[rows_of(b), :], w_qkv[...])
        c, s = turns(b)
        for i in range(2):
            q = turn(qkv[:, i * TILE : (i + 1) * TILE], c, s) * 0.125
            q_buf[rows_of(b), i * TILE : (i + 1) * TILE] = q.astype(BF)
        key = turn(qkv[:, 2 * TILE : 3 * TILE], c, s)
        value = qkv[:, 3 * TILE :]
        key = jnp.where(kv_head == 0, key, pltpu.roll(key, HD, 1))
        value = jnp.where(kv_head == 1, value, pltpu.roll(value, HD, 1))
        kv_all[z, b, :, :] = jnp.where(low_lane, key, value).astype(BF)
        ids[z, pl.ds(b, 1), :] = tb[b, 64:65, :]

    qkv_block(0)
    for k in (1, 2, 3):
        gather_take(0, x1, k)

    @pl.loop(1, 4)
    def _(k):
        qkv_block(k)

    z_sem = [[next(sems) for _ in range(2)] for _ in range(3)]
    for k in (1, 2, 3):
        remote(kv_all.at[z], kv_all.at[z], z_sem[k - 1][0], column(k)).start()
        remote(ids.at[z], ids.at[z], z_sem[k - 1][1], column(k)).start()
    for k in (1, 2, 3):
        zz = flip(z, k)
        remote(kv_all.at[zz], kv_all.at[zz], z_sem[k - 1][0], column(k)).wait_recv()
        remote(ids.at[zz], ids.at[zz], z_sem[k - 1][1], column(k)).wait_recv()
    lc.wait()
    weights_wait("u")
    column_each("u", False, lambda cp: cp.start())

    low_keys = lax.broadcasted_iota(jnp.int32, (4 * T, TILE), 1) < HD

    def bias_of(s):
        query_id = ids[z, pl.ds(s, 1), :]
        for j in range(4):
            key_id = jnp.transpose(jnp.broadcast_to(ids[j, pl.ds(s, 1), :], (8, T)))[:, 0:1]
            bias[j * T : (j + 1) * T, :] = jnp.where(key_id <= query_id, 0.0, NEGATIVE).astype(BF)

    def kv_of(s):
        kv = jnp.concatenate([kv_all[j, s, :, :] for j in range(4)], 0).astype(F32)
        turned = pltpu.roll(kv, HD, 1)
        keys = jnp.where(low_keys, kv, turned).astype(BF)
        values = jnp.where(low_keys, turned, kv).astype(BF)
        return kv, keys, values

    def only(v, parity):
        return jnp.where(low_lane if parity == 0 else ~low_lane, v.astype(F32), 0.0).astype(BF)

    @pl.loop(0, 4)
    def _(s):
        bias_of(s)
        kv, keys, _ = kv_of(s)
        values_t = jnp.transpose(kv)[HD:, :].astype(BF)

        for i in range(2):
            mixed = []
            for parity in range(2):
                q = only(q_buf[rows_of(s), i * TILE : (i + 1) * TILE], parity)
                scores = nt(keys, q) + bias[...].astype(F32)
                top = jnp.max(scores, axis=0, keepdims=True)
                raw = jnp.exp(scores - top)
                norm = jnp.sum(raw, axis=0, keepdims=True)
                lse[s, 2 * i + parity : 2 * i + parity + 1, :] = top + jnp.log(norm)
                weights = (raw * (1.0 / norm)).astype(BF)
                mixed.append(nn(values_t, weights))
            ob[rows_of(s), i * TILE : (i + 1) * TILE] = jnp.transpose(jnp.concatenate(mixed, 0)).astype(BF)

    p_sem = [[next(sems) for _ in range(4)]] * 4
    s_sem = [next(sems) for _ in range(6)]
    COLS = 256
    lows, highs = pl.ds(0, 512), pl.ds(512, 512)

    def pass_first(k):
        return remote(ps.at[3, :, (lows, highs)[k - 1]], rd.at[k - 1], s_sem[k - 1], plane(k))

    def pass_second(k, added):
        cols = (lows, highs)[k - 1 if not added else 2 - k]
        return remote(ps.at[k, :, cols], rr.at[k - 1, :, cols], s_sem[2 * k + added], plane(k))

    def scatter_start(u, product):
        p0 = p_sem[u][0]

        def tiles(run):
            @pl.loop(0, H // COLS)
            def _(j):
                run(pl.ds(al(j * COLS, COLS), COLS), j * COLS)

        @pl.loop(0, 4)
        def _(i):
            k = (7 - i) % 4

            def run(cols, c):
                ps[k, :, cols] = product(flip(f, k), (1 - t) * H + c).astype(BF)

            tiles(run)
            remote(ps.at[k], pr.at[k], p0 + k, core).start()

        def own(k):
            remote(ps.at[k], pr.at[k], p0 + k, core).wait()

            def run(cols, c):
                ps[k, :, cols] = (product(flip(f, k), t * H + c) + pr[k, :, cols].astype(F32)).astype(BF)

            tiles(run)

        own(3)
        pass_first(1).start()
        pass_first(2).start()

        @pl.loop(1, 3)
        def _(k):
            own(k)

        pass_second(1, 0).start()
        pass_second(2, 0).start()
        remote(ps.at[0], pr.at[0], p0, core).wait()

        def run(cols, c):
            yo[:, cols] = product(f, t * H + c) + pr[0, :, cols].astype(F32)

        tiles(run)

    def scatter_relay():
        for k in (1, 2):
            pass_first(3 - k).wait()
            c = (512, 0)[k - 1]

            @pl.loop(0, T // STEP)
            def _(i):
                ps[k, sub(i), c : c + 512] = (ps[k, sub(i), c : c + 512].astype(F32) + rd[2 - k, sub(i), :].astype(F32)).astype(BF)

            pass_second(k, 1).start()

    def scatter_wait(u):
        for k in (1, 2):
            for added in (0, 1):
                pass_second(k, added).wait()

    def scattered(i):
        return yo[sub(i), :] + rr[0, sub(i), :].astype(F32) + rr[1, sub(i), :].astype(F32)

    n_sem = [next(sems) for _ in range(3)]

    def core_sums(u):
        remote(ss_own.at[u], ss_other.at[u], n_sem[u], core).start()
        remote(ss_own.at[u], ss_other.at[u], n_sem[u], core).wait()

    weights_wait("o")
    scatter_start(0, lambda b, c: nn(ob[rows_of(b), :], w_o[:, pl.ds(al(c, COLS), COLS)]))
    scatter_relay()
    weights_wait("d")
    column_each("d", False, lambda cp: cp.start())
    scatter_wait(0)

    @pl.loop(0, T // STEP)
    def _(i):
        rows = xv[sub(i), half].astype(F32) + scattered(i)
        hid[sub(i), :] = rows
        ss_own[0, sub(i), :] = jnp.broadcast_to(jnp.sum(rows * rows, axis=-1, keepdims=True), (STEP, TILE))

    core_sums(0)
    gain_one, gain_two = ga[0:1, half], ga[1:2, half]

    @pl.loop(0, T // STEP)
    def _(i):
        scale = lax.rsqrt((ss_own[0, sub(i), 0:1] + ss_other[0, sub(i), 0:1]) * (1.0 / W) + EPSILON)
        r2s[sub(i), :] = jnp.broadcast_to(scale, (STEP, TILE))
        x2[pl.ds(al(f * T + i * STEP, STEP), STEP), half] = (hid[sub(i), :] * scale * gain_two).astype(BF)

    gather_start(2, x2, True)
    gather_forward(2, x2)
    gather_start(1, ct, False, cot_in.at[0, :, half])
    weights_wait("g")
    column_each("u", True, lambda cp: cp.wait_recv())

    UNITS = 256

    def feed_block(k):
        b = flip(f, k)

        @pl.loop(0, WIN // UNITS)
        def _(j):
            cols = pl.ds(al(j * UNITS, UNITS), UNITS)
            gate = nn(x2[rows_of(b), :], w_g[:, cols])
            up = nn(x2[rows_of(b), :], w_u[:, cols])
            sigma = jax.nn.sigmoid(gate)
            silu = gate * sigma
            act[rows_of(b), cols] = (silu * up).astype(BF)
            dg[rows_of(b), cols] = (up * sigma * (1.0 + gate * (1.0 - sigma))).astype(BF)
            du[rows_of(b), cols] = silu.astype(BF)

    for k in (0, 1, 2):
        gather_take(2, x2, k)

    @pl.loop(0, 3)
    def _(k):
        feed_block(k)

    gather_diagonal(2, x2)
    gather_take(2, x2, 3)
    feed_block(3)
    gather_forward(1, ct)
    gather_diagonal(1, ct)
    for k in (1, 2, 3):
        gather_take(1, ct, k)

    GROUPS = ("dA", "dB", "gA", "gB", "uA", "uB", "o", "q", "k")
    e_sem = {(name, i): [next(sems) for _ in range(3)][0] for name in GROUPS for i in range(2 if name[-1] == "B" else 1)}
    e_local = {(name, i): next(local_count) for name in GROUPS for i in range(2 if name[-1] == "B" else 1)}

    def stage(name, k):
        if name == "d":
            return gs_d.at[pl.ds(al(k * WIN, WIN), WIN), :]
        if name in "gu":
            return ct.at[pl.ds(al((k // 2) * 512, 512), 512), pl.ds(al((k % 2) * H, H), WIN)]
        if name == "o":
            return gs_d.at[pl.ds(al(k * WIN, WIN), T), :]
        return x2.at[pl.ds(al((k // 2) * 512, 512), 512), pl.ds(al((k % 2) * 512 + (0 if name == "q" else T), T), T)]

    def grad_moves(group, k, sender):
        name = group[0]
        buf, begin = stage(name, k), al(starts(sender) * TILE, TILE)
        if name in "dgu":
            parts = [(0, PART)] if group[1] == "A" else [(PART, MAIN - PART), (MAIN, TILE)]
            if name == "d":
                return [(buf.at[pl.ds(c, size), :], first["d"].at[pl.ds(al(begin + c, TILE), size), :]) for c, size in parts]
            return [(buf.at[:, pl.ds(c, size)], first[name].at[:, pl.ds(al(begin + c, TILE), size)]) for c, size in parts]
        if name == "o":
            return [(buf, first["o"].at[rows_of(sender), :])]
        if name == "q":
            return [(buf, first["q"].at[:, rows_of(sender)])]
        return [(buf, kv_g.at[k - 1])]

    def grad_send(group, k, act_on):
        for i, (src, dst) in enumerate(grad_moves(group, k, f)):

            def run(i=i, src=src, dst=dst):
                if isinstance(k, int) and k == 0:
                    cp = here(src, dst, e_local[group, i])
                    cp.wait() if act_on == "wait" else cp.start()
                else:
                    cp = remote(src, dst, e_sem[group, i] + k - 1, plane(k))
                    cp.wait_send() if act_on == "wait" else cp.start()

            if i == 0:
                run()
            else:
                pl.when(full(f))(run)

    def grad_take(group):
        for k in (1, 2, 3):
            sender = flip(f, k)
            for i, (src, dst) in enumerate(grad_moves(group, k, sender)):

                def run(i=i, src=src, dst=dst):
                    remote(src, dst, e_sem[group, i] + k - 1, plane(k)).wait_recv()

                if i == 0:
                    run()
                else:
                    pl.when(full(sender))(run)

    def sent(*groups):
        for group in groups:
            for k in (1, 2, 3):
                grad_send(group, k, "wait")

    def block_cols(k):
        return pl.ds(al(flip(f, k) * 512, 512), 512)

    def each_owner(run):
        @pl.loop(1, 4)
        def _(k):
            run(k)

        run(0)

    def down_grads(which):
        c = 0 if which == "A" else PART

        def run(k):
            stage("d", k)[c : c + PART, :] = tn(act[:, c : c + PART], ct[:, block_cols(k)]).astype(BF)
            grad_send("d" + which, k, "start")

        each_owner(run)

    def feed_grads(name, which, right):
        c = 0 if which == "A" else PART

        def run(k):
            @pl.loop(0, 2)
            def _(i):
                xs = x2[:, pl.ds(al(flip(f, k) * 512 + i * T, T), T)]
                stage(name, k)[pl.ds(al(i * T, T), T), c : c + PART] = tn(xs, right[:, c : c + PART]).astype(BF)

            grad_send(name + which, k, "start")

        each_owner(run)

    down_grads("A")

    column_each("d", True, lambda cp: cp.wait_recv())

    @pl.loop(0, 4)
    def _(b):
        @pl.loop(0, WIN // UNITS)
        def _(j):
            cols = pl.ds(al(j * UNITS, UNITS), UNITS)
            back = nt(ct[rows_of(b), :], w_d[cols, :])
            dg[rows_of(b), cols] = (back * dg[rows_of(b), cols].astype(F32)).astype(BF)
            du[rows_of(b), cols] = (back * du[rows_of(b), cols].astype(F32)).astype(BF)

    end = (z == 0) | (z == 3)
    middle = (z == 1) | (z == 2)
    next_in = (f, jnp.where(z < 2, 1, 2), t)
    next_out = (f, jnp.where(z < 2, 0, 3), t)
    facing = (f, 3 - z, t)
    across = [next(sems) for _ in range(2 * DEPTH)]
    l_sem = [[next(sems), across[i % (2 * DEPTH)], next(sems)] for i in range(len(CHUNKS))]
    v_sem = [next(local_count) for _ in range(2)]
    o_sem = [next(local_count) for _ in range(4)]

    def square(buf, i):
        return buf.at[pl.ds(i * 512, 512), pl.ds(0, 512)]

    ring, la = [square(w_u, i) for i in range(DEPTH)], square(w_g, 3)
    tt, lb = [square(w_g, i) for i in range(2)], square(w_g, 2)

    kept, given = (w_g.at[:, pl.ds(512 + j * TILE, TILE)] for j in range(2))
    even = f % 2 == 0

    def pair_rows(pair, j):
        return pl.ds(j * 512 + pair * T, T)


    def window(arrays, i):
        group, name, r, c, rows, cols = CHUNKS[i]
        if name in "dgu":
            j = r if group[1] == "A" else flip(r, t)
            at = al(starts(j) * TILE + (0 if group[1] == "A" else PART), TILE)
            r, c = (at, 0) if name == "d" else (0, at)
        return arrays[name].at[pl.ds(r, rows), pl.ds(c, cols)]

    def line_send(group):
        @pl.when(end)
        def _():
            for i, chunk in enumerate(CHUNKS):
                if chunk[0] == group:
                    remote(window(first, i), window(left, i), l_sem[i][0], next_in).start()

    def add_into(dst, a, b, rows, cols):
        @pl.loop(0, rows // STEP)
        def _(i):
            at = sub(i)
            dst[at, pl.ds(0, cols)] = (a[at, pl.ds(0, cols)].astype(F32) + b[at, pl.ds(0, cols)].astype(F32)).astype(BF)

    def line_one(i):
        _, name, r, c, rows, cols = CHUNKS[i]
        part = (pl.ds(0, rows), pl.ds(0, cols))
        a, b, keep = la.at[part], lb.at[part], ring[i % DEPTH]

        @pl.when(middle)
        def _():
            get_a = here(window(first, i), a, v_sem[0])
            get_a.start()
            remote(window(first, i), window(left, i), l_sem[i][0], next_in).wait_recv()
            get_b = here(window(left, i), b, v_sem[1])
            get_b.start()
            get_a.wait()
            get_b.wait()
            add_into(keep, la, lb, rows, cols)
            remote(keep.at[part], window(cross, i), l_sem[i][1], facing).start()

    def line_two(i):
        _, name, r, c, rows, cols = CHUNKS[i]
        part = (pl.ds(0, rows), pl.ds(0, cols))
        keep, done = ring[i % DEPTH], tt[i % 2]

        @pl.when(middle)
        def _():
            remote(keep.at[part], window(cross, i), l_sem[i][1], facing).wait()
            get = here(window(cross, i), lb.at[part], v_sem[1])
            get.start()
            if i >= 2:
                line_out(i - 2)
            get.wait()
            add_into(done, keep, lb, rows, cols)
            remote(done.at[part], window(total, i), l_sem[i][2], next_out).start()
            here(done.at[part], window(total, i), o_sem[i % 4]).start()

    def line_out(i):
        _, name, r, c, rows, cols = CHUNKS[i]
        done = tt[i % 2].at[pl.ds(0, rows), pl.ds(0, cols)]
        remote(done, window(total, i), l_sem[i][2], next_out).wait_send()
        here(done, window(total, i), o_sem[i % 4]).wait()

    pumped, ready = [0, 0], set()

    def ahead():
        i = pumped[0]
        assert CHUNKS[i][0] in ready and i < pumped[1] + DEPTH
        line_one(i)
        pumped[0] += 1

    def behind():
        i = pumped[1]
        assert i < pumped[0]
        line_two(i)
        pumped[1] += 1

    def grad_ready(group):
        grad_take(group)
        grad_send(group, 0, "wait")
        line_send(group)
        ready.add(group)

    lh.wait()
    @pl.when(end)
    def _():
        grad_take("dA")
        grad_send("dA", 0, "wait")

    line_send("dA")
    scatter_start(1, lambda b, c: nt(dg[rows_of(b), :], w_g[pl.ds(al(c, COLS), COLS), :]) + nt(du[rows_of(b), :], w_u[pl.ds(al(c, COLS), COLS), :]))
    @pl.when(middle)
    def _():
        grad_take("dA")
        grad_send("dA", 0, "wait")

    ready.add("dA")
    column_each("u", False, lambda cp: cp.wait_send())
    gather_drain(1, ct, False, cot_in.at[0, :, half])
    gather_drain(2, x2, True)
    g_sum[...] = jnp.zeros((8, H), F32)
    k_sem = [next(sems) for _ in range(3)]
    q_sem = [[next(sems) for _ in range(3)] for _ in range(2)]
    d_ob, d_qkv = ob, dg
    here_half = (lane // HD) == kv_head
    out_local = here(out_s, out_ref.at[:, half], next(local_count))
    out_remote = remote(out_s, out_ref.at[:, half], next(sems), core)
    in_local = here(d_hid, in_grad_ref.at[:, half], next(local_count))
    in_remote = remote(d_hid, in_grad_ref.at[:, half], next(sems), core)
    kv_copy = here(x2.at[pl.ds(0, 512), pl.ds(T, T)], first["k"], next(local_count))
    whole_move = remote(g_whole.at[:, half], g_whole.at[:, half], next(sems), core)
    gain_move = here(g_whole.at[:, pl.ds(al(f * 512, 512), 512)], gain_ref, next(local_count))

    def norm_two_back():
        scatter_wait(1)

        def rows_back(i, carry):
            rows = scattered(i)
            yo[sub(i), :] = rows
            hat = hid[sub(i), :] * r2s[sub(i), 0:1]
            ss_own[1, sub(i), :] = jnp.broadcast_to(jnp.sum(rows * gain_two * hat, axis=-1, keepdims=True), (STEP, TILE))
            return carry + jnp.sum(rows * hat, axis=0, keepdims=True)

        g_sum[1:2, :] = lax.fori_loop(0, T // STEP, rows_back, jnp.zeros((1, H), F32))
        core_sums(1)

        @pl.loop(0, T // STEP)
        def _(i):
            scale = r2s[sub(i), 0:1]
            hat = hid[sub(i), :] * scale
            mean = (ss_own[1, sub(i), 0:1] + ss_other[1, sub(i), 0:1]) * (1.0 / W)
            rows = out_s[sub(i), :].astype(F32) + scale * (yo[sub(i), :] * gain_two - hat * mean)
            d_hid[sub(i), :] = rows
            dh[pl.ds(al(f * T + i * STEP, STEP), STEP), half] = rows.astype(BF)

        gather_start(3, dh, True)

    def dh_take():
        gather_forward(3, dh)
        for k in range(4):
            gather_take(3, dh, k)

    def out_grads():
        sent("dA", "dB")

        def run(k):
            stage("o", k)[...] = tn(ob[...], dh[:, block_cols(k)]).astype(BF)
            grad_send("o", k, "start")

        each_owner(run)

        @pl.loop(0, 4)
        def _(b):
            ob[rows_of(b), :] = nt(dh[rows_of(b), :], w_o[...]).astype(BF)

    def attend_back(s):
        bias_of(s)
        kv, keys, values = kv_of(s)
        keys_t = jnp.transpose(kv)[:HD, :].astype(BF)
        c, sn = turns(s)
        d_key = jnp.zeros((4 * T, TILE), F32)
        d_value = jnp.zeros((4 * T, TILE), F32)
        for i in range(2):
            d_query = []
            for parity in range(2):
                q = only(q_buf[rows_of(s), i * TILE : (i + 1) * TILE], parity)
                do = only(d_ob[rows_of(s), i * TILE : (i + 1) * TILE], parity)
                weights = jnp.exp(nt(keys, q) + bias[...].astype(F32) - lse[s, 2 * i + parity : 2 * i + parity + 1, :])
                d_weights = nt(values, do)
                delta = jnp.sum(weights * d_weights, axis=0, keepdims=True)
                d_scores = (weights * (d_weights - delta)).astype(BF)
                d_value = d_value + nn(weights.astype(BF), do)
                d_key = d_key + nn(d_scores, q)
                d_query.append(nn(keys_t, d_scores))
            d_query = jnp.transpose(jnp.concatenate(d_query, 0)) * 0.125
            d_qkv[rows_of(s), i * TILE : (i + 1) * TILE] = turn(d_query, c, -sn).astype(BF)
        d_key = d_key + pltpu.roll(d_key, HD, 1)
        d_value = d_value + pltpu.roll(d_value, HD, 1)
        lanes = slice(s % 2 * HD, s % 2 * HD + HD)
        keep, give = jnp.where(even, d_key, d_value).astype(BF), jnp.where(even, d_value, d_key).astype(BF)
        for j in range(4):
            kept[pair_rows(s // 2, j), lanes] = keep[j * T : (j + 1) * T, lanes]
            given[pair_rows(s // 2, j), lanes] = give[j * T : (j + 1) * T, lanes]

    pair_move = remote(given, d_kv_pair, next(sems), plane(1))

    def pair_sum():
        pair_move.wait()

        @pl.loop(0, W // STEP)
        def _(i):
            rows = kept[sub(i), :].astype(F32) + d_kv_pair[sub(i), :].astype(F32)
            kept[sub(i), :] = rows.astype(BF)

            @pl.when(i // (512 // STEP) == z)
            def _():
                d_kv[pl.ds(al(i % (512 // STEP) * STEP, STEP), STEP), :] = rows

        for move in d_kv_moves():
            move.start()

    def d_kv_moves():
        return [remote(kept.at[pl.ds(al(flip(z, k) * 512, 512), 512), :], d_kv_recv.at[k - 1], k_sem[k - 1], column(k)) for k in (1, 2, 3)]

    def up_A():
        sent("gA", "gB")
        feed_grads("u", "A", du)

    def d_kv_take():
        for move in d_kv_moves():
            move.wait()

        for s in range(4):
            c, sn = turns(s)
            rows = pl.ds(s // 2 * T, T)
            whole = d_kv[rows, :]
            for k in range(3):
                whole = whole + d_kv_recv[k, rows, :].astype(F32)
            turned = pltpu.roll(whole, HD, 1)
            whole = jnp.where(low_lane, whole, turned) if s % 2 == 0 else jnp.where(low_lane, turned, whole)
            d_qkv[rows_of(s), 2 * TILE : 3 * TILE] = jnp.where(here_half & even, turn(whole, c, -sn), 0.0).astype(BF)
            d_qkv[rows_of(s), 3 * TILE : 4 * TILE] = jnp.where(here_half & ~even, whole, 0.0).astype(BF)

    def qkv_grads():
        def run(k):
            @pl.loop(0, 2)
            def _(i):
                xs = x1[:, pl.ds(al(flip(f, k) * 512 + i * T, T), T)]
                grads = tn(xs, d_qkv[:, 0:512]).astype(BF)
                stage("q", k)[pl.ds(al(i * T, T), T), :] = grads[:, 0:T]
                stage("k", k)[pl.ds(al(i * T, T), T), :] = grads[:, T:]

            grad_send("q", k, "start")
            if not (isinstance(k, int) and k == 0):
                grad_send("k", k, "start")

        each_owner(run)

    def d1_begin():
        scatter_start(2, lambda b, c: nt(d_qkv[rows_of(b), 0:512], w_qkv[pl.ds(al(c, COLS), COLS), :]))

    def kv_ready():
        grad_take("k")

        @pl.loop(0, 512 // STEP)
        def _(i):
            rows = x2[sub(i), T : 2 * T].astype(F32)
            for k in (1, 2, 3):
                rows = rows + kv_g[k - 1, sub(i), :].astype(F32)
            x2[sub(i), T : 2 * T] = rows.astype(BF)

        kv_copy.start()
        kv_copy.wait()
        line_send("k")
        ready.add("k")

    def norm_one_back():
        scatter_wait(2)

        def rows_back(i, carry):
            rows = scattered(i)
            yo[sub(i), :] = rows
            hat = xv[sub(i), half].astype(F32) * r1s[sub(i), 0:1]
            ss_own[2, sub(i), :] = jnp.broadcast_to(jnp.sum(rows * gain_one * hat, axis=-1, keepdims=True), (STEP, TILE))
            return carry + jnp.sum(rows * hat, axis=0, keepdims=True)

        g_sum[0:1, :] = lax.fori_loop(0, T // STEP, rows_back, jnp.zeros((1, H), F32))
        for k in (1, 2, 3):
            pl.semaphore_signal(credit, inc=1, device_id=plane(k), device_id_type=MESH)
        pl.semaphore_signal(credit, inc=1, device_id=core, device_id_type=MESH)
        core_sums(2)
        g_plane[f, :, :] = g_sum[...]
        for k in (1, 2, 3):
            remote(g_sum, g_plane.at[f], q_sem[0][k - 1], plane(k)).start()

        @pl.loop(0, T // STEP)
        def _(i):
            scale = r1s[sub(i), 0:1]
            hat = xv[sub(i), half].astype(F32) * scale
            mean = (ss_own[2, sub(i), 0:1] + ss_other[2, sub(i), 0:1]) * (1.0 / W)
            d_hid[sub(i), :] = d_hid[sub(i), :] + scale * (yo[sub(i), :] * gain_one - hat * mean)

        in_local.start()
        in_remote.start()

    def out_begin():
        pl.semaphore_wait(credit, 4)
        scatter_start(3, lambda b, c: nn(act[rows_of(b), :], w_d[:, pl.ds(al(c, COLS), COLS)]))

    def out_end():
        scatter_wait(3)

        @pl.loop(0, T // STEP)
        def _(i):
            out_s[sub(i), :] = (hid[sub(i), :] + scattered(i)).astype(BF)

        out_local.start()
        out_remote.start()

    def gains_column():
        for k in (1, 2, 3):
            remote(g_sum, g_plane.at[flip(f, k)], q_sem[0][k - 1], plane(k)).wait_recv()
        g_column[z, :, :] = ((g_plane[0, :, :] + g_plane[1, :, :]) + g_plane[2, :, :]) + g_plane[3, :, :]
        for k in (1, 2, 3):
            remote(g_column.at[z], g_column.at[z], q_sem[1][k - 1], column(k)).start()

    def gains_end():
        for k in (1, 2, 3):
            remote(g_column.at[z], g_column.at[flip(z, k)], q_sem[1][k - 1], column(k)).wait_recv()
        g_whole[:, half] = ((g_column[0, :, :] + g_column[1, :, :]) + g_column[2, :, :]) + g_column[3, :, :]
        whole_move.start()
        whole_move.wait()
        gain_move.start()

    steps = {
        "down_B": lambda: down_grads("B"),
        "gate_A": lambda: feed_grads("g", "A", dg),
        "gate_B": lambda: feed_grads("g", "B", dg),
        "up_A": up_A,
        "up_B": lambda: feed_grads("u", "B", du),
        "relay": scatter_relay,
        "norm_two_back": norm_two_back,
        "dh_take": dh_take,
        "out_grads": out_grads,
        "pair_send": lambda: pair_move.start(),
        "pair_sum": pair_sum,
        "d_kv_take": d_kv_take,
        "qkv_grads": qkv_grads,
        "d1_begin": d1_begin,
        "kv_ready": kv_ready,
        "norm_one_back": norm_one_back,
        "out_begin": out_begin,
        "out_end": out_end,
        "gains_column": gains_column,
        "gains_end": gains_end,
    }
    for step in ORDER:
        if step == "+":
            ahead()
        elif step == "-":
            behind()
        elif step == 1:
            ahead()
            behind()
        elif step in GROUPS:
            grad_ready(step)
        elif step[:6] == "attend":
            attend_back(int(step[6]))
        else:
            steps[step]()
    while pumped[0] < len(CHUNKS):
        ahead()
        behind()
    while pumped[1] < len(CHUNKS):
        behind()

    @pl.when(middle)
    def _():
        line_out(len(CHUNKS) - 2)
        line_out(len(CHUNKS) - 1)

    @pl.when(end)
    def _():
        for i in range(len(CHUNKS)):
            remote(window(first, i), window(left, i), l_sem[i][0], next_in).wait_send()
            remote(window(total, i), window(total, i), l_sem[i][2], next_in).wait_recv()

    gain_move.wait()
    out_local.wait()
    out_remote.wait()
    in_local.wait()
    in_remote.wait()
    weights_drain()
    column_each("d", False, lambda cp: cp.wait_send())
    column_each("qkv", False, lambda cp: cp.wait_send())
    gather_drain(0, x1, False)
    gather_drain(3, dh, True)
    for k in (1, 2, 3):
        remote(own_gain, own_gain, a_sem[k - 1], plane(k)).wait_send()
        remote(tb.at[f], tb.at[f], t_sem[k - 1], plane(k)).wait_send()
        remote(kv_all.at[z], kv_all.at[z], z_sem[k - 1][0], column(k)).wait_send()
        remote(ids.at[z], ids.at[z], z_sem[k - 1][1], column(k)).wait_send()
        remote(g_sum, g_plane.at[f], q_sem[0][k - 1], plane(k)).wait_send()
        remote(g_column.at[z], g_column.at[z], q_sem[1][k - 1], column(k)).wait_send()
        for name in ("uA", "uB", "o", "q", "k"):
            grad_send(name, k, "wait")
    assert (next(sems), next(local_count)) == (REMOTE_SEMS, LOCAL_SEMS)


REMOTE_SEMS, LOCAL_SEMS = 231, 37


def layer_call(inputs, positions, blocks, cotangent, attn_gain, w_query, w_key, w_value, w_out, mlp_gain, w_gate, w_up, w_down):
    frequency = jnp.exp(jnp.arange(HD // 2, dtype=F32) * (-2.0 * math.log(10000.0) / HD))
    turned = frequency[:, None] * positions.astype(F32)
    table = jnp.concatenate([jnp.cos(turned), jnp.sin(turned), jnp.broadcast_to(blocks.astype(F32), (8, T))], 0)
    gains = jnp.concatenate([attn_gain[None], mlp_gain[None], jnp.zeros((6, 512), BF)], 0).astype(F32)
    shape = jax.ShapeDtypeStruct
    grads = [shape((rows, cols), BF) for _, rows, cols in GRADS]
    any_spec = pl.BlockSpec(memory_space=pl.ANY)
    v = pltpu.VMEM
    results = pl.pallas_call(
        layer_kernel,
        out_shape=[shape((T, W), BF), shape((T, W), F32), shape((8, 512), F32)] + grads * 4,
        in_specs=[any_spec] * 11,
        out_specs=[any_spec] * 27,
        scratch_shapes=[
            v((4 * T, W), BF), v((4 * T, W), BF), v((4 * T, W), BF), v((4 * T, W), BF),
            v((W, 512), BF), v((T, W), BF), v((W, WIN), BF), v((W, WIN), BF), v((WIN, W), BF),
            v((4 * T, WIN), BF), v((4 * T, WIN), BF), v((4 * T, WIN), BF),
            v((4 * T, T), BF), v((4, 4, T, TILE), BF), v((4 * T, T), BF),
            v((4, T, H), BF), v((4, T, H), BF), v((2, T, H), BF), v((2, T, 512), BF), v((T, H), F32), v((T, H), F32), v((T, H), F32), v((T, W), BF),
            v((4, 72, T), F32), v((8, W), F32), v((4, 8, T), F32), v((T, TILE), F32), v((T, TILE), F32),
            v((3, T, TILE), F32), v((3, T, TILE), F32), v((4, 8, T), F32), v((4 * T, T), BF),
            v((4 * WIN, 512), BF), v((3, 512, T), BF),
            v((512, TILE), F32), v((W, TILE), BF), v((3, 512, TILE), BF),
            v((T, H), BF), v((8, H), F32), v((4, 8, H), F32), v((4, 8, H), F32), v((8, W), F32),
            pltpu.SemaphoreType.DMA((REMOTE_SEMS,)), pltpu.SemaphoreType.DMA((REMOTE_SEMS,)),
            pltpu.SemaphoreType.DMA((LOCAL_SEMS,)), pltpu.SemaphoreType.REGULAR,
        ],
        compiler_params=pltpu.CompilerParams(collective_id=0, has_side_effects=True, vmem_limit_bytes=62 << 20),
    )(inputs, table, gains, cotangent, w_query, w_key, w_value, w_out, w_gate, w_up, w_down)
    return finish(*results[:3], *results[-6:])


def finish_kernel(*refs):
    output, input_grad, gains, down, gate, up, out, query, kv = refs[:9]
    targets = refs[9:]
    for source, target in zip((output, input_grad), targets):
        target[0] = source[...]
    attn_target, q_target, k_target, v_target, o_target, mlp_target, g_target, u_target, d_target = targets[2:]
    attn_target[...] = gains[0:1, :]
    mlp_target[...] = gains[1:2, :]
    k_target[...] = kv[:, :TILE].astype(F32)
    v_target[...] = kv[:, TILE:].astype(F32)
    for source, target in ((query, q_target), (out, o_target), (gate, g_target), (up, u_target), (down, d_target)):
        target[...] = source[...].astype(F32)


def finish(output, input_grad, gains, down, gate, up, out, query, kv):
    parts = 4
    shape = jax.ShapeDtypeStruct

    def rows(count, cols):
        return pl.BlockSpec((count // parts, cols), lambda i: (i, 0))

    def page(count, cols):
        return pl.BlockSpec((1, count // parts, cols), lambda i: (0, i, 0))

    line = pl.BlockSpec((1, 512), lambda i: (0, 0))
    results = pl.pallas_call(
        finish_kernel,
        grid=(parts,),
        in_specs=[rows(T, W), rows(T, W), pl.BlockSpec((8, 512), lambda i: (0, 0))] + [rows(*a.shape) for a in (down, gate, up, out, query, kv)],
        out_specs=[page(T, W), page(T, W), line, rows(512, 1024), rows(512, TILE), rows(512, TILE), rows(1024, 512), line, rows(512, 2816), rows(512, 2816), rows(2816, 512)],
        out_shape=[shape((1, T, W), BF), shape((1, T, W), F32), shape((1, 512), F32)]
        + [shape(a, F32) for a in ((512, 1024), (512, TILE), (512, TILE), (1024, 512), (1, 512), (512, 2816), (512, 2816), (2816, 512))],
        compiler_params=pltpu.CompilerParams(dimension_semantics=("arbitrary",)),
    )(output, input_grad, gains, down, gate, up, out, query, kv)
    results = list(results)
    results[2], results[7] = results[2][0], results[7][0]
    return tuple(results)


def solution(mesh):
    n, m = mesh.shape["fsdp"], mesh.shape["ctx"]

    def step(*args):
        return layer_call(*args) if n == m == 4 else local(n, m, *args)

    return jax.shard_map(
        step,
        mesh=mesh,
        in_specs=(
            P("fsdp", "ctx", None),
            P("fsdp", "ctx"),
            P("fsdp", "ctx"),
            P("fsdp", "ctx", None),
            P("fsdp"),
            P("fsdp", "tp"),
            P("fsdp", "tp"),
            P("fsdp", "tp"),
            P("tp", "fsdp"),
            P("fsdp"),
            P("fsdp", "tp"),
            P("fsdp", "tp"),
            P("tp", "fsdp"),
        ),
        out_specs=(
            P("fsdp", "ctx", None),
            P("fsdp", "ctx", None),
            P("fsdp"),
            P("fsdp", "tp"),
            P("fsdp", "tp"),
            P("fsdp", "tp"),
            P("tp", "fsdp"),
            P("fsdp"),
            P("fsdp", "tp"),
            P("fsdp", "tp"),
            P("tp", "fsdp"),
        ),
        check_vma=False,
    )
```

```python
import functools
import math

import jax
import jax.numpy as jnp
from jax import lax
from jax.experimental import pallas as pl
from jax.experimental.pallas import tpu as pltpu
from jax.sharding import PartitionSpec as P

HD = 64
EPSILON = 1e-05
NEGATIVE = -1e30
BF = jnp.bfloat16
F32 = jnp.float32


def dot(a, b, ca, cb):
    return lax.dot_general(a, b, (((ca,), (cb,)), ((), ())), preferred_element_type=F32)


def angles(positions):
    half = HD // 2
    frequency = jnp.exp(jnp.arange(half, dtype=F32) * (-2.0 * math.log(10000.0) / HD))
    turned = positions.astype(F32)[:, None] * frequency[None, :]
    return jnp.cos(turned)[:, None, :], jnp.sin(turned)[:, None, :]


def rotate(values, cosine, sine):
    half = HD // 2
    a, b = values[..., :half], values[..., half:]
    return jnp.concatenate([a * cosine - b * sine, b * cosine + a * sine], axis=-1)


def gated(values, after):
    return lax.optimization_barrier((values, after))[0]


def local(n, m, inputs, positions, blocks, cotangent, attn_gain, w_query, w_key, w_value, w_out, mlp_gain, w_gate, w_up, w_down):
    f = lax.axis_index("fsdp")
    z = lax.axis_index("ctx")
    t = lax.axis_index("tp")
    tokens, width = inputs.shape[1:]
    half = width // 2
    peers = range(1, n)

    def plane(x, k):
        return x if k == 0 else lax.ppermute(x, "fsdp", [(i, i ^ k) for i in range(n)])

    def column(x, k):
        return x if k == 0 else lax.ppermute(x, "ctx", [(i, i ^ k) for i in range(m)])

    def swap(x):
        return lax.ppermute(x, "tp", [(0, 1), (1, 0)])

    def part(x, index, axis):
        size = x.shape[axis] // n
        return lax.dynamic_slice_in_dim(x, index * size, size, axis)

    def mine(x, which):
        return lax.dynamic_slice_in_dim(x, which * half, half, x.ndim - 1)

    def place(pieces, axis):
        size = pieces[0].shape[axis]
        shape = list(pieces[0].shape)
        shape[axis] = size * n
        whole = jnp.zeros(shape, pieces[0].dtype)
        for k in range(n):
            whole = lax.dynamic_update_slice_in_dim(whole, pieces[k], (f ^ k) * size, axis)
        return whole

    def join(own, other):
        return jnp.where(t == 0, jnp.concatenate([own, other], -1), jnp.concatenate([other, own], -1))

    def gather(x):
        rows = jnp.concatenate([plane(x, k) for k in range(n)], 0)
        return join(rows, swap(rows))

    def scatter(partial):
        own = mine(partial, t) + swap(mine(partial.astype(BF), 1 - t)).astype(F32)
        low = own.astype(BF)
        total = own[:tokens]
        for k in peers:
            total = total + plane(low[k * tokens : (k + 1) * tokens], k).astype(F32)
        return total

    def row_mean(own):
        own = jnp.sum(own, -1)
        return ((own + swap(own)) / width)[:, None]

    x = inputs[0].astype(F32)
    gains = jnp.stack([attn_gain, mlp_gain])
    gains = place([plane(gains, k) for k in range(n)], 1).astype(F32)
    marks = jnp.stack([positions[0], blocks[0]])
    marks = [plane(marks, k) for k in range(n)]
    place_rows = jnp.concatenate([mk[0] for mk in marks])
    query_ids = jnp.stack([mk[1] for mk in marks])
    scale_one = lax.rsqrt(jnp.mean(x * x, axis=-1, keepdims=True) + EPSILON)
    x_half = mine(x, t)
    hat_one = x_half * scale_one
    gain_one, gain_two = mine(gains[0:1], t), mine(gains[1:2], t)
    xn_one = gather((hat_one * gain_one).astype(BF))

    heads = w_query.shape[1] // HD // n
    cols = heads * HD
    kv_pair = jnp.concatenate([w_key, w_value], 1)
    kv_heads = w_key.shape[1] // HD
    w_qkv = place([plane(jnp.concatenate([part(w_query, f ^ k, 1), kv_pair], 1), k) for k in range(n)], 0)
    wo = gated(w_out, xn_one)
    wo = place([plane(part(wo, f ^ k, 0), k) for k in range(n)], 1)
    gate_up = gated((w_gate, w_up), xn_one)
    gate_up = [plane(jnp.stack([part(gate_up[0], f ^ k, 1), part(gate_up[1], f ^ k, 1)]), k) for k in range(n)]
    wg = place([g[0] for g in gate_up], 0)
    wu = place([g[1] for g in gate_up], 0)

    qkv = dot(xn_one, w_qkv, 1, 0)
    cosine, sine = angles(place_rows)
    kv_here = (heads * f) // ((w_query.shape[1] // HD) // kv_heads)

    def pick(both):
        out = both[:, :HD]
        for g in range(1, kv_heads):
            out = jnp.where(kv_here == g, both[:, g * HD : (g + 1) * HD], out)
        return out

    kw = kv_heads * HD
    query = rotate(qkv[:, :cols].reshape(-1, heads, HD), cosine, sine).astype(BF)
    key = rotate(pick(qkv[:, cols : cols + kw])[:, None, :], cosine, sine)[:, 0, :].astype(BF)
    value = pick(qkv[:, cols + kw :]).astype(BF)
    key_value = jnp.concatenate([key, value], 1).reshape(n, tokens, 2 * HD)
    kv_all = jnp.concatenate([column(key_value, k) for k in range(m)], 1)
    ids_all = jnp.concatenate([column(query_ids, k) for k in range(m)], 1)
    keys, values = kv_all[..., :HD], kv_all[..., HD:]
    factor = 1.0 / math.sqrt(HD)
    query = query.reshape(n, tokens, heads, HD)
    allowed = (ids_all[:, None, :] <= query_ids[:, :, None])[:, None]
    scores = jnp.einsum("nthd,nsd->nhts", query, keys, preferred_element_type=F32) * factor
    scores = jnp.where(allowed, scores, NEGATIVE)
    top = jnp.max(scores, -1, keepdims=True)
    raw = jnp.where(allowed, jnp.exp(scores - top), 0.0)
    weights = raw / jnp.sum(raw, -1, keepdims=True)
    weights_low = weights.astype(BF)
    attended = jnp.einsum("nhts,nsd->nthd", weights_low, values, preferred_element_type=F32)
    attended_low = attended.astype(BF).reshape(n * tokens, cols)

    hidden = x_half + scatter(dot(attended_low, wo, 1, 0))
    scale_two = lax.rsqrt(row_mean(hidden * hidden) + EPSILON)
    hat_two = hidden * scale_two
    xn_two = gather((hat_two * gain_two).astype(BF))
    cot = gather(gated(mine(cotangent[0], t), wg))
    wd = gated(w_down, wg)
    wd = place([plane(part(wd, f ^ k, 0), k) for k in range(n)], 1)
    gate = dot(xn_two, wg, 1, 0)
    up = dot(xn_two, wu, 1, 0)
    sigma = jax.nn.sigmoid(gate)
    silu = gate * sigma
    act = (silu * up).astype(BF)
    dact = dot(cot, wd, 1, 1)
    dgate = (dact * up * sigma * (1.0 + gate * (1.0 - sigma))).astype(BF)
    dup = (dact * silu).astype(BF)

    def reduce(piece):
        if m != 4:
            return lax.psum(piece, "ctx")
        one = (piece.astype(F32) + lax.ppermute(piece, "ctx", [(0, 1), (3, 2)]).astype(F32)).astype(BF)
        two = (one.astype(F32) + lax.ppermute(one, "ctx", [(1, 2), (2, 1)]).astype(F32)).astype(BF)
        three = lax.ppermute(two, "ctx", [(1, 0), (2, 3)])
        return jnp.where((z == 0) | (z == 3), three, two)

    def share(grad, axis):
        low = grad.astype(BF)
        return [plane(part(low, f ^ k, axis), k) for k in range(n)]

    down_parts = [reduce(p) for p in share(dot(act, cot, 0, 0), 1)]
    gate_parts = [reduce(p) for p in share(dot(xn_two, dgate, 0, 0), 0)]
    up_parts = [reduce(p) for p in share(dot(xn_two, dup, 0, 0), 0)]
    d_two = scatter(dot(dgate, wg, 1, 1) + dot(dup, wu, 1, 1))
    out_half = (hidden + scatter(dot(act, wd, 1, 0))).astype(BF)
    output = join(out_half, swap(out_half))
    gain_two_grad = jnp.sum(d_two * hat_two, 0)
    e_two = d_two * gain_two
    d_hidden = mine(cotangent[0], t).astype(F32) + scale_two * (e_two - hat_two * row_mean(e_two * hat_two))
    dhb = gather(d_hidden.astype(BF))
    out_parts = [reduce(p) for p in share(dot(attended_low, dhb, 0, 0), 1)]

    d_att = dot(dhb, wo, 1, 1).astype(BF).reshape(n, tokens, heads, HD)
    delta = jnp.einsum("nthd,nthd->nht", d_att.astype(F32), attended)
    d_weights = jnp.einsum("nthd,nsd->nhts", d_att, values, preferred_element_type=F32)
    d_scores = (weights * (d_weights - delta[..., None])).astype(BF)
    dv = jnp.einsum("nhts,nthd->nsd", weights_low, d_att, preferred_element_type=F32)
    dk = jnp.einsum("nhts,nthd->nsd", d_scores, query, preferred_element_type=F32) * factor
    dq = jnp.einsum("nhts,nsd->nthd", d_scores, keys, preferred_element_type=F32) * factor
    d_kv = jnp.concatenate([dk, dv], -1).reshape(n, m, tokens, 2 * HD)
    d_low = d_kv.astype(BF)
    d_kv_own = d_kv[:, 0]
    for k in range(1, m):
        d_kv_own = d_kv_own + column(d_low[:, k], k).astype(F32)
    d_kv_own = d_kv_own.reshape(n * tokens, 2 * HD)
    dq = rotate(dq.reshape(n * tokens, heads, HD), cosine, -sine).reshape(n * tokens, cols)
    dk = rotate(d_kv_own[:, None, :HD], cosine, -sine)[:, 0, :]
    d_qkv = jnp.concatenate([dq, dk, d_kv_own[:, HD:]], 1).astype(BF)
    w_here = jnp.concatenate([w_qkv[:, :cols], pick(w_qkv[:, cols : cols + kw]), pick(w_qkv[:, cols + kw :])], 1)
    d_one = scatter(dot(d_qkv, w_here, 1, 1))
    qkv_parts = share(dot(xn_one, d_qkv, 0, 0), 0)
    key_parts, value_parts = [0.0] * kv_heads, [0.0] * kv_heads
    for k in range(n):
        owner = (heads * (f ^ k)) // ((w_query.shape[1] // HD) // kv_heads)
        piece = qkv_parts[k].astype(F32)
        for g in range(kv_heads):
            key_parts[g] = key_parts[g] + jnp.where(owner == g, piece[:, cols : cols + HD], 0.0)
            value_parts[g] = value_parts[g] + jnp.where(owner == g, piece[:, cols + HD :], 0.0)
    small = reduce(jnp.concatenate(key_parts + value_parts, 1).astype(BF)).astype(F32)
    query_parts = [reduce(p[:, :cols]) for p in qkv_parts]
    gain_one_grad = jnp.sum(d_one * hat_one, 0)
    e_one = d_one * gain_one
    in_half = d_hidden + scale_one * (e_one - hat_one * row_mean(e_one * hat_one))
    input_grad = join(in_half, swap(in_half))
    gain_grads = jnp.stack([gain_one_grad, gain_two_grad])
    nothing = jnp.zeros_like(gain_grads)
    gain_grads = jnp.where(t == 0, jnp.concatenate([gain_grads, nothing], 1), jnp.concatenate([nothing, gain_grads], 1))
    gain_grads = part(lax.psum(gain_grads, ("fsdp", "ctx", "tp")), f, 1)

    def settle(pieces, axis):
        return place(pieces, axis).astype(F32)

    return (
        output[None],
        input_grad[None],
        gain_grads[0],
        settle(query_parts, 1),
        small[:, :kw],
        small[:, kw:],
        settle(out_parts, 0),
        gain_grads[1],
        settle(gate_parts, 1),
        settle(up_parts, 1),
        settle(down_parts, 0),
    )


T, W, H, TILE = 256, 2048, 1024, 128
MAIN, WIN = 640, 768
GRADS = (("d", 2816, 512), ("g", 512, 2816), ("u", 512, 2816), ("o", 1024, 512), ("q", 512, 1024), ("k", 512, 256))
PART = 384


PARTS = {"dA": (0, 128), "dB": (128, 256), "dC": (PART, PART)}
PARTS |= {name + which: (0 if which == "A" else PART, PART) for name in "gu" for which in "AB"}
LAST = ("dC", "gB", "uB")
GROUPS = tuple(PARTS) + ("o", "q", "k")


def chunk_list():
    chunks = []
    for group, (_, size) in PARTS.items():
        for j in range(4):
            part = MAIN - PART if group in LAST and j % 2 else size
            chunks.append((group, group[0], j, j) + ((part, 512) if group[0] == "d" else (512, part)))
    chunks += [("o", "o", r, 0, 256, 512) for r in range(0, 1024, 256)]
    chunks += [("q", "q", 0, c, 512, 256) for c in range(0, 1024, 256)]
    return chunks + [("k", "k", r, 0, 256, 256) for r in (0, 256)]


CHUNKS = chunk_list()
DEPTH = 4
ORDER = (
    "dA", "+", "feed_back", 1, 1, 1, "dB", "gate_A", 1, 1, "d2_first", 1, "d2_own", 1, "dC", "relay", 1, 1, "gate_B", "gA", 1,
    "norm_two_back", 1, 1, 1, "gB", "up_A", 1, 1, "dh_take", "+", "out_grads", 1, "attend0", 1, "attend1", 1, "uA", "+", "up_B", 1, "attend2", 1,
    "attend3", "pair_send", 1, "-", "pair_sum", "uB", "+", 1, "o", "d_kv_take", 1, "qkv_grads", 1, "d1_first", 1, "d1_own", 1, "q", 1, "relay", 1,
    "kv_ready", 1, 1, "norm_one_back", 1, "out_first", 1, "out_own", 1, "relay", 1, "-", "gains_column", "-", "out_end", "gains_end",
)
MESH = pl.DeviceIdType.MESH


def nn(a, b):
    return lax.dot_general(a, b, (((1,), (0,)), ((), ())), preferred_element_type=F32)


def nt(a, b):
    return lax.dot_general(a, b, (((1,), (1,)), ((), ())), preferred_element_type=F32)


def tn(a, b):
    return lax.dot_general(a, b, (((0,), (0,)), ((), ())), preferred_element_type=F32)


def flip(a, k):
    return (a % 2 + k % 2) % 2 + 2 * ((a // 2 + k // 2) % 2)


def layer_kernel(*refs):
    names = iter(refs)

    def take(count):
        return [next(names) for _ in range(count)]

    x_in, table_in, gains_in, cot_in, wq, wk, wv, wo, wg, wu, wd = take(11)
    out_ref, in_grad_ref, gain_ref = take(3)
    first, left, cross, total = ({name: next(names) for name, _, _ in GRADS} for _ in range(4))
    (x1, x2, ct, dh, w_qkv, w_o, w_g, w_u, w_d, act, dg, du, q_buf, kv_all, ob) = take(15)
    (ps, pr, rr, rd, yo, hid, d_hid, xv, tb, ga, ids, r1s, r2s, ss_own, ss_other, lse, bias) = take(17)
    (gs_d, kv_g, line, d_kv, d_kv_pair, d_kv_recv, out_s, g_sum, g_plane, g_column, g_whole) = take(11)
    send_sem, recv_sem, local_sem, credit = take(4)
    f, z, t = lax.axis_index("fsdp"), lax.axis_index("ctx"), lax.axis_index("tp")
    sems = iter(range(10**6))
    drains = []

    def al(v, by):
        return pl.multiple_of(v, by)

    def plane(k):
        return (flip(f, k), z, t)

    def column(k):
        return (f, flip(z, k), t)

    core = (f, z, 1 - t)
    rows_f = pl.ds(al(f * T, T), T)
    half = pl.ds(al(t * H, H), H)
    rest = pl.ds(al((1 - t) * H, H), H)

    def rows_of(b):
        return pl.ds(al(b * T, T), T)

    def remote(src, dst, s, device):
        return pltpu.make_async_remote_copy(src_ref=src, dst_ref=dst, send_sem=send_sem.at[s], recv_sem=recv_sem.at[s], device_id=device, device_id_type=MESH)

    def here(src, dst, s):
        return pltpu.make_async_copy(src, dst, local_sem.at[s])

    local_count = iter(range(10**6))

    lx = here(x_in.at[0], xv, next(local_count))
    lx.start()
    lc = here(cot_in.at[0], ct.at[rows_f, :], next(local_count))
    lc.start()
    lh = here(cot_in.at[0, :, half], out_s, next(local_count))
    lh.start()
    lt = here(table_in, tb.at[f], next(local_count))
    lt.start()
    lg = here(gains_in, ga.at[:, pl.ds(al(f * 512, 512), 512)], next(local_count))
    lg.start()

    def starts(r):
        return (11 * r + 1 - t) // 2

    def full(r):
        return (r + t) % 2 == 0

    def weight_moves(k, taking):
        r = flip(f, k)
        sender, taker = (r, f) if taking else (f, r)
        rows = pl.ds(al(sender * 512, 512), 512)
        row_part = pl.ds(al(sender * 512 + z * TILE, TILE), TILE)
        own_part = pl.ds(al(z * TILE, TILE), TILE)
        begin = al(starts(taker) * TILE, TILE)
        tail = al(begin + MAIN, TILE)
        col = al(taker * T, T)
        moves = {
            "o": [(wo.at[pl.ds(col, T), :], w_o.at[:, rows])],
            "g": [(wg.at[:, pl.ds(begin, MAIN)], w_g.at[rows, pl.ds(0, MAIN)])],
            "g+": [(wg.at[:, pl.ds(tail, TILE)], w_g.at[rows, pl.ds(MAIN, TILE)])],
        }
        from_rows, to_rows = pl.ds(0, 512), rows
        if k:
            from_rows, to_rows = pl.ds(al(z % 2 * T, T), T), pl.ds(al(sender * 512 + z % 2 * T, T), T)
        moves["qkv"] = [
            (wq.at[from_rows, pl.ds(col, T)], w_qkv.at[to_rows, pl.ds(0, T)]),
            (wk.at[from_rows, :], w_qkv.at[to_rows, pl.ds(T, TILE)]),
            (wv.at[from_rows, :], w_qkv.at[to_rows, pl.ds(T + TILE, TILE)]),
        ]
        if k == 0:
            moves["u"] = [(wu.at[:, pl.ds(begin, MAIN)], w_u.at[rows, pl.ds(0, MAIN)])]
            moves["u+"] = [(wu.at[:, pl.ds(tail, TILE)], w_u.at[rows, pl.ds(MAIN, TILE)])]
            moves["d"] = [(wd.at[pl.ds(begin, MAIN), :], w_d.at[pl.ds(0, MAIN), rows])]
            moves["d+"] = [(wd.at[pl.ds(tail, TILE), :], w_d.at[pl.ds(MAIN, TILE), rows])]
        else:
            moves["u"] = [(wu.at[own_part, pl.ds(begin, MAIN)], w_u.at[row_part, pl.ds(0, MAIN)])]
            moves["u+"] = [(wu.at[own_part, pl.ds(tail, TILE)], w_u.at[row_part, pl.ds(MAIN, TILE)])]
            moves["d"] = [(wd.at[pl.ds(begin, MAIN), own_part], w_d.at[pl.ds(0, MAIN), row_part])]
            moves["d+"] = [(wd.at[pl.ds(tail, TILE), own_part], w_d.at[pl.ds(MAIN, TILE), row_part])]
        return moves

    w_counts = (("qkv", 3), ("o", 1), ("g", 1), ("g+", 1), ("u", 1), ("u+", 1), ("d", 1), ("d+", 1))
    w_sem = {(key, k, i): next(sems) for key, c in w_counts for k in (1, 2, 3) for i in range(c)}
    w_local = {(key, i): next(local_count) for key, c in w_counts for i in range(c)}

    def weights_each(key, taking, run):
        for k in (1, 2, 3):
            moves = weight_moves(k, taking)
            for i, (src, dst) in enumerate(moves[key]):
                run(remote(src, dst, w_sem[key, k, i], plane(k)))
            if key + "+" in moves:

                @pl.when(full(f if taking else flip(f, k)))
                def _():
                    (src, dst), = moves[key + "+"]
                    run(remote(src, dst, w_sem[key + "+", k, 0], plane(k)))

    def weights_start(key):
        weights_each(key, False, lambda cp: cp.start())

    def weights_wait(key):
        weights_each(key, True, lambda cp: cp.wait_recv())

    def weights_drain():
        for key in ("qkv", "o", "g", "u", "d"):
            weights_each(key, False, lambda cp: cp.wait_send())

    def weights_own(keys, wait):
        moves = weight_moves(0, False)

        def run(key):
            for i, (src, dst) in enumerate(moves[key]):
                cp = here(src, dst, w_local[key, i])
                cp.wait() if wait else cp.start()

        for key in keys:
            run(key)
            if key + "+" in moves:
                pl.when(full(f))(functools.partial(run, key + "+"))

    y_sem = {(key, k, j): next(sems) for key in ("qkv", "u", "d") for k in (1, 2, 3) for j in (1, 2, 3) if key != "qkv" or j == 1}

    def column_each(key, taking, run):
        for k in (1, 2, 3):
            for j in (1, 2, 3):
                from_z = flip(z, j) if taking else z
                part = pl.ds(al(flip(f, k) * 512 + from_z * TILE, TILE), TILE)

                def move(size):
                    ref = w_u.at[part, pl.ds(0, size)] if key == "u" else w_d.at[pl.ds(0, size), part]
                    run(remote(ref, ref, y_sem[key, k, j], column(j)))

                if key == "qkv":
                    if j == 1:
                        ref = w_qkv.at[pl.ds(al(flip(f, k) * 512 + from_z % 2 * T, T), T), :]
                        run(remote(ref, ref, y_sem[key, k, j], column(j)))
                    continue
                pl.when(full(f))(functools.partial(move, WIN))
                pl.when(full(f + 1))(functools.partial(move, MAIN))

    g_sem = [[next(sems) for _ in range(4)] for _ in range(4)]
    f_sem = [[next(sems) for _ in range(4)] for _ in range(4)]
    quarters = (pl.ds(al(t * H, 512), 512), pl.ds(al(t * H + 512, 512), 512))

    def gather_direct(g):
        return (1, 2, 3) if g == 3 else (1, 2)

    def gather_start(g, buf, with_own, src=None):
        block = buf.at[rows_f, half]
        for k in gather_direct(g):
            remote(block if src is None else src, block, g_sem[g][k - 1], plane(k)).start()
        if with_own:
            remote(block, block, f_sem[g][3], core).start()

    def gather_hand(g, buf, k):
        block = buf.at[rows_of(flip(f, k)), half]
        return remote(block, block, f_sem[g][k - 1], core)

    def gather_relay(g, buf, k):
        part = buf.at[rows_of(flip(f, k)), quarters[k - 1]]
        return remote(part, part, g_sem[g][4 - k], plane(3 - k))

    def gather_forward(g, buf):
        for k in gather_direct(g):
            block = buf.at[rows_of(flip(f, k)), half]
            remote(block, block, g_sem[g][k - 1], plane(k)).wait_recv()
            if g != 3:
                gather_relay(g, buf, k).start()
            gather_hand(g, buf, k).start()

    def gather_diagonal(g, buf):
        for k in (1, 2):
            part = buf.at[rows_of(flip(f, 3)), quarters[k - 1]]
            remote(part, part, g_sem[g][4 - k], plane(3 - k)).wait_recv()
        gather_hand(g, buf, 3).start()

    def gather_take(g, buf, k):
        if k == 0:
            block = buf.at[rows_f, rest]
            remote(block, block, f_sem[g][3], core).wait_recv()
        else:
            block = buf.at[rows_of(flip(f, k)), rest]
            remote(block, block, f_sem[g][k - 1], core).wait_recv()

    def gather_drain(g, buf, with_own, src=None):
        block = buf.at[rows_f, half]
        for k in gather_direct(g):
            remote(block if src is None else src, block, g_sem[g][k - 1], plane(k)).wait_send()
        for k in (1, 2, 3):
            gather_hand(g, buf, k).wait_send()
            if g != 3 and k != 3:
                gather_relay(g, buf, k).wait_send()
        if with_own:
            remote(block, block, f_sem[g][3], core).wait_send()

    t_sem = [next(sems) for _ in range(3)]
    a_sem = [next(sems) for _ in range(3)]
    own_gain = ga.at[:, pl.ds(al(f * 512, 512), 512)]

    barrier = pltpu.get_barrier_semaphore()
    for k in (1, 2, 3):
        pl.semaphore_signal(barrier, inc=1, device_id=plane(k), device_id_type=MESH)
        pl.semaphore_signal(barrier, inc=1, device_id=column(k), device_id_type=MESH)
    pl.semaphore_signal(barrier, inc=1, device_id=core, device_id_type=MESH)
    pl.semaphore_wait(barrier, 7)

    lt.wait()
    lg.wait()
    for k in (1, 2, 3):
        remote(own_gain, own_gain, a_sem[k - 1], plane(k)).start()
        remote(tb.at[f], tb.at[f], t_sem[k - 1], plane(k)).start()
    weights_start("qkv")
    weights_own(("qkv",), False)

    @pl.when(full(f + 1))
    def _():
        w_g[:, MAIN:WIN] = jnp.zeros((W, TILE), BF)
        w_u[:, MAIN:WIN] = jnp.zeros((W, TILE), BF)
        w_d[MAIN:WIN, :] = jnp.zeros((TILE, W), BF)

    lx.wait()
    for k in (1, 2, 3):
        dst = ga.at[:, pl.ds(al(flip(f, k) * 512, 512), 512)]
        remote(dst, dst, a_sem[k - 1], plane(k)).wait_recv()

    STEP = 32

    def sub(i):
        return pl.ds(al(i * STEP, STEP), STEP)

    @pl.loop(0, T // STEP)
    def _(i):
        xs = xv[sub(i), :].astype(F32)
        scale = lax.rsqrt(jnp.mean(xs * xs, axis=-1, keepdims=True) + EPSILON)
        r1s[sub(i), :] = jnp.broadcast_to(scale, (STEP, TILE))
        x1[pl.ds(al(f * T + i * STEP, STEP), STEP), :] = (xs * scale * ga[0:1, :]).astype(BF)

    weights_wait("qkv")
    column_each("qkv", False, lambda cp: cp.start())
    gather_start(0, x1, False)
    gather_forward(0, x1)
    for key in "oudg":
        weights_start(key)
    weights_own("oudg", False)
    gather_diagonal(0, x1)
    for k in (1, 2, 3):
        dst = tb.at[flip(f, k)]
        remote(dst, dst, t_sem[k - 1], plane(k)).wait_recv()
    weights_own(("qkv",), True)
    column_each("qkv", True, lambda cp: cp.wait_recv())

    lane = lax.broadcasted_iota(jnp.int32, (T, TILE), 1)
    low_lane = lane < HD
    first_half = lane % HD < HD // 2
    kv_head = f // 2

    def turns(b):
        cosine, sine = tb[b, 0:32, :], tb[b, 32:64, :]
        return (
            jnp.transpose(jnp.concatenate([cosine] * 4, 0)),
            jnp.transpose(jnp.concatenate([-sine, sine, -sine, sine], 0)),
        )

    def turn(v, c, s):
        swapped = jnp.where(first_half, pltpu.roll(v, TILE - 32, 1), pltpu.roll(v, 32, 1))
        return v * c + swapped * s

    def qkv_block(k):
        b = flip(f, k)
        qkv = nn(x1[rows_of(b), :], w_qkv[...])
        c, s = turns(b)
        for i in range(2):
            q = turn(qkv[:, i * TILE : (i + 1) * TILE], c, s) * 0.125
            q_buf[rows_of(b), i * TILE : (i + 1) * TILE] = q.astype(BF)
        key = turn(qkv[:, 2 * TILE : 3 * TILE], c, s)
        value = qkv[:, 3 * TILE :]
        key = jnp.where(kv_head == 0, key, pltpu.roll(key, HD, 1))
        value = jnp.where(kv_head == 1, value, pltpu.roll(value, HD, 1))
        kv_all[z, b, :, :] = jnp.where(low_lane, key, value).astype(BF)
        ids[z, pl.ds(b, 1), :] = tb[b, 64:65, :]

    qkv_block(0)
    for k in (1, 2, 3):
        gather_take(0, x1, k)

    @pl.loop(1, 4)
    def _(k):
        qkv_block(k)

    z_sem = [[next(sems) for _ in range(2)] for _ in range(3)]
    for k in (1, 2, 3):
        remote(kv_all.at[z], kv_all.at[z], z_sem[k - 1][0], column(k)).start()
        remote(ids.at[z], ids.at[z], z_sem[k - 1][1], column(k)).start()
    for k in (1, 2, 3):
        zz = flip(z, k)
        remote(kv_all.at[zz], kv_all.at[zz], z_sem[k - 1][0], column(k)).wait_recv()
        remote(ids.at[zz], ids.at[zz], z_sem[k - 1][1], column(k)).wait_recv()
    lc.wait()
    weights_wait("u")
    column_each("u", False, lambda cp: cp.start())

    low_keys = lax.broadcasted_iota(jnp.int32, (4 * T, TILE), 1) < HD

    def bias_of(s):
        query_id = ids[z, pl.ds(s, 1), :]
        for j in range(4):
            key_id = jnp.transpose(jnp.broadcast_to(ids[j, pl.ds(s, 1), :], (8, T)))[:, 0:1]
            bias[j * T : (j + 1) * T, :] = jnp.where(key_id <= query_id, 0.0, NEGATIVE).astype(BF)

    def kv_of(s):
        kv = jnp.concatenate([kv_all[j, s, :, :] for j in range(4)], 0).astype(F32)
        turned = pltpu.roll(kv, HD, 1)
        keys = jnp.where(low_keys, kv, turned).astype(BF)
        values = jnp.where(low_keys, turned, kv).astype(BF)
        return kv, keys, values

    def only(v, parity):
        return jnp.where(low_lane if parity == 0 else ~low_lane, v.astype(F32), 0.0).astype(BF)

    @pl.loop(0, 4)
    def _(s):
        bias_of(s)
        kv, keys, _ = kv_of(s)
        values_t = jnp.transpose(kv)[HD:, :].astype(BF)

        for i in range(2):
            mixed = []
            for parity in range(2):
                q = only(q_buf[rows_of(s), i * TILE : (i + 1) * TILE], parity)
                scores = nt(keys, q) + bias[...].astype(F32)
                top = jnp.max(scores, axis=0, keepdims=True)
                raw = jnp.exp(scores - top)
                norm = jnp.sum(raw, axis=0, keepdims=True)
                lse[s, 2 * i + parity : 2 * i + parity + 1, :] = top + jnp.log(norm)
                mixed.append(nn(values_t, raw.astype(BF)) * (1.0 / norm))
            ob[rows_of(s), i * TILE : (i + 1) * TILE] = jnp.transpose(jnp.concatenate(mixed, 0)).astype(BF)

    p_sem = [next(sems) for _ in range(4)][0]
    s_sem = [next(sems) for _ in range(6)]
    COLS = 256
    lows, highs = pl.ds(0, 512), pl.ds(512, 512)

    def pass_first(k):
        return remote(ps.at[3, :, (lows, highs)[k - 1]], rd.at[k - 1], s_sem[k - 1], plane(k))

    def pass_second(k, added):
        cols = (lows, highs)[k - 1 if not added else 2 - k]
        return remote(ps.at[k, :, cols], rr.at[k - 1, :, cols], s_sem[2 * k + added], plane(k))

    def tiles(run):
        @pl.loop(0, H // COLS)
        def _(j):
            run(pl.ds(al(j * COLS, COLS), COLS), j * COLS)

    def core_move(k):
        return remote(ps.at[k], pr.at[k], p_sem + k, core)

    def scatter_first(product):
        @pl.loop(0, 4)
        def _(i):
            k = (7 - i) % 4

            def run(cols, c):
                ps[k, :, cols] = product(flip(f, k), (1 - t) * H + c).astype(BF)

            tiles(run)
            core_move(k).start()

    def scatter_own(product):
        @pl.loop(0, 3)
        def _(i):
            k = (i + 2) % 3 + 1
            core_move(k).wait()

            def run(cols, c):
                ps[k, :, cols] = (product(flip(f, k), t * H + c) + pr[k, :, cols].astype(F32)).astype(BF)

            tiles(run)

            @pl.when(k == 3)
            def _():
                pass_first(1).start()
                pass_first(2).start()

        pass_second(1, 0).start()
        pass_second(2, 0).start()
        core_move(0).wait()

        def run(cols, c):
            yo[:, cols] = product(f, t * H + c) + pr[0, :, cols].astype(F32)

        tiles(run)

    def scatter_steps(product):
        return functools.partial(scatter_first, product), functools.partial(scatter_own, product)

    def scatter_relay():
        for k in (1, 2):
            pass_first(3 - k).wait()
            c = (512, 0)[k - 1]

            @pl.loop(0, T // STEP)
            def _(i):
                ps[k, sub(i), c : c + 512] = (ps[k, sub(i), c : c + 512].astype(F32) + rd[2 - k, sub(i), :].astype(F32)).astype(BF)

            pass_second(k, 1).start()

    def scatter_wait():
        for k in (1, 2):
            for added in (0, 1):
                pass_second(k, added).wait()

    def scattered(i):
        return yo[sub(i), :] + rr[0, sub(i), :].astype(F32) + rr[1, sub(i), :].astype(F32)

    n_sem = [next(sems) for _ in range(3)]

    def core_sums(u):
        remote(ss_own.at[u], ss_other.at[u], n_sem[u], core).start()
        remote(ss_own.at[u], ss_other.at[u], n_sem[u], core).wait()

    weights_wait("o")
    weights_own("o", True)
    for step in scatter_steps(lambda b, c: nn(ob[rows_of(b), :], w_o[:, pl.ds(al(c, COLS), COLS)])):
        step()
    scatter_relay()
    scatter_wait()
    weights_wait("d")
    column_each("d", False, lambda cp: cp.start())

    @pl.loop(0, T // STEP)
    def _(i):
        rows = xv[sub(i), half].astype(F32) + scattered(i)
        hid[sub(i), :] = rows
        ss_own[0, sub(i), :] = jnp.broadcast_to(jnp.sum(rows * rows, axis=-1, keepdims=True), (STEP, TILE))

    core_sums(0)
    gain_one, gain_two = ga[0:1, half], ga[1:2, half]

    @pl.loop(0, T // STEP)
    def _(i):
        scale = lax.rsqrt((ss_own[0, sub(i), 0:1] + ss_other[0, sub(i), 0:1]) * (1.0 / W) + EPSILON)
        r2s[sub(i), :] = jnp.broadcast_to(scale, (STEP, TILE))
        x2[pl.ds(al(f * T + i * STEP, STEP), STEP), half] = (hid[sub(i), :] * scale * gain_two).astype(BF)

    gather_start(2, x2, True)
    gather_forward(2, x2)
    gather_start(1, ct, False, cot_in.at[0, :, half])
    weights_wait("g")
    weights_own("ugd", True)
    column_each("u", True, lambda cp: cp.wait_recv())

    UNITS = 256

    def feed_block(k):
        b = flip(f, k)

        @pl.loop(0, WIN // UNITS)
        def _(j):
            cols = pl.ds(al(j * UNITS, UNITS), UNITS)
            gate = nn(x2[rows_of(b), :], w_g[:, cols])
            up = nn(x2[rows_of(b), :], w_u[:, cols])
            sigma = jax.nn.sigmoid(gate)
            silu = gate * sigma
            act[rows_of(b), cols] = (silu * up).astype(BF)
            dg[rows_of(b), cols] = (up * sigma * (1.0 + gate * (1.0 - sigma))).astype(BF)
            du[rows_of(b), cols] = silu.astype(BF)

    for k in (0, 1, 2):
        gather_take(2, x2, k)

    @pl.loop(0, 3)
    def _(k):
        feed_block(k)

    gather_diagonal(2, x2)
    gather_take(2, x2, 3)
    feed_block(3)
    gather_forward(1, ct)
    gather_diagonal(1, ct)
    for k in (1, 2, 3):
        gather_take(1, ct, k)

    e_sem = {(name, i): [next(sems) for _ in range(3)][0] for name in GROUPS for i in range(2 if name in LAST else 1)}
    e_local = {(name, i): next(local_count) for name in GROUPS for i in range(2 if name in LAST else 1)}

    def stage(name, k):
        if name == "d":
            return gs_d.at[pl.ds(al(k * WIN, WIN), WIN), :]
        if name in "gu":
            return ct.at[pl.ds(al((k // 2) * 512, 512), 512), pl.ds(al((k % 2) * H, H), WIN)]
        if name == "o":
            return gs_d.at[pl.ds(al(k * WIN, WIN), T), :]
        return x2.at[pl.ds(al((k // 2) * 512, 512), 512), pl.ds(al((k % 2) * 512 + (0 if name == "q" else T), T), T)]

    def grad_moves(group, k, sender):
        name = group[0]
        buf, begin = stage(name, k), al(starts(sender) * TILE, TILE)
        if name in "dgu":
            parts = [(PART, MAIN - PART), (MAIN, TILE)] if group in LAST else [PARTS[group]]
            if name == "d":
                return [(buf.at[pl.ds(c, size), :], first["d"].at[pl.ds(al(begin + c, TILE), size), :]) for c, size in parts]
            return [(buf.at[:, pl.ds(c, size)], first[name].at[:, pl.ds(al(begin + c, TILE), size)]) for c, size in parts]
        if name == "o":
            return [(buf, first["o"].at[rows_of(sender), :])]
        if name == "q":
            return [(buf, first["q"].at[:, rows_of(sender)])]
        return [(buf, kv_g.at[k - 1])]

    def grad_send(group, k, act_on):
        for i, (src, dst) in enumerate(grad_moves(group, k, f)):

            def run(i=i, src=src, dst=dst):
                if isinstance(k, int) and k == 0:
                    cp = here(src, dst, e_local[group, i])
                    cp.wait() if act_on == "wait" else cp.start()
                else:
                    cp = remote(src, dst, e_sem[group, i] + k - 1, plane(k))
                    cp.wait_send() if act_on == "wait" else cp.start()

            if i == 0:
                run()
            else:
                pl.when(full(f))(run)

    def grad_take(group):
        for k in (1, 2, 3):
            sender = flip(f, k)
            for i, (src, dst) in enumerate(grad_moves(group, k, sender)):

                def run(i=i, src=src, dst=dst):
                    remote(src, dst, e_sem[group, i] + k - 1, plane(k)).wait_recv()

                if i == 0:
                    run()
                else:
                    pl.when(full(sender))(run)

    def sent(*groups):
        for group in groups:
            for k in (1, 2, 3):
                grad_send(group, k, "wait")

    def block_cols(k):
        return pl.ds(al(flip(f, k) * 512, 512), 512)

    def each_owner(product, *groups):
        @pl.loop(0, 4)
        def _(i):
            k = (i + 1) % 4
            product(k)

            @pl.when(k != 0)
            def _():
                for group in groups:
                    grad_send(group, k, "start")

            @pl.when(k == 0)
            def _():
                for group in groups:
                    if group != "k":
                        grad_send(group, 0, "start")

    def down_grads(group):
        c, size = PARTS[group]

        def product(k):
            stage("d", k)[c : c + size, :] = tn(act[:, c : c + size], ct[:, block_cols(k)]).astype(BF)

        each_owner(product, group)

    def feed_grads(name, which, right):
        c = 0 if which == "A" else PART

        def product(k):
            @pl.loop(0, 2)
            def _(i):
                xs = x2[:, pl.ds(al(flip(f, k) * 512 + i * T, T), T)]
                stage(name, k)[pl.ds(al(i * T, T), T), c : c + PART] = tn(xs, right[:, c : c + PART]).astype(BF)

        each_owner(product, name + which)

    for group in ("dA", "dB", "dC"):
        down_grads(group)

    def feed_back():
        column_each("d", True, lambda cp: cp.wait_recv())

        @pl.loop(0, 4)
        def _(b):
            @pl.loop(0, WIN // UNITS)
            def _(j):
                cols = pl.ds(al(j * UNITS, UNITS), UNITS)
                back = nt(ct[rows_of(b), :], w_d[cols, :])
                dg[rows_of(b), cols] = (back * dg[rows_of(b), cols].astype(F32)).astype(BF)
                du[rows_of(b), cols] = (back * du[rows_of(b), cols].astype(F32)).astype(BF)

    def gate_A():
        gather_drain(1, ct, False, cot_in.at[0, :, half])
        feed_grads("g", "A", dg)

    d2_first, d2_own = scatter_steps(
        lambda b, c: nt(dg[rows_of(b), :], w_g[pl.ds(al(c, COLS), COLS), :]) + nt(du[rows_of(b), :], w_u[pl.ds(al(c, COLS), COLS), :])
    )

    end = (z == 0) | (z == 3)
    middle = (z == 1) | (z == 2)
    next_in = (f, jnp.where(z < 2, 1, 2), t)
    next_out = (f, jnp.where(z < 2, 0, 3), t)
    facing = (f, 3 - z, t)
    across = [next(sems) for _ in range(2 * DEPTH)]
    l_sem = [[next(sems), across[i % (2 * DEPTH)], next(sems)] for i in range(len(CHUNKS))]
    v_sem = [next(local_count) for _ in range(2)]
    o_sem = [next(local_count) for _ in range(4)]

    la, lb, *rest_of_line = (line.at[i] for i in range(8))
    tt, ring = rest_of_line[:2], rest_of_line[2:]

    kept, given = (w_g.at[:, pl.ds(512 + j * TILE, TILE)] for j in range(2))
    even = f % 2 == 0

    def pair_rows(pair, j):
        return pl.ds(j * 512 + pair * T, T)


    def window(arrays, i):
        group, name, r, c, rows, cols = CHUNKS[i]
        if name in "dgu":
            j = flip(r, t) if group in LAST else r
            at = al(starts(j) * TILE + PARTS[group][0], TILE)
            r, c = (at, 0) if name == "d" else (0, at)
        return arrays[name].at[pl.ds(r, rows), pl.ds(c, cols)]

    def line_send(group):
        @pl.when(end)
        def _():
            for i, chunk in enumerate(CHUNKS):
                if chunk[0] == group:
                    remote(window(first, i), window(left, i), l_sem[i][0], next_in).start()

    def add_into(dst, a, b, rows, cols):
        @pl.loop(0, rows // STEP)
        def _(i):
            at = sub(i)
            dst[at, pl.ds(0, cols)] = (a[at, pl.ds(0, cols)].astype(F32) + b[at, pl.ds(0, cols)].astype(F32)).astype(BF)

    def line_one(i):
        _, name, r, c, rows, cols = CHUNKS[i]
        part = (pl.ds(0, rows), pl.ds(0, cols))
        a, b, keep = la.at[part], lb.at[part], ring[i % DEPTH]

        @pl.when(middle)
        def _():
            get_a = here(window(first, i), a, v_sem[0])
            get_a.start()
            remote(window(first, i), window(left, i), l_sem[i][0], next_in).wait_recv()
            get_b = here(window(left, i), b, v_sem[1])
            get_b.start()
            get_a.wait()
            get_b.wait()
            add_into(keep, la, lb, rows, cols)
            remote(keep.at[part], window(cross, i), l_sem[i][1], facing).start()

    def line_two(i):
        _, name, r, c, rows, cols = CHUNKS[i]
        part = (pl.ds(0, rows), pl.ds(0, cols))
        keep, done = ring[i % DEPTH], tt[i % 2]

        @pl.when(middle)
        def _():
            remote(keep.at[part], window(cross, i), l_sem[i][1], facing).wait()
            get = here(window(cross, i), lb.at[part], v_sem[1])
            get.start()
            if i >= 2:
                line_out(i - 2)
            get.wait()
            add_into(done, keep, lb, rows, cols)
            remote(done.at[part], window(total, i), l_sem[i][2], next_out).start()
            here(done.at[part], window(total, i), o_sem[i % 4]).start()

    def line_out(i):
        _, name, r, c, rows, cols = CHUNKS[i]
        done = tt[i % 2].at[pl.ds(0, rows), pl.ds(0, cols)]
        remote(done, window(total, i), l_sem[i][2], next_out).wait_send()
        here(done, window(total, i), o_sem[i % 4]).wait()

    pumped, ready = [0, 0], set()

    def ahead():
        i = pumped[0]
        assert CHUNKS[i][0] in ready and i < pumped[1] + DEPTH
        line_one(i)
        pumped[0] += 1

    def behind():
        i = pumped[1]
        assert i < pumped[0]
        line_two(i)
        pumped[1] += 1

    def grad_ready(group):
        grad_take(group)
        grad_send(group, 0, "wait")
        line_send(group)
        ready.add(group)

    g_sum[...] = jnp.zeros((8, H), F32)
    k_sem = [next(sems) for _ in range(3)]
    q_sem = [[next(sems) for _ in range(3)] for _ in range(2)]
    d_ob, d_qkv = ob, dg
    here_half = (lane // HD) == kv_head
    out_local = here(out_s, out_ref.at[:, half], next(local_count))
    out_remote = remote(out_s, out_ref.at[:, half], next(sems), core)
    in_local = here(d_hid, in_grad_ref.at[:, half], next(local_count))
    in_remote = remote(d_hid, in_grad_ref.at[:, half], next(sems), core)
    kv_copy = here(x2.at[pl.ds(0, 512), pl.ds(T, T)], first["k"], next(local_count))
    whole_move = remote(g_whole.at[:, half], g_whole.at[:, half], next(sems), core)
    gain_move = here(g_whole.at[:, pl.ds(al(f * 512, 512), 512)], gain_ref, next(local_count))

    def norm_two_back():
        lh.wait()
        scatter_wait()

        def rows_back(i, carry):
            rows = scattered(i)
            yo[sub(i), :] = rows
            hat = hid[sub(i), :] * r2s[sub(i), 0:1]
            ss_own[1, sub(i), :] = jnp.broadcast_to(jnp.sum(rows * gain_two * hat, axis=-1, keepdims=True), (STEP, TILE))
            return carry + jnp.sum(rows * hat, axis=0, keepdims=True)

        g_sum[1:2, :] = lax.fori_loop(0, T // STEP, rows_back, jnp.zeros((1, H), F32))
        core_sums(1)

        @pl.loop(0, T // STEP)
        def _(i):
            scale = r2s[sub(i), 0:1]
            hat = hid[sub(i), :] * scale
            mean = (ss_own[1, sub(i), 0:1] + ss_other[1, sub(i), 0:1]) * (1.0 / W)
            rows = out_s[sub(i), :].astype(F32) + scale * (yo[sub(i), :] * gain_two - hat * mean)
            d_hid[sub(i), :] = rows
            dh[pl.ds(al(f * T + i * STEP, STEP), STEP), half] = rows.astype(BF)

        gather_start(3, dh, True)

    def dh_take():
        gather_forward(3, dh)
        for k in range(4):
            gather_take(3, dh, k)

    def out_grads():
        sent("dA", "dB", "dC")

        def product(k):
            stage("o", k)[...] = tn(ob[...], dh[:, block_cols(k)]).astype(BF)

        each_owner(product, "o")

        @pl.loop(0, 4)
        def _(b):
            ob[rows_of(b), :] = nt(dh[rows_of(b), :], w_o[...]).astype(BF)

    def attend_back(pair, i_seq):
        s = 2 * pair + i_seq
        bias_of(s)
        kv, keys, values = kv_of(s)
        keys_t = jnp.transpose(kv)[:HD, :].astype(BF)
        c, sn = turns(s)
        d_key = jnp.zeros((4 * T, TILE), F32)
        d_value = jnp.zeros((4 * T, TILE), F32)
        for i in range(2):
            d_query = []
            for parity in range(2):
                q = only(q_buf[rows_of(s), i * TILE : (i + 1) * TILE], parity)
                do = only(d_ob[rows_of(s), i * TILE : (i + 1) * TILE], parity)
                weights = jnp.exp(nt(keys, q) + bias[...].astype(F32) - lse[s, 2 * i + parity : 2 * i + parity + 1, :])
                d_weights = nt(values, do)
                delta = jnp.sum(weights * d_weights, axis=0, keepdims=True)
                d_scores = (weights * (d_weights - delta)).astype(BF)
                d_value = d_value + nn(weights.astype(BF), do)
                d_key = d_key + nn(d_scores, q)
                d_query.append(nn(keys_t, d_scores))
            d_query = jnp.transpose(jnp.concatenate(d_query, 0)) * 0.125
            d_qkv[rows_of(s), i * TILE : (i + 1) * TILE] = turn(d_query, c, -sn).astype(BF)
        d_key = d_key + pltpu.roll(d_key, HD, 1)
        d_value = d_value + pltpu.roll(d_value, HD, 1)
        keep, give = jnp.where(even, d_key, d_value), jnp.where(even, d_value, d_key)
        mine_here = lane // HD == i_seq
        for j in range(4):
            for place, values in ((kept, keep), (given, give)):
                at = pair_rows(pair, j)
                place[at, :] = jnp.where(mine_here, values[j * T : (j + 1) * T, :], place[at, :].astype(F32)).astype(BF)

    pair_move = remote(given, d_kv_pair, next(sems), plane(1))

    def pair_sum():
        pair_move.wait()

        @pl.loop(0, W // STEP)
        def _(i):
            rows = kept[sub(i), :].astype(F32) + d_kv_pair[sub(i), :].astype(F32)
            kept[sub(i), :] = rows.astype(BF)

            @pl.when(i // (512 // STEP) == z)
            def _():
                d_kv[pl.ds(al(i % (512 // STEP) * STEP, STEP), STEP), :] = rows

        for move in d_kv_moves():
            move.start()

    def d_kv_moves():
        return [remote(kept.at[pl.ds(al(flip(z, k) * 512, 512), 512), :], d_kv_recv.at[k - 1], k_sem[k - 1], column(k)) for k in (1, 2, 3)]

    def up_A():
        sent("gA", "gB")
        feed_grads("u", "A", du)

    def d_kv_take():
        for move in d_kv_moves():
            move.wait()

        for s in range(4):
            c, sn = turns(s)
            rows = pl.ds(s // 2 * T, T)
            whole = d_kv[rows, :]
            for k in range(3):
                whole = whole + d_kv_recv[k, rows, :].astype(F32)
            turned = pltpu.roll(whole, HD, 1)
            whole = jnp.where(low_lane, whole, turned) if s % 2 == 0 else jnp.where(low_lane, turned, whole)
            d_qkv[rows_of(s), 2 * TILE : 3 * TILE] = jnp.where(here_half & even, turn(whole, c, -sn), 0.0).astype(BF)
            d_qkv[rows_of(s), 3 * TILE : 4 * TILE] = jnp.where(here_half & ~even, whole, 0.0).astype(BF)

    def qkv_grads():
        gather_drain(2, x2, True)

        def product(k):
            @pl.loop(0, 2)
            def _(i):
                xs = x1[:, pl.ds(al(flip(f, k) * 512 + i * T, T), T)]
                grads = tn(xs, d_qkv[:, 0:512]).astype(BF)
                stage("q", k)[pl.ds(al(i * T, T), T), :] = grads[:, 0:T]
                stage("k", k)[pl.ds(al(i * T, T), T), :] = grads[:, T:]

        each_owner(product, "q", "k")

    d1_first, d1_own = scatter_steps(lambda b, c: nt(d_qkv[rows_of(b), 0:512], w_qkv[pl.ds(al(c, COLS), COLS), :]))
    out_first, out_own = scatter_steps(lambda b, c: nn(act[rows_of(b), :], w_d[:, pl.ds(al(c, COLS), COLS)]))

    def kv_ready():
        grad_take("k")

        @pl.loop(0, 512 // STEP)
        def _(i):
            rows = x2[sub(i), T : 2 * T].astype(F32)
            for k in (1, 2, 3):
                rows = rows + kv_g[k - 1, sub(i), :].astype(F32)
            x2[sub(i), T : 2 * T] = rows.astype(BF)

        kv_copy.start()
        kv_copy.wait()
        line_send("k")
        ready.add("k")

    def norm_one_back():
        scatter_wait()

        def rows_back(i, carry):
            rows = scattered(i)
            yo[sub(i), :] = rows
            hat = xv[sub(i), half].astype(F32) * r1s[sub(i), 0:1]
            ss_own[2, sub(i), :] = jnp.broadcast_to(jnp.sum(rows * gain_one * hat, axis=-1, keepdims=True), (STEP, TILE))
            return carry + jnp.sum(rows * hat, axis=0, keepdims=True)

        g_sum[0:1, :] = lax.fori_loop(0, T // STEP, rows_back, jnp.zeros((1, H), F32))
        for k in (1, 2, 3):
            pl.semaphore_signal(credit, inc=1, device_id=plane(k), device_id_type=MESH)
        pl.semaphore_signal(credit, inc=1, device_id=core, device_id_type=MESH)
        core_sums(2)
        g_plane[f, :, :] = g_sum[...]
        for k in (1, 2, 3):
            remote(g_sum, g_plane.at[f], q_sem[0][k - 1], plane(k)).start()

        @pl.loop(0, T // STEP)
        def _(i):
            scale = r1s[sub(i), 0:1]
            hat = xv[sub(i), half].astype(F32) * scale
            mean = (ss_own[2, sub(i), 0:1] + ss_other[2, sub(i), 0:1]) * (1.0 / W)
            d_hid[sub(i), :] = d_hid[sub(i), :] + scale * (yo[sub(i), :] * gain_one - hat * mean)

        in_local.start()
        in_remote.start()

    def out_begin():
        pl.semaphore_wait(credit, 4)
        out_first()

    def out_end():
        scatter_wait()

        @pl.loop(0, T // STEP)
        def _(i):
            out_s[sub(i), :] = (hid[sub(i), :] + scattered(i)).astype(BF)

        out_local.start()
        out_remote.start()

    def gains_column():
        for k in (1, 2, 3):
            remote(g_sum, g_plane.at[flip(f, k)], q_sem[0][k - 1], plane(k)).wait_recv()
        g_column[z, :, :] = ((g_plane[0, :, :] + g_plane[1, :, :]) + g_plane[2, :, :]) + g_plane[3, :, :]
        for k in (1, 2, 3):
            remote(g_column.at[z], g_column.at[z], q_sem[1][k - 1], column(k)).start()

    def gains_end():
        for k in (1, 2, 3):
            remote(g_column.at[z], g_column.at[flip(z, k)], q_sem[1][k - 1], column(k)).wait_recv()
        g_whole[:, half] = ((g_column[0, :, :] + g_column[1, :, :]) + g_column[2, :, :]) + g_column[3, :, :]
        whole_move.start()
        whole_move.wait()
        gain_move.start()

    steps = {
        "feed_back": feed_back,
        "gate_A": gate_A,
        "d2_first": d2_first,
        "d2_own": d2_own,
        "gate_B": lambda: feed_grads("g", "B", dg),
        "up_A": up_A,
        "up_B": lambda: feed_grads("u", "B", du),
        "relay": scatter_relay,
        "norm_two_back": norm_two_back,
        "dh_take": dh_take,
        "out_grads": out_grads,
        "pair_send": lambda: pair_move.start(),
        "pair_sum": pair_sum,
        "d_kv_take": d_kv_take,
        "qkv_grads": qkv_grads,
        "d1_first": d1_first,
        "d1_own": d1_own,
        "kv_ready": kv_ready,
        "norm_one_back": norm_one_back,
        "out_first": out_begin,
        "out_own": out_own,
        "out_end": out_end,
        "gains_column": gains_column,
        "gains_end": gains_end,
    }
    for step in ORDER:
        if step == "+":
            ahead()
        elif step == "-":
            behind()
        elif step == 1:
            ahead()
            behind()
        elif step in GROUPS:
            grad_ready(step)
        elif step[:6] == "attend":
            attend_back(int(step[6]) // 2, int(step[6]) % 2)
        else:
            steps[step]()
    while pumped[0] < len(CHUNKS):
        ahead()
        behind()
    while pumped[1] < len(CHUNKS):
        behind()

    @pl.when(middle)
    def _():
        line_out(len(CHUNKS) - 2)
        line_out(len(CHUNKS) - 1)

    @pl.when(end)
    def _():
        for i in range(len(CHUNKS)):
            remote(window(first, i), window(left, i), l_sem[i][0], next_in).wait_send()
            remote(window(total, i), window(total, i), l_sem[i][2], next_in).wait_recv()

    gain_move.wait()
    out_local.wait()
    out_remote.wait()
    in_local.wait()
    in_remote.wait()
    weights_drain()
    column_each("d", False, lambda cp: cp.wait_send())
    column_each("u", False, lambda cp: cp.wait_send())
    column_each("qkv", False, lambda cp: cp.wait_send())
    gather_drain(0, x1, False)
    gather_drain(3, dh, True)
    for k in (1, 2, 3):
        remote(own_gain, own_gain, a_sem[k - 1], plane(k)).wait_send()
        remote(tb.at[f], tb.at[f], t_sem[k - 1], plane(k)).wait_send()
        remote(kv_all.at[z], kv_all.at[z], z_sem[k - 1][0], column(k)).wait_send()
        remote(ids.at[z], ids.at[z], z_sem[k - 1][1], column(k)).wait_send()
        remote(g_sum, g_plane.at[f], q_sem[0][k - 1], plane(k)).wait_send()
        remote(g_column.at[z], g_column.at[z], q_sem[1][k - 1], column(k)).wait_send()
        for name in ("uA", "uB", "o", "q", "k"):
            grad_send(name, k, "wait")
    assert (next(sems), next(local_count)) == (REMOTE_SEMS, LOCAL_SEMS)


REMOTE_SEMS, LOCAL_SEMS = 244, 38


def layer_call(inputs, positions, blocks, cotangent, attn_gain, w_query, w_key, w_value, w_out, mlp_gain, w_gate, w_up, w_down):
    frequency = jnp.exp(jnp.arange(HD // 2, dtype=F32) * (-2.0 * math.log(10000.0) / HD))
    turned = frequency[:, None] * positions.astype(F32)
    table = jnp.concatenate([jnp.cos(turned), jnp.sin(turned), jnp.broadcast_to(blocks.astype(F32), (8, T))], 0)
    gains = jnp.concatenate([attn_gain[None], mlp_gain[None], jnp.zeros((6, 512), BF)], 0).astype(F32)
    shape = jax.ShapeDtypeStruct
    grads = [shape((rows, cols), BF) for _, rows, cols in GRADS]
    any_spec = pl.BlockSpec(memory_space=pl.ANY)
    v = pltpu.VMEM
    results = pl.pallas_call(
        layer_kernel,
        out_shape=[shape((T, W), BF), shape((T, W), F32), shape((8, 512), F32)] + grads * 4,
        in_specs=[any_spec] * 11,
        out_specs=[any_spec] * 27,
        scratch_shapes=[
            v((4 * T, W), BF), v((4 * T, W), BF), v((4 * T, W), BF), v((4 * T, W), BF),
            v((W, 512), BF), v((T, W), BF), v((W, WIN), BF), v((W, WIN), BF), v((WIN, W), BF),
            v((4 * T, WIN), BF), v((4 * T, WIN), BF), v((4 * T, WIN), BF),
            v((4 * T, T), BF), v((4, 4, T, TILE), BF), v((4 * T, T), BF),
            v((4, T, H), BF), v((4, T, H), BF), v((2, T, H), BF), v((2, T, 512), BF), v((T, H), F32), v((T, H), F32), v((T, H), F32), v((T, W), BF),
            v((4, 72, T), F32), v((8, W), F32), v((4, 8, T), F32), v((T, TILE), F32), v((T, TILE), F32),
            v((3, T, TILE), F32), v((3, T, TILE), F32), v((4, 8, T), F32), v((4 * T, T), BF),
            v((4 * WIN, 512), BF), v((3, 512, T), BF), v((8, 512, 512), BF),
            v((512, TILE), F32), v((W, TILE), BF), v((3, 512, TILE), BF),
            v((T, H), BF), v((8, H), F32), v((4, 8, H), F32), v((4, 8, H), F32), v((8, W), F32),
            pltpu.SemaphoreType.DMA((REMOTE_SEMS,)), pltpu.SemaphoreType.DMA((REMOTE_SEMS,)),
            pltpu.SemaphoreType.DMA((LOCAL_SEMS,)), pltpu.SemaphoreType.REGULAR,
        ],
        compiler_params=pltpu.CompilerParams(collective_id=0, has_side_effects=True, vmem_limit_bytes=62 << 20),
    )(inputs, table, gains, cotangent, w_query, w_key, w_value, w_out, w_gate, w_up, w_down)
    return finish(*results[:3], *results[-6:])


def finish_kernel(*refs):
    output, input_grad, gains, down, gate, up, out, query, kv = refs[:9]
    targets = refs[9:]
    for source, target in zip((output, input_grad), targets):
        target[0] = source[...]
    attn_target, q_target, k_target, v_target, o_target, mlp_target, g_target, u_target, d_target = targets[2:]
    attn_target[...] = gains[0:1, :]
    mlp_target[...] = gains[1:2, :]
    k_target[...] = kv[:, :TILE].astype(F32)
    v_target[...] = kv[:, TILE:].astype(F32)
    for source, target in ((query, q_target), (out, o_target), (gate, g_target), (up, u_target), (down, d_target)):
        target[...] = source[...].astype(F32)


def finish(output, input_grad, gains, down, gate, up, out, query, kv):
    parts = 4
    shape = jax.ShapeDtypeStruct

    def rows(count, cols):
        return pl.BlockSpec((count // parts, cols), lambda i: (i, 0))

    def page(count, cols):
        return pl.BlockSpec((1, count // parts, cols), lambda i: (0, i, 0))

    line = pl.BlockSpec((1, 512), lambda i: (0, 0))
    results = pl.pallas_call(
        finish_kernel,
        grid=(parts,),
        in_specs=[rows(T, W), rows(T, W), pl.BlockSpec((8, 512), lambda i: (0, 0))] + [rows(*a.shape) for a in (down, gate, up, out, query, kv)],
        out_specs=[page(T, W), page(T, W), line, rows(512, 1024), rows(512, TILE), rows(512, TILE), rows(1024, 512), line, rows(512, 2816), rows(512, 2816), rows(2816, 512)],
        out_shape=[shape((1, T, W), BF), shape((1, T, W), F32), shape((1, 512), F32)]
        + [shape(a, F32) for a in ((512, 1024), (512, TILE), (512, TILE), (1024, 512), (1, 512), (512, 2816), (512, 2816), (2816, 512))],
        compiler_params=pltpu.CompilerParams(dimension_semantics=("arbitrary",)),
    )(output, input_grad, gains, down, gate, up, out, query, kv)
    results = list(results)
    results[2], results[7] = results[2][0], results[7][0]
    return tuple(results)


def solution(mesh):
    n, m = mesh.shape["fsdp"], mesh.shape["ctx"]

    def step(*args):
        return layer_call(*args) if n == m == 4 else local(n, m, *args)

    return jax.shard_map(
        step,
        mesh=mesh,
        in_specs=(
            P("fsdp", "ctx", None),
            P("fsdp", "ctx"),
            P("fsdp", "ctx"),
            P("fsdp", "ctx", None),
            P("fsdp"),
            P("fsdp", "tp"),
            P("fsdp", "tp"),
            P("fsdp", "tp"),
            P("tp", "fsdp"),
            P("fsdp"),
            P("fsdp", "tp"),
            P("fsdp", "tp"),
            P("tp", "fsdp"),
        ),
        out_specs=(
            P("fsdp", "ctx", None),
            P("fsdp", "ctx", None),
            P("fsdp"),
            P("fsdp", "tp"),
            P("fsdp", "tp"),
            P("fsdp", "tp"),
            P("tp", "fsdp"),
            P("fsdp"),
            P("fsdp", "tp"),
            P("fsdp", "tp"),
            P("tp", "fsdp"),
        ),
        check_vma=False,
    )
```

```python
import functools
import math

import jax
import jax.numpy as jnp
from jax import lax
from jax.experimental import pallas as pl
from jax.experimental.pallas import tpu as pltpu
from jax.sharding import PartitionSpec as P

HD = 64
EPSILON = 1e-05
NEGATIVE = -1e30
BF = jnp.bfloat16
F32 = jnp.float32


def dot(a, b, ca, cb):
    return lax.dot_general(a, b, (((ca,), (cb,)), ((), ())), preferred_element_type=F32)


def angles(positions):
    half = HD // 2
    frequency = jnp.exp(jnp.arange(half, dtype=F32) * (-2.0 * math.log(10000.0) / HD))
    turned = positions.astype(F32)[:, None] * frequency[None, :]
    return jnp.cos(turned)[:, None, :], jnp.sin(turned)[:, None, :]


def rotate(values, cosine, sine):
    half = HD // 2
    a, b = values[..., :half], values[..., half:]
    return jnp.concatenate([a * cosine - b * sine, b * cosine + a * sine], axis=-1)


def gated(values, after):
    return lax.optimization_barrier((values, after))[0]


def local(n, m, inputs, positions, blocks, cotangent, attn_gain, w_query, w_key, w_value, w_out, mlp_gain, w_gate, w_up, w_down):
    f = lax.axis_index("fsdp")
    z = lax.axis_index("ctx")
    t = lax.axis_index("tp")
    tokens, width = inputs.shape[1:]
    half = width // 2
    peers = range(1, n)

    def plane(x, k):
        return x if k == 0 else lax.ppermute(x, "fsdp", [(i, i ^ k) for i in range(n)])

    def column(x, k):
        return x if k == 0 else lax.ppermute(x, "ctx", [(i, i ^ k) for i in range(m)])

    def swap(x):
        return lax.ppermute(x, "tp", [(0, 1), (1, 0)])

    def part(x, index, axis):
        size = x.shape[axis] // n
        return lax.dynamic_slice_in_dim(x, index * size, size, axis)

    def mine(x, which):
        return lax.dynamic_slice_in_dim(x, which * half, half, x.ndim - 1)

    def place(pieces, axis):
        size = pieces[0].shape[axis]
        shape = list(pieces[0].shape)
        shape[axis] = size * n
        whole = jnp.zeros(shape, pieces[0].dtype)
        for k in range(n):
            whole = lax.dynamic_update_slice_in_dim(whole, pieces[k], (f ^ k) * size, axis)
        return whole

    def join(own, other):
        return jnp.where(t == 0, jnp.concatenate([own, other], -1), jnp.concatenate([other, own], -1))

    def gather(x):
        rows = jnp.concatenate([plane(x, k) for k in range(n)], 0)
        return join(rows, swap(rows))

    def scatter(partial):
        own = mine(partial, t) + swap(mine(partial.astype(BF), 1 - t)).astype(F32)
        low = own.astype(BF)
        total = own[:tokens]
        for k in peers:
            total = total + plane(low[k * tokens : (k + 1) * tokens], k).astype(F32)
        return total

    def row_mean(own):
        own = jnp.sum(own, -1)
        return ((own + swap(own)) / width)[:, None]

    x = inputs[0].astype(F32)
    gains = jnp.stack([attn_gain, mlp_gain])
    gains = place([plane(gains, k) for k in range(n)], 1).astype(F32)
    marks = jnp.stack([positions[0], blocks[0]])
    marks = [plane(marks, k) for k in range(n)]
    place_rows = jnp.concatenate([mk[0] for mk in marks])
    query_ids = jnp.stack([mk[1] for mk in marks])
    scale_one = lax.rsqrt(jnp.mean(x * x, axis=-1, keepdims=True) + EPSILON)
    x_half = mine(x, t)
    hat_one = x_half * scale_one
    gain_one, gain_two = mine(gains[0:1], t), mine(gains[1:2], t)
    xn_one = gather((hat_one * gain_one).astype(BF))

    heads = w_query.shape[1] // HD // n
    cols = heads * HD
    kv_pair = jnp.concatenate([w_key, w_value], 1)
    kv_heads = w_key.shape[1] // HD
    w_qkv = place([plane(jnp.concatenate([part(w_query, f ^ k, 1), kv_pair], 1), k) for k in range(n)], 0)
    wo = gated(w_out, xn_one)
    wo = place([plane(part(wo, f ^ k, 0), k) for k in range(n)], 1)
    gate_up = gated((w_gate, w_up), xn_one)
    gate_up = [plane(jnp.stack([part(gate_up[0], f ^ k, 1), part(gate_up[1], f ^ k, 1)]), k) for k in range(n)]
    wg = place([g[0] for g in gate_up], 0)
    wu = place([g[1] for g in gate_up], 0)

    qkv = dot(xn_one, w_qkv, 1, 0)
    cosine, sine = angles(place_rows)
    kv_here = (heads * f) // ((w_query.shape[1] // HD) // kv_heads)

    def pick(both):
        out = both[:, :HD]
        for g in range(1, kv_heads):
            out = jnp.where(kv_here == g, both[:, g * HD : (g + 1) * HD], out)
        return out

    kw = kv_heads * HD
    query = rotate(qkv[:, :cols].reshape(-1, heads, HD), cosine, sine).astype(BF)
    key = rotate(pick(qkv[:, cols : cols + kw])[:, None, :], cosine, sine)[:, 0, :].astype(BF)
    value = pick(qkv[:, cols + kw :]).astype(BF)
    key_value = jnp.concatenate([key, value], 1).reshape(n, tokens, 2 * HD)
    kv_all = jnp.concatenate([column(key_value, k) for k in range(m)], 1)
    ids_all = jnp.concatenate([column(query_ids, k) for k in range(m)], 1)
    keys, values = kv_all[..., :HD], kv_all[..., HD:]
    factor = 1.0 / math.sqrt(HD)
    query = query.reshape(n, tokens, heads, HD)
    allowed = (ids_all[:, None, :] <= query_ids[:, :, None])[:, None]
    scores = jnp.einsum("nthd,nsd->nhts", query, keys, preferred_element_type=F32) * factor
    scores = jnp.where(allowed, scores, NEGATIVE)
    top = jnp.max(scores, -1, keepdims=True)
    raw = jnp.where(allowed, jnp.exp(scores - top), 0.0)
    weights = raw / jnp.sum(raw, -1, keepdims=True)
    weights_low = weights.astype(BF)
    attended = jnp.einsum("nhts,nsd->nthd", weights_low, values, preferred_element_type=F32)
    attended_low = attended.astype(BF).reshape(n * tokens, cols)

    hidden = x_half + scatter(dot(attended_low, wo, 1, 0))
    scale_two = lax.rsqrt(row_mean(hidden * hidden) + EPSILON)
    hat_two = hidden * scale_two
    xn_two = gather((hat_two * gain_two).astype(BF))
    cot = gather(gated(mine(cotangent[0], t), wg))
    wd = gated(w_down, wg)
    wd = place([plane(part(wd, f ^ k, 0), k) for k in range(n)], 1)
    gate = dot(xn_two, wg, 1, 0)
    up = dot(xn_two, wu, 1, 0)
    sigma = jax.nn.sigmoid(gate)
    silu = gate * sigma
    act = (silu * up).astype(BF)
    dact = dot(cot, wd, 1, 1)
    dgate = (dact * up * sigma * (1.0 + gate * (1.0 - sigma))).astype(BF)
    dup = (dact * silu).astype(BF)

    def reduce(piece):
        if m != 4:
            return lax.psum(piece, "ctx")
        one = (piece.astype(F32) + lax.ppermute(piece, "ctx", [(0, 1), (3, 2)]).astype(F32)).astype(BF)
        two = (one.astype(F32) + lax.ppermute(one, "ctx", [(1, 2), (2, 1)]).astype(F32)).astype(BF)
        three = lax.ppermute(two, "ctx", [(1, 0), (2, 3)])
        return jnp.where((z == 0) | (z == 3), three, two)

    def share(grad, axis):
        low = grad.astype(BF)
        return [plane(part(low, f ^ k, axis), k) for k in range(n)]

    down_parts = [reduce(p) for p in share(dot(act, cot, 0, 0), 1)]
    gate_parts = [reduce(p) for p in share(dot(xn_two, dgate, 0, 0), 0)]
    up_parts = [reduce(p) for p in share(dot(xn_two, dup, 0, 0), 0)]
    d_two = scatter(dot(dgate, wg, 1, 1) + dot(dup, wu, 1, 1))
    out_half = (hidden + scatter(dot(act, wd, 1, 0))).astype(BF)
    output = join(out_half, swap(out_half))
    gain_two_grad = jnp.sum(d_two * hat_two, 0)
    e_two = d_two * gain_two
    d_hidden = mine(cotangent[0], t).astype(F32) + scale_two * (e_two - hat_two * row_mean(e_two * hat_two))
    dhb = gather(d_hidden.astype(BF))
    out_parts = [reduce(p) for p in share(dot(attended_low, dhb, 0, 0), 1)]

    d_att = dot(dhb, wo, 1, 1).astype(BF).reshape(n, tokens, heads, HD)
    delta = jnp.einsum("nthd,nthd->nht", d_att.astype(F32), attended)
    d_weights = jnp.einsum("nthd,nsd->nhts", d_att, values, preferred_element_type=F32)
    d_scores = (weights * (d_weights - delta[..., None])).astype(BF)
    dv = jnp.einsum("nhts,nthd->nsd", weights_low, d_att, preferred_element_type=F32)
    dk = jnp.einsum("nhts,nthd->nsd", d_scores, query, preferred_element_type=F32) * factor
    dq = jnp.einsum("nhts,nsd->nthd", d_scores, keys, preferred_element_type=F32) * factor
    d_kv = jnp.concatenate([dk, dv], -1).reshape(n, m, tokens, 2 * HD)
    d_low = d_kv.astype(BF)
    d_kv_own = d_kv[:, 0]
    for k in range(1, m):
        d_kv_own = d_kv_own + column(d_low[:, k], k).astype(F32)
    d_kv_own = d_kv_own.reshape(n * tokens, 2 * HD)
    dq = rotate(dq.reshape(n * tokens, heads, HD), cosine, -sine).reshape(n * tokens, cols)
    dk = rotate(d_kv_own[:, None, :HD], cosine, -sine)[:, 0, :]
    d_qkv = jnp.concatenate([dq, dk, d_kv_own[:, HD:]], 1).astype(BF)
    w_here = jnp.concatenate([w_qkv[:, :cols], pick(w_qkv[:, cols : cols + kw]), pick(w_qkv[:, cols + kw :])], 1)
    d_one = scatter(dot(d_qkv, w_here, 1, 1))
    qkv_parts = share(dot(xn_one, d_qkv, 0, 0), 0)
    key_parts, value_parts = [0.0] * kv_heads, [0.0] * kv_heads
    for k in range(n):
        owner = (heads * (f ^ k)) // ((w_query.shape[1] // HD) // kv_heads)
        piece = qkv_parts[k].astype(F32)
        for g in range(kv_heads):
            key_parts[g] = key_parts[g] + jnp.where(owner == g, piece[:, cols : cols + HD], 0.0)
            value_parts[g] = value_parts[g] + jnp.where(owner == g, piece[:, cols + HD :], 0.0)
    small = reduce(jnp.concatenate(key_parts + value_parts, 1).astype(BF)).astype(F32)
    query_parts = [reduce(p[:, :cols]) for p in qkv_parts]
    gain_one_grad = jnp.sum(d_one * hat_one, 0)
    e_one = d_one * gain_one
    in_half = d_hidden + scale_one * (e_one - hat_one * row_mean(e_one * hat_one))
    input_grad = join(in_half, swap(in_half))
    gain_grads = jnp.stack([gain_one_grad, gain_two_grad])
    nothing = jnp.zeros_like(gain_grads)
    gain_grads = jnp.where(t == 0, jnp.concatenate([gain_grads, nothing], 1), jnp.concatenate([nothing, gain_grads], 1))
    gain_grads = part(lax.psum(gain_grads, ("fsdp", "ctx", "tp")), f, 1)

    def settle(pieces, axis):
        return place(pieces, axis).astype(F32)

    return (
        output[None],
        input_grad[None],
        gain_grads[0],
        settle(query_parts, 1),
        small[:, :kw],
        small[:, kw:],
        settle(out_parts, 0),
        gain_grads[1],
        settle(gate_parts, 1),
        settle(up_parts, 1),
        settle(down_parts, 0),
    )


T, W, H, TILE = 256, 2048, 1024, 128
MAIN, WIN = 640, 768
GRADS = (("d", 2816, 512), ("g", 512, 2816), ("u", 512, 2816), ("o", 1024, 512), ("q", 512, 1024), ("k", 512, 256))
PART = 384


PARTS = {"dA": (0, 128), "dB": (128, 256), "dC": (PART, PART)}
PARTS |= {name + which: (0 if which == "A" else PART, PART) for name in "gu" for which in "AB"}
LAST = ("dC", "gB", "uB")
GROUPS = tuple(PARTS) + ("o", "q", "k")


def chunk_list():
    chunks = []
    for group, (_, size) in PARTS.items():
        for j in range(4):
            part = MAIN - PART if group in LAST and j % 2 else size
            chunks.append((group, group[0], j, j) + ((part, 512) if group[0] == "d" else (512, part)))
    chunks += [("o", "o", r, 0, 256, 512) for r in range(0, 1024, 256)]
    chunks += [("q", "q", 0, c, 512, 256) for c in range(0, 1024, 256)]
    return chunks + [("k", "k", r, 0, 256, 256) for r in (0, 256)]


CHUNKS = chunk_list()
DEPTH = 4
ORDER = (
    "dA", "+", "feed_back", 1, 1, 1, "dB", 1, "gate_A", 1, 1, "d2_first", 1, "d2_own", "dC", 1, "relay", 1, "gate_B", "gA", 1, 1, 1,
    "norm_two_back", 1, "gB", "up_A", 1, 1, "dh_take", "+", "out_grads", 1, "attend0", 1, "attend1", 1, "uA", "+", "up_B", 1, "attend2", 1,
    "attend3", "pair_send", 1, "-", "pair_sum", "uB", "+", 1, "o", "d_kv_take", 1, "qkv_grads", 1, "d1_first", 1, "d1_own", 1, "q", 1, "relay", 1,
    "kv_ready", 1, 1, "norm_one_back", 1, "out_first", 1, "out_own", 1, "relay", 1, "-", "gains_column", "-", "out_end", "gains_end",
)
MESH = pl.DeviceIdType.MESH


def nn(a, b):
    return lax.dot_general(a, b, (((1,), (0,)), ((), ())), preferred_element_type=F32)


def nt(a, b):
    return lax.dot_general(a, b, (((1,), (1,)), ((), ())), preferred_element_type=F32)


def tn(a, b):
    return lax.dot_general(a, b, (((0,), (0,)), ((), ())), preferred_element_type=F32)


def flip(a, k):
    return (a % 2 + k % 2) % 2 + 2 * ((a // 2 + k // 2) % 2)


def layer_kernel(*refs):
    names = iter(refs)

    def take(count):
        return [next(names) for _ in range(count)]

    x_in, place_in, block_in, gain_in_one, gain_in_two, cot_in, wq, wk, wv, wo, wg, wu, wd = take(13)
    out_ref, in_grad_ref, gain_ref = take(3)
    first, left, cross, total = ({name: next(names) for name, _, _ in GRADS} for _ in range(4))
    (x1, x2, ct, dh, w_qkv, w_o, w_g, w_u, w_d, act, dg, du, q_buf, kv_all, ob) = take(15)
    (ps, pr, rr, rd, yo, hid, d_hid, xv, tb, ga, ids, r1s, r2s, ss_own, ss_other, lse, bias) = take(17)
    (gs_d, line, waves, d_kv, d_kv_recv, out_s, g_sum, g_plane, g_column, g_whole) = take(10)
    send_sem, recv_sem, local_sem, credit = take(4)
    f, z, t = lax.axis_index("fsdp"), lax.axis_index("ctx"), lax.axis_index("tp")
    sems = iter(range(10**6))
    drains = []

    def al(v, by):
        return pl.multiple_of(v, by)

    def plane(k):
        return (flip(f, k), z, t)

    def column(k):
        return (f, flip(z, k), t)

    core = (f, z, 1 - t)
    rows_f = pl.ds(al(f * T, T), T)
    half = pl.ds(al(t * H, H), H)
    rest = pl.ds(al((1 - t) * H, H), H)

    def rows_of(b):
        return pl.ds(al(b * T, T), T)

    def remote(src, dst, s, device):
        return pltpu.make_async_remote_copy(src_ref=src, dst_ref=dst, send_sem=send_sem.at[s], recv_sem=recv_sem.at[s], device_id=device, device_id_type=MESH)

    def here(src, dst, s):
        return pltpu.make_async_copy(src, dst, local_sem.at[s])

    local_count = iter(range(10**6))

    lx = here(x_in.at[0], xv, next(local_count))
    lx.start()
    lc = here(cot_in.at[0], ct.at[rows_f, :], next(local_count))
    lc.start()
    lh = here(cot_in.at[0, :, half], out_s, next(local_count))
    lh.start()
    own_gain = ga.at[:, pl.ds(al(f * 512, 512), 512)]
    own_gain[0:1, :] = gain_in_one[...].astype(F32).reshape(1, 512)
    own_gain[1:2, :] = gain_in_two[...].astype(F32).reshape(1, 512)
    tb[f, 0:1, :] = place_in[...].astype(F32)
    tb[f, 1:2, :] = block_in[...].astype(F32)

    def starts(r):
        return (11 * r + 1 - t) // 2

    def full(r):
        return (r + t) % 2 == 0

    def weight_moves(k, taking):
        r = flip(f, k)
        sender, taker = (r, f) if taking else (f, r)
        rows = pl.ds(al(sender * 512, 512), 512)
        row_part = pl.ds(al(sender * 512 + z * TILE, TILE), TILE)
        own_part = pl.ds(al(z * TILE, TILE), TILE)
        begin = al(starts(taker) * TILE, TILE)
        tail = al(begin + MAIN, TILE)
        col = al(taker * T, T)
        moves = {
            "o": [(wo.at[pl.ds(col, T), :], w_o.at[:, rows])],
            "g": [(wg.at[:, pl.ds(begin, MAIN)], w_g.at[rows, pl.ds(0, MAIN)])],
            "g+": [(wg.at[:, pl.ds(tail, TILE)], w_g.at[rows, pl.ds(MAIN, TILE)])],
        }
        from_rows, to_rows = pl.ds(0, 512), rows
        if k:
            from_rows, to_rows = pl.ds(al(z % 2 * T, T), T), pl.ds(al(sender * 512 + z % 2 * T, T), T)
        moves["qkv"] = [
            (wq.at[from_rows, pl.ds(col, T)], w_qkv.at[to_rows, pl.ds(0, T)]),
            (wk.at[from_rows, :], w_qkv.at[to_rows, pl.ds(T, TILE)]),
            (wv.at[from_rows, :], w_qkv.at[to_rows, pl.ds(T + TILE, TILE)]),
        ]
        if k == 0:
            moves["u"] = [(wu.at[:, pl.ds(begin, MAIN)], w_u.at[rows, pl.ds(0, MAIN)])]
            moves["u+"] = [(wu.at[:, pl.ds(tail, TILE)], w_u.at[rows, pl.ds(MAIN, TILE)])]
            moves["d"] = [(wd.at[pl.ds(begin, MAIN), :], w_d.at[pl.ds(0, MAIN), rows])]
            moves["d+"] = [(wd.at[pl.ds(tail, TILE), :], w_d.at[pl.ds(MAIN, TILE), rows])]
        else:
            moves["u"] = [(wu.at[own_part, pl.ds(begin, MAIN)], w_u.at[row_part, pl.ds(0, MAIN)])]
            moves["u+"] = [(wu.at[own_part, pl.ds(tail, TILE)], w_u.at[row_part, pl.ds(MAIN, TILE)])]
            moves["d"] = [(wd.at[pl.ds(begin, MAIN), own_part], w_d.at[pl.ds(0, MAIN), row_part])]
            moves["d+"] = [(wd.at[pl.ds(tail, TILE), own_part], w_d.at[pl.ds(MAIN, TILE), row_part])]
        return moves

    w_counts = (("qkv", 3), ("o", 1), ("g", 1), ("g+", 1), ("u", 1), ("u+", 1), ("d", 1), ("d+", 1))
    w_sem = {(key, k, i): next(sems) for key, c in w_counts for k in (1, 2, 3) for i in range(c)}
    w_local = {(key, i): next(local_count) for key, c in w_counts for i in range(c)}

    def weights_each(key, taking, run):
        for k in (1, 2, 3):
            moves = weight_moves(k, taking)
            for i, (src, dst) in enumerate(moves[key]):
                run(remote(src, dst, w_sem[key, k, i], plane(k)))
            if key + "+" in moves:

                @pl.when(full(f if taking else flip(f, k)))
                def _():
                    (src, dst), = moves[key + "+"]
                    run(remote(src, dst, w_sem[key + "+", k, 0], plane(k)))

    def weights_start(key):
        weights_each(key, False, lambda cp: cp.start())

    def weights_wait(key):
        weights_each(key, True, lambda cp: cp.wait_recv())

    def weights_drain():
        for key in ("qkv", "o", "g", "u", "d"):
            weights_each(key, False, lambda cp: cp.wait_send())

    def weights_own(keys, wait):
        moves = weight_moves(0, False)

        def run(key):
            for i, (src, dst) in enumerate(moves[key]):
                cp = here(src, dst, w_local[key, i])
                cp.wait() if wait else cp.start()

        for key in keys:
            run(key)
            if key + "+" in moves:
                pl.when(full(f))(functools.partial(run, key + "+"))

    y_sem = {(key, k, j): next(sems) for key in ("qkv", "u", "d") for k in (1, 2, 3) for j in (1, 2, 3) if key != "qkv" or j == 1}

    def column_each(key, taking, run):
        for k in (1, 2, 3):
            for j in (1, 2, 3):
                from_z = flip(z, j) if taking else z
                part = pl.ds(al(flip(f, k) * 512 + from_z * TILE, TILE), TILE)

                def move(size):
                    ref = w_u.at[part, pl.ds(0, size)] if key == "u" else w_d.at[pl.ds(0, size), part]
                    run(remote(ref, ref, y_sem[key, k, j], column(j)))

                if key == "qkv":
                    if j == 1:
                        ref = w_qkv.at[pl.ds(al(flip(f, k) * 512 + from_z % 2 * T, T), T), :]
                        run(remote(ref, ref, y_sem[key, k, j], column(j)))
                    continue
                pl.when(full(f))(functools.partial(move, WIN))
                pl.when(full(f + 1))(functools.partial(move, MAIN))

    g_sem = [[next(sems) for _ in range(4)] for _ in range(4)]
    f_sem = [[next(sems) for _ in range(4)] for _ in range(4)]
    quarters = (pl.ds(al(t * H, 512), 512), pl.ds(al(t * H + 512, 512), 512))

    def gather_direct(g):
        return (1, 2, 3) if g == 3 else (1, 2)

    def gather_start(g, buf, with_own, src=None):
        block = buf.at[rows_f, half]
        for k in gather_direct(g):
            remote(block if src is None else src, block, g_sem[g][k - 1], plane(k)).start()
        if with_own:
            remote(block, block, f_sem[g][3], core).start()

    def gather_hand(g, buf, k):
        block = buf.at[rows_of(flip(f, k)), half]
        return remote(block, block, f_sem[g][k - 1], core)

    def gather_relay(g, buf, k):
        part = buf.at[rows_of(flip(f, k)), quarters[k - 1]]
        return remote(part, part, g_sem[g][4 - k], plane(3 - k))

    def gather_forward(g, buf):
        for k in gather_direct(g):
            block = buf.at[rows_of(flip(f, k)), half]
            remote(block, block, g_sem[g][k - 1], plane(k)).wait_recv()
            if g != 3:
                gather_relay(g, buf, k).start()
            gather_hand(g, buf, k).start()

    def gather_diagonal(g, buf):
        for k in (1, 2):
            part = buf.at[rows_of(flip(f, 3)), quarters[k - 1]]
            remote(part, part, g_sem[g][4 - k], plane(3 - k)).wait_recv()
        gather_hand(g, buf, 3).start()

    def gather_take(g, buf, k):
        if k == 0:
            block = buf.at[rows_f, rest]
            remote(block, block, f_sem[g][3], core).wait_recv()
        else:
            block = buf.at[rows_of(flip(f, k)), rest]
            remote(block, block, f_sem[g][k - 1], core).wait_recv()

    def gather_drain(g, buf, with_own, src=None):
        block = buf.at[rows_f, half]
        for k in gather_direct(g):
            remote(block if src is None else src, block, g_sem[g][k - 1], plane(k)).wait_send()
        for k in (1, 2, 3):
            gather_hand(g, buf, k).wait_send()
            if g != 3 and k != 3:
                gather_relay(g, buf, k).wait_send()
        if with_own:
            remote(block, block, f_sem[g][3], core).wait_send()

    t_sem = [next(sems) for _ in range(3)]
    a_sem = [next(sems) for _ in range(3)]
    barrier = pltpu.get_barrier_semaphore()
    for k in (1, 2, 3):
        pl.semaphore_signal(barrier, inc=1, device_id=plane(k), device_id_type=MESH)
        pl.semaphore_signal(barrier, inc=1, device_id=column(k), device_id_type=MESH)
    pl.semaphore_signal(barrier, inc=1, device_id=core, device_id_type=MESH)
    pl.semaphore_wait(barrier, 7)

    for k in (1, 2, 3):
        remote(own_gain, own_gain, a_sem[k - 1], plane(k)).start()
        remote(tb.at[f], tb.at[f], t_sem[k - 1], plane(k)).start()
    weights_start("qkv")
    weights_own(("qkv",), False)

    @pl.when(full(f + 1))
    def _():
        w_g[:, MAIN:WIN] = jnp.zeros((W, TILE), BF)
        w_u[:, MAIN:WIN] = jnp.zeros((W, TILE), BF)
        w_d[MAIN:WIN, :] = jnp.zeros((TILE, W), BF)

    lx.wait()
    for k in (1, 2, 3):
        dst = ga.at[:, pl.ds(al(flip(f, k) * 512, 512), 512)]
        remote(dst, dst, a_sem[k - 1], plane(k)).wait_recv()

    STEP = 32

    def sub(i):
        return pl.ds(al(i * STEP, STEP), STEP)

    @pl.loop(0, T // STEP)
    def _(i):
        xs = xv[sub(i), :].astype(F32)
        scale = lax.rsqrt(jnp.mean(xs * xs, axis=-1, keepdims=True) + EPSILON)
        r1s[sub(i), :] = jnp.broadcast_to(scale, (STEP, TILE))
        x1[pl.ds(al(f * T + i * STEP, STEP), STEP), :] = (xs * scale * ga[0:1, :]).astype(BF)

    weights_wait("qkv")
    column_each("qkv", False, lambda cp: cp.start())
    gather_start(0, x1, False)
    gather_forward(0, x1)
    for key in "oudg":
        weights_start(key)
    weights_own("oudg", False)
    gather_diagonal(0, x1)
    for k in (1, 2, 3):
        dst = tb.at[flip(f, k)]
        remote(dst, dst, t_sem[k - 1], plane(k)).wait_recv()
    weights_own(("qkv",), True)
    column_each("qkv", True, lambda cp: cp.wait_recv())

    lane = lax.broadcasted_iota(jnp.int32, (T, TILE), 1)
    low_lane = lane < HD
    first_half = lane % HD < HD // 2
    kv_head = f // 2

    def make_turns(b):
        exponent = lax.broadcasted_iota(jnp.int32, (HD // 2, T), 0).astype(F32) * (-2.0 * math.log(10000.0) / HD)
        turned = jnp.exp(exponent) * tb[b, 0:1, :]
        cosine, sine = jnp.cos(turned), jnp.sin(turned)
        waves[b, 0, :, :] = jnp.transpose(jnp.concatenate([cosine] * 4, 0))
        waves[b, 1, :, :] = jnp.transpose(jnp.concatenate([-sine, sine, -sine, sine], 0))

    def turns(b):
        return waves[b, 0, :, :], waves[b, 1, :, :]

    def turn(v, c, s):
        swapped = jnp.where(first_half, pltpu.roll(v, TILE - 32, 1), pltpu.roll(v, 32, 1))
        return v * c + swapped * s

    def qkv_block(k):
        b = flip(f, k)
        qkv = nn(x1[rows_of(b), :], w_qkv[...])
        make_turns(b)
        c, s = turns(b)
        for i in range(2):
            q = turn(qkv[:, i * TILE : (i + 1) * TILE], c, s) * 0.125
            q_buf[rows_of(b), i * TILE : (i + 1) * TILE] = q.astype(BF)
        key = turn(qkv[:, 2 * TILE : 3 * TILE], c, s)
        value = qkv[:, 3 * TILE :]
        key = jnp.where(kv_head == 0, key, pltpu.roll(key, HD, 1))
        value = jnp.where(kv_head == 1, value, pltpu.roll(value, HD, 1))
        kv_all[z, b, :, :] = jnp.where(low_lane, key, value).astype(BF)
        ids[z, pl.ds(b, 1), :] = tb[b, 1:2, :]

    qkv_block(0)
    for k in (1, 2, 3):
        gather_take(0, x1, k)

    @pl.loop(1, 4)
    def _(k):
        qkv_block(k)

    z_sem = [[next(sems) for _ in range(2)] for _ in range(3)]
    for k in (1, 2, 3):
        remote(kv_all.at[z], kv_all.at[z], z_sem[k - 1][0], column(k)).start()
        remote(ids.at[z], ids.at[z], z_sem[k - 1][1], column(k)).start()
    for k in (1, 2, 3):
        zz = flip(z, k)
        remote(kv_all.at[zz], kv_all.at[zz], z_sem[k - 1][0], column(k)).wait_recv()
        remote(ids.at[zz], ids.at[zz], z_sem[k - 1][1], column(k)).wait_recv()
    lc.wait()
    weights_wait("u")
    column_each("u", False, lambda cp: cp.start())

    low_keys = lax.broadcasted_iota(jnp.int32, (4 * T, TILE), 1) < HD

    def bias_of(s):
        query_id = ids[z, pl.ds(s, 1), :]
        for j in range(4):
            key_id = jnp.transpose(jnp.broadcast_to(ids[j, pl.ds(s, 1), :], (8, T)))[:, 0:1]
            bias[j * T : (j + 1) * T, :] = jnp.where(key_id <= query_id, 0.0, NEGATIVE).astype(BF)

    def kv_of(s):
        kv = jnp.concatenate([kv_all[j, s, :, :] for j in range(4)], 0).astype(F32)
        turned = pltpu.roll(kv, HD, 1)
        keys = jnp.where(low_keys, kv, turned).astype(BF)
        values = jnp.where(low_keys, turned, kv).astype(BF)
        return kv, keys, values

    def only(v, parity):
        return jnp.where(low_lane if parity == 0 else ~low_lane, v.astype(F32), 0.0).astype(BF)

    @pl.loop(0, 4)
    def _(s):
        bias_of(s)
        kv, keys, _ = kv_of(s)
        values_t = jnp.transpose(kv)[HD:, :].astype(BF)

        for i in range(2):
            mixed = []
            for parity in range(2):
                q = only(q_buf[rows_of(s), i * TILE : (i + 1) * TILE], parity)
                scores = nt(keys, q) + bias[...].astype(F32)
                top = jnp.max(scores, axis=0, keepdims=True)
                raw = jnp.exp(scores - top)
                norm = jnp.sum(raw, axis=0, keepdims=True)
                lse[s, 2 * i + parity : 2 * i + parity + 1, :] = top + jnp.log(norm)
                mixed.append(nn(values_t, raw.astype(BF)) * (1.0 / norm))
            ob[rows_of(s), i * TILE : (i + 1) * TILE] = jnp.transpose(jnp.concatenate(mixed, 0)).astype(BF)

    p_sem = [next(sems) for _ in range(4)][0]
    s_sem = [next(sems) for _ in range(6)]
    COLS = 256
    lows, highs = pl.ds(0, 512), pl.ds(512, 512)

    def pass_first(k):
        return remote(ps.at[3, :, (lows, highs)[k - 1]], rd.at[k - 1], s_sem[k - 1], plane(k))

    def pass_second(k, added):
        cols = (lows, highs)[k - 1 if not added else 2 - k]
        return remote(ps.at[k, :, cols], rr.at[k - 1, :, cols], s_sem[2 * k + added], plane(k))

    def tiles(run):
        @pl.loop(0, H // COLS)
        def _(j):
            run(pl.ds(al(j * COLS, COLS), COLS), j * COLS)

    def core_move(k):
        return remote(ps.at[k], pr.at[k], p_sem + k, core)

    def scatter_first(product):
        @pl.loop(0, 4)
        def _(i):
            k = (7 - i) % 4

            def run(cols, c):
                ps[k, :, cols] = product(flip(f, k), (1 - t) * H + c).astype(BF)

            tiles(run)
            core_move(k).start()

    def scatter_own(product):
        @pl.loop(0, 3)
        def _(i):
            k = (i + 2) % 3 + 1
            core_move(k).wait()

            def run(cols, c):
                ps[k, :, cols] = (product(flip(f, k), t * H + c) + pr[k, :, cols].astype(F32)).astype(BF)

            tiles(run)

            @pl.when(k == 3)
            def _():
                pass_first(1).start()
                pass_first(2).start()

        pass_second(1, 0).start()
        pass_second(2, 0).start()
        core_move(0).wait()

        def run(cols, c):
            yo[:, cols] = product(f, t * H + c) + pr[0, :, cols].astype(F32)

        tiles(run)

    def scatter_steps(product):
        return functools.partial(scatter_first, product), functools.partial(scatter_own, product)

    def scatter_relay():
        for k in (1, 2):
            pass_first(3 - k).wait()
            c = (512, 0)[k - 1]

            @pl.loop(0, T // STEP)
            def _(i):
                ps[k, sub(i), c : c + 512] = (ps[k, sub(i), c : c + 512].astype(F32) + rd[2 - k, sub(i), :].astype(F32)).astype(BF)

            pass_second(k, 1).start()

    def scatter_wait():
        for k in (1, 2):
            for added in (0, 1):
                pass_second(k, added).wait()

    def scattered(i):
        return yo[sub(i), :] + rr[0, sub(i), :].astype(F32) + rr[1, sub(i), :].astype(F32)

    n_sem = [next(sems) for _ in range(3)]

    def core_sums(u):
        remote(ss_own.at[u], ss_other.at[u], n_sem[u], core).start()
        remote(ss_own.at[u], ss_other.at[u], n_sem[u], core).wait()

    weights_wait("o")
    weights_own("o", True)
    for step in scatter_steps(lambda b, c: nn(ob[rows_of(b), :], w_o[:, pl.ds(al(c, COLS), COLS)])):
        step()
    scatter_relay()
    scatter_wait()
    weights_wait("d")
    column_each("d", False, lambda cp: cp.start())

    @pl.loop(0, T // STEP)
    def _(i):
        rows = xv[sub(i), half].astype(F32) + scattered(i)
        hid[sub(i), :] = rows
        ss_own[0, sub(i), :] = jnp.broadcast_to(jnp.sum(rows * rows, axis=-1, keepdims=True), (STEP, TILE))

    core_sums(0)
    gain_one, gain_two = ga[0:1, half], ga[1:2, half]

    @pl.loop(0, T // STEP)
    def _(i):
        scale = lax.rsqrt((ss_own[0, sub(i), 0:1] + ss_other[0, sub(i), 0:1]) * (1.0 / W) + EPSILON)
        r2s[sub(i), :] = jnp.broadcast_to(scale, (STEP, TILE))
        x2[pl.ds(al(f * T + i * STEP, STEP), STEP), half] = (hid[sub(i), :] * scale * gain_two).astype(BF)

    gather_start(2, x2, True)
    gather_forward(2, x2)
    gather_start(1, ct, False, cot_in.at[0, :, half])
    weights_wait("g")
    weights_own("ugd", True)
    column_each("u", True, lambda cp: cp.wait_recv())

    UNITS = 256

    def feed_block(k):
        b = flip(f, k)

        @pl.loop(0, WIN // UNITS)
        def _(j):
            cols = pl.ds(al(j * UNITS, UNITS), UNITS)
            gate = nn(x2[rows_of(b), :], w_g[:, cols])
            up = nn(x2[rows_of(b), :], w_u[:, cols])
            sigma = jax.nn.sigmoid(gate)
            silu = gate * sigma
            act[rows_of(b), cols] = (silu * up).astype(BF)
            dg[rows_of(b), cols] = (up * sigma * (1.0 + gate * (1.0 - sigma))).astype(BF)
            du[rows_of(b), cols] = silu.astype(BF)

    for k in (0, 1, 2):
        gather_take(2, x2, k)

    @pl.loop(0, 3)
    def _(k):
        feed_block(k)

    gather_diagonal(2, x2)
    gather_take(2, x2, 3)
    feed_block(3)
    gather_forward(1, ct)
    gather_diagonal(1, ct)
    for k in (1, 2, 3):
        gather_take(1, ct, k)

    e_sem = {(name, i): [next(sems) for _ in range(3)][0] for name in GROUPS for i in range(2 if name in LAST else 1)}
    e_local = {(name, i): next(local_count) for name in GROUPS for i in range(2 if name in LAST else 1)}

    def kv_place(k):
        return w_u.at[pl.ds(al((k - 1) * 512, 512), 512), pl.ds(0, T)]

    def stage(name, k):
        if name == "d":
            return gs_d.at[pl.ds(al(k * WIN, WIN), WIN), :]
        if name in "gu":
            return ct.at[pl.ds(al((k // 2) * 512, 512), 512), pl.ds(al((k % 2) * H, H), WIN)]
        if name == "o":
            return gs_d.at[pl.ds(al(k * WIN, WIN), T), :]
        return x2.at[pl.ds(al((k // 2) * 512, 512), 512), pl.ds(al((k % 2) * 512 + (0 if name == "q" else T), T), T)]

    def grad_moves(group, k, sender):
        name = group[0]
        buf, begin = stage(name, k), al(starts(sender) * TILE, TILE)
        if name in "dgu":
            parts = [(PART, MAIN - PART), (MAIN, TILE)] if group in LAST else [PARTS[group]]
            if name == "d":
                return [(buf.at[pl.ds(c, size), :], first["d"].at[pl.ds(al(begin + c, TILE), size), :]) for c, size in parts]
            return [(buf.at[:, pl.ds(c, size)], first[name].at[:, pl.ds(al(begin + c, TILE), size)]) for c, size in parts]
        if name == "o":
            return [(buf, first["o"].at[rows_of(sender), :])]
        if name == "q":
            return [(buf, first["q"].at[:, rows_of(sender)])]
        return [(buf, kv_place(k))]

    def grad_send(group, k, act_on):
        for i, (src, dst) in enumerate(grad_moves(group, k, f)):

            def run(i=i, src=src, dst=dst):
                if isinstance(k, int) and k == 0:
                    cp = here(src, dst, e_local[group, i])
                    cp.wait() if act_on == "wait" else cp.start()
                else:
                    cp = remote(src, dst, e_sem[group, i] + k - 1, plane(k))
                    cp.wait_send() if act_on == "wait" else cp.start()

            if i == 0:
                run()
            else:
                pl.when(full(f))(run)

    def grad_take(group):
        for k in (1, 2, 3):
            sender = flip(f, k)
            for i, (src, dst) in enumerate(grad_moves(group, k, sender)):

                def run(i=i, src=src, dst=dst):
                    remote(src, dst, e_sem[group, i] + k - 1, plane(k)).wait_recv()

                if i == 0:
                    run()
                else:
                    pl.when(full(sender))(run)

    def sent(*groups):
        for group in groups:
            for k in (1, 2, 3):
                grad_send(group, k, "wait")

    def block_cols(k):
        return pl.ds(al(flip(f, k) * 512, 512), 512)

    def each_owner(product, *groups):
        @pl.loop(0, 4)
        def _(i):
            k = (i + 1) % 4
            product(k)

            @pl.when(k != 0)
            def _():
                for group in groups:
                    grad_send(group, k, "start")

            @pl.when(k == 0)
            def _():
                for group in groups:
                    if group != "k":
                        grad_send(group, 0, "start")

    def down_grads(group):
        c, size = PARTS[group]

        def product(k):
            stage("d", k)[c : c + size, :] = tn(act[:, c : c + size], ct[:, block_cols(k)]).astype(BF)

        each_owner(product, group)

    def feed_grads(name, which, right):
        c = 0 if which == "A" else PART

        def product(k):
            @pl.loop(0, 2)
            def _(i):
                xs = x2[:, pl.ds(al(flip(f, k) * 512 + i * T, T), T)]
                stage(name, k)[pl.ds(al(i * T, T), T), c : c + PART] = tn(xs, right[:, c : c + PART]).astype(BF)

        each_owner(product, name + which)

    for group in ("dA", "dB", "dC"):
        down_grads(group)

    def feed_back():
        column_each("d", True, lambda cp: cp.wait_recv())

        @pl.loop(0, 4)
        def _(b):
            @pl.loop(0, WIN // UNITS)
            def _(j):
                cols = pl.ds(al(j * UNITS, UNITS), UNITS)
                back = nt(ct[rows_of(b), :], w_d[cols, :])
                dg[rows_of(b), cols] = (back * dg[rows_of(b), cols].astype(F32)).astype(BF)
                du[rows_of(b), cols] = (back * du[rows_of(b), cols].astype(F32)).astype(BF)

    def gate_A():
        gather_drain(1, ct, False, cot_in.at[0, :, half])
        feed_grads("g", "A", dg)

    d2_first, d2_own = scatter_steps(
        lambda b, c: nt(dg[rows_of(b), :], w_g[pl.ds(al(c, COLS), COLS), :]) + nt(du[rows_of(b), :], w_u[pl.ds(al(c, COLS), COLS), :])
    )

    end = (z == 0) | (z == 3)
    middle = (z == 1) | (z == 2)
    next_in = (f, jnp.where(z < 2, 1, 2), t)
    next_out = (f, jnp.where(z < 2, 0, 3), t)
    facing = (f, 3 - z, t)
    across = [next(sems) for _ in range(2 * DEPTH)]
    l_sem = [[next(sems), across[i % (2 * DEPTH)], next(sems)] for i in range(len(CHUNKS))]
    v_sem = [next(local_count) for _ in range(2)]
    o_sem = [next(local_count) for _ in range(4)]

    la, lb, *rest_of_line = (line.at[i] for i in range(8))
    tt, ring = rest_of_line[:2], rest_of_line[2:]

    kept, given = (w_g.at[:, pl.ds(512 + j * TILE, TILE)] for j in range(2))
    even = f % 2 == 0

    def pair_rows(pair, j):
        return pl.ds(j * 512 + pair * T, T)


    def window(arrays, i):
        group, name, r, c, rows, cols = CHUNKS[i]
        if name in "dgu":
            j = flip(r, t) if group in LAST else r
            at = al(starts(j) * TILE + PARTS[group][0], TILE)
            r, c = (at, 0) if name == "d" else (0, at)
        return arrays[name].at[pl.ds(r, rows), pl.ds(c, cols)]

    def line_send(group):
        @pl.when(end)
        def _():
            for i, chunk in enumerate(CHUNKS):
                if chunk[0] == group:
                    remote(window(first, i), window(left, i), l_sem[i][0], next_in).start()

    def add_into(dst, a, b, rows, cols):
        @pl.loop(0, rows // STEP)
        def _(i):
            at = sub(i)
            dst[at, pl.ds(0, cols)] = (a[at, pl.ds(0, cols)].astype(F32) + b[at, pl.ds(0, cols)].astype(F32)).astype(BF)

    def line_one(i):
        _, name, r, c, rows, cols = CHUNKS[i]
        part = (pl.ds(0, rows), pl.ds(0, cols))
        a, b, keep = la.at[part], lb.at[part], ring[i % DEPTH]

        @pl.when(middle)
        def _():
            get_a = here(window(first, i), a, v_sem[0])
            get_a.start()
            remote(window(first, i), window(left, i), l_sem[i][0], next_in).wait_recv()
            get_b = here(window(left, i), b, v_sem[1])
            get_b.start()
            get_a.wait()
            get_b.wait()
            add_into(keep, la, lb, rows, cols)
            remote(keep.at[part], window(cross, i), l_sem[i][1], facing).start()

    def line_two(i):
        _, name, r, c, rows, cols = CHUNKS[i]
        part = (pl.ds(0, rows), pl.ds(0, cols))
        keep, done = ring[i % DEPTH], tt[i % 2]

        @pl.when(middle)
        def _():
            remote(keep.at[part], window(cross, i), l_sem[i][1], facing).wait()
            get = here(window(cross, i), lb.at[part], v_sem[1])
            get.start()
            if i >= 2:
                line_out(i - 2)
            get.wait()
            add_into(done, keep, lb, rows, cols)
            remote(done.at[part], window(total, i), l_sem[i][2], next_out).start()
            here(done.at[part], window(total, i), o_sem[i % 4]).start()

    def line_out(i):
        _, name, r, c, rows, cols = CHUNKS[i]
        done = tt[i % 2].at[pl.ds(0, rows), pl.ds(0, cols)]
        remote(done, window(total, i), l_sem[i][2], next_out).wait_send()
        here(done, window(total, i), o_sem[i % 4]).wait()

    pumped, ready = [0, 0], set()

    def ahead():
        i = pumped[0]
        assert CHUNKS[i][0] in ready and i < pumped[1] + DEPTH
        line_one(i)
        pumped[0] += 1

    def behind():
        i = pumped[1]
        assert i < pumped[0]
        line_two(i)
        pumped[1] += 1

    def grad_ready(group):
        grad_take(group)
        grad_send(group, 0, "wait")
        line_send(group)
        ready.add(group)

    g_sum[...] = jnp.zeros((8, H), F32)
    k_sem = [next(sems) for _ in range(3)]
    q_sem = [[next(sems) for _ in range(3)] for _ in range(2)]
    d_ob, d_qkv = ob, dg
    here_half = (lane // HD) == kv_head
    out_local = here(out_s, out_ref.at[:, half], next(local_count))
    out_remote = remote(out_s, out_ref.at[:, half], next(sems), core)
    in_local = here(d_hid, in_grad_ref.at[:, half], next(local_count))
    in_remote = remote(d_hid, in_grad_ref.at[:, half], next(sems), core)
    kv_copy = here(x2.at[pl.ds(0, 512), pl.ds(T, T)], first["k"], next(local_count))
    whole_move = remote(g_whole.at[:, half], g_whole.at[:, half], next(sems), core)
    gain_move = here(g_whole.at[:, pl.ds(al(f * 512, 512), 512)], gain_ref, next(local_count))

    def norm_two_back():
        lh.wait()
        scatter_wait()

        def rows_back(i, carry):
            rows = scattered(i)
            yo[sub(i), :] = rows
            hat = hid[sub(i), :] * r2s[sub(i), 0:1]
            ss_own[1, sub(i), :] = jnp.broadcast_to(jnp.sum(rows * gain_two * hat, axis=-1, keepdims=True), (STEP, TILE))
            return carry + jnp.sum(rows * hat, axis=0, keepdims=True)

        g_sum[1:2, :] = lax.fori_loop(0, T // STEP, rows_back, jnp.zeros((1, H), F32))
        core_sums(1)

        @pl.loop(0, T // STEP)
        def _(i):
            scale = r2s[sub(i), 0:1]
            hat = hid[sub(i), :] * scale
            mean = (ss_own[1, sub(i), 0:1] + ss_other[1, sub(i), 0:1]) * (1.0 / W)
            rows = out_s[sub(i), :].astype(F32) + scale * (yo[sub(i), :] * gain_two - hat * mean)
            d_hid[sub(i), :] = rows
            dh[pl.ds(al(f * T + i * STEP, STEP), STEP), half] = rows.astype(BF)

        column_each("u", False, lambda cp: cp.wait_send())
        gather_start(3, dh, True)

    def dh_take():
        gather_forward(3, dh)
        for k in range(4):
            gather_take(3, dh, k)

    def out_grads():
        sent("dA", "dB", "dC")

        def product(k):
            stage("o", k)[...] = tn(ob[...], dh[:, block_cols(k)]).astype(BF)

        each_owner(product, "o")

        @pl.loop(0, 4)
        def _(b):
            ob[rows_of(b), :] = nt(dh[rows_of(b), :], w_o[...]).astype(BF)

    def attend_back(pair, i_seq):
        s = 2 * pair + i_seq
        bias_of(s)
        kv, keys, values = kv_of(s)
        keys_t = jnp.transpose(kv)[:HD, :].astype(BF)
        c, sn = turns(s)
        d_key = jnp.zeros((4 * T, TILE), F32)
        d_value = jnp.zeros((4 * T, TILE), F32)
        for i in range(2):
            d_query = []
            for parity in range(2):
                q = only(q_buf[rows_of(s), i * TILE : (i + 1) * TILE], parity)
                do = only(d_ob[rows_of(s), i * TILE : (i + 1) * TILE], parity)
                weights = jnp.exp(nt(keys, q) + bias[...].astype(F32) - lse[s, 2 * i + parity : 2 * i + parity + 1, :])
                d_weights = nt(values, do)
                delta = jnp.sum(weights * d_weights, axis=0, keepdims=True)
                d_scores = (weights * (d_weights - delta)).astype(BF)
                d_value = d_value + nn(weights.astype(BF), do)
                d_key = d_key + nn(d_scores, q)
                d_query.append(nn(keys_t, d_scores))
            d_query = jnp.transpose(jnp.concatenate(d_query, 0)) * 0.125
            d_qkv[rows_of(s), i * TILE : (i + 1) * TILE] = turn(d_query, c, -sn).astype(BF)
        d_key = d_key + pltpu.roll(d_key, HD, 1)
        d_value = d_value + pltpu.roll(d_value, HD, 1)
        keep, give = jnp.where(even, d_key, d_value), jnp.where(even, d_value, d_key)
        mine_here = lane // HD == i_seq
        for j in range(4):
            for place, values in ((kept, keep), (given, give)):
                at = pair_rows(pair, j)
                place[at, :] = jnp.where(mine_here, values[j * T : (j + 1) * T, :], place[at, :].astype(F32)).astype(BF)

    d_kv_pair = w_u.at[:, pl.ds(T, TILE)]
    pair_move = remote(given, d_kv_pair, next(sems), plane(1))

    def pair_sum():
        pair_move.wait()

        @pl.loop(0, W // STEP)
        def _(i):
            rows = kept[sub(i), :].astype(F32) + d_kv_pair[sub(i), :].astype(F32)
            kept[sub(i), :] = rows.astype(BF)

            @pl.when(i // (512 // STEP) == z)
            def _():
                d_kv[pl.ds(al(i % (512 // STEP) * STEP, STEP), STEP), :] = rows

        for move in d_kv_moves():
            move.start()

    def d_kv_moves():
        return [remote(kept.at[pl.ds(al(flip(z, k) * 512, 512), 512), :], d_kv_recv.at[k - 1], k_sem[k - 1], column(k)) for k in (1, 2, 3)]

    def up_A():
        sent("gA", "gB")
        feed_grads("u", "A", du)

    def d_kv_take():
        for move in d_kv_moves():
            move.wait()

        for s in range(4):
            c, sn = turns(s)
            rows = pl.ds(s // 2 * T, T)
            whole = d_kv[rows, :]
            for k in range(3):
                whole = whole + d_kv_recv[k, rows, :].astype(F32)
            turned = pltpu.roll(whole, HD, 1)
            whole = jnp.where(low_lane, whole, turned) if s % 2 == 0 else jnp.where(low_lane, turned, whole)
            d_qkv[rows_of(s), 2 * TILE : 3 * TILE] = jnp.where(here_half & even, turn(whole, c, -sn), 0.0).astype(BF)
            d_qkv[rows_of(s), 3 * TILE : 4 * TILE] = jnp.where(here_half & ~even, whole, 0.0).astype(BF)

    def qkv_grads():
        gather_drain(2, x2, True)

        def product(k):
            @pl.loop(0, 2)
            def _(i):
                xs = x1[:, pl.ds(al(flip(f, k) * 512 + i * T, T), T)]
                grads = tn(xs, d_qkv[:, 0:512]).astype(BF)
                stage("q", k)[pl.ds(al(i * T, T), T), :] = grads[:, 0:T]
                stage("k", k)[pl.ds(al(i * T, T), T), :] = grads[:, T:]

        each_owner(product, "q", "k")

    d1_first, d1_own = scatter_steps(lambda b, c: nt(d_qkv[rows_of(b), 0:512], w_qkv[pl.ds(al(c, COLS), COLS), :]))
    out_first, out_own = scatter_steps(lambda b, c: nn(act[rows_of(b), :], w_d[:, pl.ds(al(c, COLS), COLS)]))

    def kv_ready():
        grad_take("k")

        @pl.loop(0, 512 // STEP)
        def _(i):
            rows = x2[sub(i), T : 2 * T].astype(F32)
            for k in (1, 2, 3):
                rows = rows + kv_place(k)[sub(i), :].astype(F32)
            x2[sub(i), T : 2 * T] = rows.astype(BF)

        kv_copy.start()
        kv_copy.wait()
        line_send("k")
        ready.add("k")

    def norm_one_back():
        scatter_wait()

        def rows_back(i, carry):
            rows = scattered(i)
            yo[sub(i), :] = rows
            hat = xv[sub(i), half].astype(F32) * r1s[sub(i), 0:1]
            ss_own[2, sub(i), :] = jnp.broadcast_to(jnp.sum(rows * gain_one * hat, axis=-1, keepdims=True), (STEP, TILE))
            return carry + jnp.sum(rows * hat, axis=0, keepdims=True)

        g_sum[0:1, :] = lax.fori_loop(0, T // STEP, rows_back, jnp.zeros((1, H), F32))
        for k in (1, 2, 3):
            pl.semaphore_signal(credit, inc=1, device_id=plane(k), device_id_type=MESH)
        pl.semaphore_signal(credit, inc=1, device_id=core, device_id_type=MESH)
        core_sums(2)
        g_plane[f, :, :] = g_sum[...]
        for k in (1, 2, 3):
            remote(g_sum, g_plane.at[f], q_sem[0][k - 1], plane(k)).start()

        @pl.loop(0, T // STEP)
        def _(i):
            scale = r1s[sub(i), 0:1]
            hat = xv[sub(i), half].astype(F32) * scale
            mean = (ss_own[2, sub(i), 0:1] + ss_other[2, sub(i), 0:1]) * (1.0 / W)
            d_hid[sub(i), :] = d_hid[sub(i), :] + scale * (yo[sub(i), :] * gain_one - hat * mean)

        in_local.start()
        in_remote.start()

    def out_begin():
        pl.semaphore_wait(credit, 4)
        out_first()

    def out_end():
        scatter_wait()

        @pl.loop(0, T // STEP)
        def _(i):
            out_s[sub(i), :] = (hid[sub(i), :] + scattered(i)).astype(BF)

        out_local.start()
        out_remote.start()

    def gains_column():
        for k in (1, 2, 3):
            remote(g_sum, g_plane.at[flip(f, k)], q_sem[0][k - 1], plane(k)).wait_recv()
        g_column[z, :, :] = ((g_plane[0, :, :] + g_plane[1, :, :]) + g_plane[2, :, :]) + g_plane[3, :, :]
        for k in (1, 2, 3):
            remote(g_column.at[z], g_column.at[z], q_sem[1][k - 1], column(k)).start()

    def gains_end():
        for k in (1, 2, 3):
            remote(g_column.at[z], g_column.at[flip(z, k)], q_sem[1][k - 1], column(k)).wait_recv()
        g_whole[:, half] = ((g_column[0, :, :] + g_column[1, :, :]) + g_column[2, :, :]) + g_column[3, :, :]
        whole_move.start()
        whole_move.wait()
        gain_move.start()

    steps = {
        "feed_back": feed_back,
        "gate_A": gate_A,
        "d2_first": d2_first,
        "d2_own": d2_own,
        "gate_B": lambda: feed_grads("g", "B", dg),
        "up_A": up_A,
        "up_B": lambda: feed_grads("u", "B", du),
        "relay": scatter_relay,
        "norm_two_back": norm_two_back,
        "dh_take": dh_take,
        "out_grads": out_grads,
        "pair_send": lambda: pair_move.start(),
        "pair_sum": pair_sum,
        "d_kv_take": d_kv_take,
        "qkv_grads": qkv_grads,
        "d1_first": d1_first,
        "d1_own": d1_own,
        "kv_ready": kv_ready,
        "norm_one_back": norm_one_back,
        "out_first": out_begin,
        "out_own": out_own,
        "out_end": out_end,
        "gains_column": gains_column,
        "gains_end": gains_end,
    }
    for step in ORDER:
        if step == "+":
            ahead()
        elif step == "-":
            behind()
        elif step == 1:
            ahead()
            behind()
        elif step in GROUPS:
            grad_ready(step)
        elif step[:6] == "attend":
            attend_back(int(step[6]) // 2, int(step[6]) % 2)
        else:
            steps[step]()
    while pumped[0] < len(CHUNKS):
        ahead()
        behind()
    while pumped[1] < len(CHUNKS):
        behind()

    @pl.when(middle)
    def _():
        line_out(len(CHUNKS) - 2)
        line_out(len(CHUNKS) - 1)

    @pl.when(end)
    def _():
        for i in range(len(CHUNKS)):
            remote(window(first, i), window(left, i), l_sem[i][0], next_in).wait_send()
            remote(window(total, i), window(total, i), l_sem[i][2], next_in).wait_recv()

    gain_move.wait()
    out_local.wait()
    out_remote.wait()
    in_local.wait()
    in_remote.wait()
    weights_drain()
    column_each("d", False, lambda cp: cp.wait_send())
    column_each("qkv", False, lambda cp: cp.wait_send())
    gather_drain(0, x1, False)
    gather_drain(3, dh, True)
    for k in (1, 2, 3):
        remote(own_gain, own_gain, a_sem[k - 1], plane(k)).wait_send()
        remote(tb.at[f], tb.at[f], t_sem[k - 1], plane(k)).wait_send()
        remote(kv_all.at[z], kv_all.at[z], z_sem[k - 1][0], column(k)).wait_send()
        remote(ids.at[z], ids.at[z], z_sem[k - 1][1], column(k)).wait_send()
        remote(g_sum, g_plane.at[f], q_sem[0][k - 1], plane(k)).wait_send()
        remote(g_column.at[z], g_column.at[z], q_sem[1][k - 1], column(k)).wait_send()
        for name in ("uA", "uB", "o", "q", "k"):
            grad_send(name, k, "wait")
    assert (next(sems), next(local_count)) == (REMOTE_SEMS, LOCAL_SEMS)


REMOTE_SEMS, LOCAL_SEMS = 244, 36


def layer_call(inputs, positions, blocks, cotangent, attn_gain, w_query, w_key, w_value, w_out, mlp_gain, w_gate, w_up, w_down):
    shape = jax.ShapeDtypeStruct
    grads = [shape((rows, cols), BF) for _, rows, cols in GRADS]
    any_spec = pl.BlockSpec(memory_space=pl.ANY)
    v = pltpu.VMEM
    results = pl.pallas_call(
        layer_kernel,
        out_shape=[shape((T, W), BF), shape((T, W), F32), shape((8, 512), F32)] + grads * 4,
        in_specs=[any_spec] + [pl.BlockSpec(memory_space=pltpu.VMEM)] * 4 + [any_spec] * 8,
        out_specs=[any_spec] * 27,
        scratch_shapes=[
            v((4 * T, W), BF), v((4 * T, W), BF), v((4 * T, W), BF), v((4 * T, W), BF),
            v((W, 512), BF), v((T, W), BF), v((W, WIN), BF), v((W, WIN), BF), v((WIN, W), BF),
            v((4 * T, WIN), BF), v((4 * T, WIN), BF), v((4 * T, WIN), BF),
            v((4 * T, T), BF), v((4, 4, T, TILE), BF), v((4 * T, T), BF),
            v((4, T, H), BF), v((4, T, H), BF), v((2, T, H), BF), v((2, T, 512), BF), v((T, H), F32), v((T, H), F32), v((T, H), F32), v((T, W), BF),
            v((4, 8, T), F32), v((8, W), F32), v((4, 8, T), F32), v((T, TILE), F32), v((T, TILE), F32),
            v((3, T, TILE), F32), v((3, T, TILE), F32), v((4, 8, T), F32), v((4 * T, T), BF),
            v((4 * WIN, 512), BF), v((8, 512, 512), BF), v((4, 2, T, TILE), F32),
            v((512, TILE), F32), v((3, 512, TILE), BF),
            v((T, H), BF), v((8, H), F32), v((4, 8, H), F32), v((4, 8, H), F32), v((8, W), F32),
            pltpu.SemaphoreType.DMA((REMOTE_SEMS,)), pltpu.SemaphoreType.DMA((REMOTE_SEMS,)),
            pltpu.SemaphoreType.DMA((LOCAL_SEMS,)), pltpu.SemaphoreType.REGULAR,
        ],
        compiler_params=pltpu.CompilerParams(collective_id=0, has_side_effects=True, vmem_limit_bytes=62 << 20),
    )(inputs, positions, blocks, attn_gain, mlp_gain, cotangent, w_query, w_key, w_value, w_out, w_gate, w_up, w_down)
    return finish(*results[:3], *results[-6:])


def finish_kernel(*refs):
    output, input_grad, gains, down, gate, up, out, query, kv = refs[:9]
    targets = refs[9:]
    for source, target in zip((output, input_grad), targets):
        target[0] = source[...]
    attn_target, q_target, k_target, v_target, o_target, mlp_target, g_target, u_target, d_target = targets[2:]
    attn_target[...] = gains[0:1, :]
    mlp_target[...] = gains[1:2, :]
    k_target[...] = kv[:, :TILE].astype(F32)
    v_target[...] = kv[:, TILE:].astype(F32)
    for source, target in ((query, q_target), (out, o_target), (gate, g_target), (up, u_target), (down, d_target)):
        target[...] = source[...].astype(F32)


def finish(output, input_grad, gains, down, gate, up, out, query, kv):
    parts = 4
    shape = jax.ShapeDtypeStruct

    def rows(count, cols):
        return pl.BlockSpec((count // parts, cols), lambda i: (i, 0))

    def page(count, cols):
        return pl.BlockSpec((1, count // parts, cols), lambda i: (0, i, 0))

    line = pl.BlockSpec((1, 512), lambda i: (0, 0))
    results = pl.pallas_call(
        finish_kernel,
        grid=(parts,),
        in_specs=[rows(T, W), rows(T, W), pl.BlockSpec((8, 512), lambda i: (0, 0))] + [rows(*a.shape) for a in (down, gate, up, out, query, kv)],
        out_specs=[page(T, W), page(T, W), line, rows(512, 1024), rows(512, TILE), rows(512, TILE), rows(1024, 512), line, rows(512, 2816), rows(512, 2816), rows(2816, 512)],
        out_shape=[shape((1, T, W), BF), shape((1, T, W), F32), shape((1, 512), F32)]
        + [shape(a, F32) for a in ((512, 1024), (512, TILE), (512, TILE), (1024, 512), (1, 512), (512, 2816), (512, 2816), (2816, 512))],
        compiler_params=pltpu.CompilerParams(dimension_semantics=("arbitrary",)),
    )(output, input_grad, gains, down, gate, up, out, query, kv)
    results = list(results)
    results[2], results[7] = results[2][0], results[7][0]
    return tuple(results)


def solution(mesh):
    n, m = mesh.shape["fsdp"], mesh.shape["ctx"]

    def step(*args):
        return layer_call(*args) if n == m == 4 else local(n, m, *args)

    return jax.shard_map(
        step,
        mesh=mesh,
        in_specs=(
            P("fsdp", "ctx", None),
            P("fsdp", "ctx"),
            P("fsdp", "ctx"),
            P("fsdp", "ctx", None),
            P("fsdp"),
            P("fsdp", "tp"),
            P("fsdp", "tp"),
            P("fsdp", "tp"),
            P("tp", "fsdp"),
            P("fsdp"),
            P("fsdp", "tp"),
            P("fsdp", "tp"),
            P("tp", "fsdp"),
        ),
        out_specs=(
            P("fsdp", "ctx", None),
            P("fsdp", "ctx", None),
            P("fsdp"),
            P("fsdp", "tp"),
            P("fsdp", "tp"),
            P("fsdp", "tp"),
            P("tp", "fsdp"),
            P("fsdp"),
            P("fsdp", "tp"),
            P("fsdp", "tp"),
            P("tp", "fsdp"),
        ),
        check_vma=False,
    )
```

```python
import functools
import math

import jax
import jax.numpy as jnp
from jax import lax
from jax.experimental import pallas as pl
from jax.experimental.pallas import tpu as pltpu
from jax.sharding import PartitionSpec as P

HD = 64
EPSILON = 1e-05
NEGATIVE = -1e30
BF = jnp.bfloat16
F32 = jnp.float32


def dot(a, b, ca, cb):
    return lax.dot_general(a, b, (((ca,), (cb,)), ((), ())), preferred_element_type=F32)


def angles(positions):
    half = HD // 2
    frequency = jnp.exp(jnp.arange(half, dtype=F32) * (-2.0 * math.log(10000.0) / HD))
    turned = positions.astype(F32)[:, None] * frequency[None, :]
    return jnp.cos(turned)[:, None, :], jnp.sin(turned)[:, None, :]


def rotate(values, cosine, sine):
    half = HD // 2
    a, b = values[..., :half], values[..., half:]
    return jnp.concatenate([a * cosine - b * sine, b * cosine + a * sine], axis=-1)


def gated(values, after):
    return lax.optimization_barrier((values, after))[0]


def local(n, m, inputs, positions, blocks, cotangent, attn_gain, w_query, w_key, w_value, w_out, mlp_gain, w_gate, w_up, w_down):
    f = lax.axis_index("fsdp")
    z = lax.axis_index("ctx")
    t = lax.axis_index("tp")
    tokens, width = inputs.shape[1:]
    half = width // 2
    peers = range(1, n)

    def plane(x, k):
        return x if k == 0 else lax.ppermute(x, "fsdp", [(i, i ^ k) for i in range(n)])

    def column(x, k):
        return x if k == 0 else lax.ppermute(x, "ctx", [(i, i ^ k) for i in range(m)])

    def swap(x):
        return lax.ppermute(x, "tp", [(0, 1), (1, 0)])

    def part(x, index, axis):
        size = x.shape[axis] // n
        return lax.dynamic_slice_in_dim(x, index * size, size, axis)

    def mine(x, which):
        return lax.dynamic_slice_in_dim(x, which * half, half, x.ndim - 1)

    def place(pieces, axis):
        size = pieces[0].shape[axis]
        shape = list(pieces[0].shape)
        shape[axis] = size * n
        whole = jnp.zeros(shape, pieces[0].dtype)
        for k in range(n):
            whole = lax.dynamic_update_slice_in_dim(whole, pieces[k], (f ^ k) * size, axis)
        return whole

    def join(own, other):
        return jnp.where(t == 0, jnp.concatenate([own, other], -1), jnp.concatenate([other, own], -1))

    def gather(x):
        rows = jnp.concatenate([plane(x, k) for k in range(n)], 0)
        return join(rows, swap(rows))

    def scatter(partial):
        own = mine(partial, t) + swap(mine(partial.astype(BF), 1 - t)).astype(F32)
        low = own.astype(BF)
        total = own[:tokens]
        for k in peers:
            total = total + plane(low[k * tokens : (k + 1) * tokens], k).astype(F32)
        return total

    def row_mean(own):
        own = jnp.sum(own, -1)
        return ((own + swap(own)) / width)[:, None]

    x = inputs[0].astype(F32)
    gains = jnp.stack([attn_gain, mlp_gain])
    gains = place([plane(gains, k) for k in range(n)], 1).astype(F32)
    marks = jnp.stack([positions[0], blocks[0]])
    marks = [plane(marks, k) for k in range(n)]
    place_rows = jnp.concatenate([mk[0] for mk in marks])
    query_ids = jnp.stack([mk[1] for mk in marks])
    scale_one = lax.rsqrt(jnp.mean(x * x, axis=-1, keepdims=True) + EPSILON)
    x_half = mine(x, t)
    hat_one = x_half * scale_one
    gain_one, gain_two = mine(gains[0:1], t), mine(gains[1:2], t)
    xn_one = gather((hat_one * gain_one).astype(BF))

    heads = w_query.shape[1] // HD // n
    cols = heads * HD
    kv_pair = jnp.concatenate([w_key, w_value], 1)
    kv_heads = w_key.shape[1] // HD
    w_qkv = place([plane(jnp.concatenate([part(w_query, f ^ k, 1), kv_pair], 1), k) for k in range(n)], 0)
    wo = gated(w_out, xn_one)
    wo = place([plane(part(wo, f ^ k, 0), k) for k in range(n)], 1)
    gate_up = gated((w_gate, w_up), xn_one)
    gate_up = [plane(jnp.stack([part(gate_up[0], f ^ k, 1), part(gate_up[1], f ^ k, 1)]), k) for k in range(n)]
    wg = place([g[0] for g in gate_up], 0)
    wu = place([g[1] for g in gate_up], 0)

    qkv = dot(xn_one, w_qkv, 1, 0)
    cosine, sine = angles(place_rows)
    kv_here = (heads * f) // ((w_query.shape[1] // HD) // kv_heads)

    def pick(both):
        out = both[:, :HD]
        for g in range(1, kv_heads):
            out = jnp.where(kv_here == g, both[:, g * HD : (g + 1) * HD], out)
        return out

    kw = kv_heads * HD
    query = rotate(qkv[:, :cols].reshape(-1, heads, HD), cosine, sine).astype(BF)
    key = rotate(pick(qkv[:, cols : cols + kw])[:, None, :], cosine, sine)[:, 0, :].astype(BF)
    value = pick(qkv[:, cols + kw :]).astype(BF)
    key_value = jnp.concatenate([key, value], 1).reshape(n, tokens, 2 * HD)
    kv_all = jnp.concatenate([column(key_value, k) for k in range(m)], 1)
    ids_all = jnp.concatenate([column(query_ids, k) for k in range(m)], 1)
    keys, values = kv_all[..., :HD], kv_all[..., HD:]
    factor = 1.0 / math.sqrt(HD)
    query = query.reshape(n, tokens, heads, HD)
    allowed = (ids_all[:, None, :] <= query_ids[:, :, None])[:, None]
    scores = jnp.einsum("nthd,nsd->nhts", query, keys, preferred_element_type=F32) * factor
    scores = jnp.where(allowed, scores, NEGATIVE)
    top = jnp.max(scores, -1, keepdims=True)
    raw = jnp.where(allowed, jnp.exp(scores - top), 0.0)
    weights = raw / jnp.sum(raw, -1, keepdims=True)
    weights_low = weights.astype(BF)
    attended = jnp.einsum("nhts,nsd->nthd", weights_low, values, preferred_element_type=F32)
    attended_low = attended.astype(BF).reshape(n * tokens, cols)

    hidden = x_half + scatter(dot(attended_low, wo, 1, 0))
    scale_two = lax.rsqrt(row_mean(hidden * hidden) + EPSILON)
    hat_two = hidden * scale_two
    xn_two = gather((hat_two * gain_two).astype(BF))
    cot = gather(gated(mine(cotangent[0], t), wg))
    wd = gated(w_down, wg)
    wd = place([plane(part(wd, f ^ k, 0), k) for k in range(n)], 1)
    gate = dot(xn_two, wg, 1, 0)
    up = dot(xn_two, wu, 1, 0)
    sigma = jax.nn.sigmoid(gate)
    silu = gate * sigma
    act = (silu * up).astype(BF)
    dact = dot(cot, wd, 1, 1)
    dgate = (dact * up * sigma * (1.0 + gate * (1.0 - sigma))).astype(BF)
    dup = (dact * silu).astype(BF)

    def reduce(piece):
        if m != 4:
            return lax.psum(piece, "ctx")
        one = (piece.astype(F32) + lax.ppermute(piece, "ctx", [(0, 1), (3, 2)]).astype(F32)).astype(BF)
        two = (one.astype(F32) + lax.ppermute(one, "ctx", [(1, 2), (2, 1)]).astype(F32)).astype(BF)
        three = lax.ppermute(two, "ctx", [(1, 0), (2, 3)])
        return jnp.where((z == 0) | (z == 3), three, two)

    def share(grad, axis):
        low = grad.astype(BF)
        return [plane(part(low, f ^ k, axis), k) for k in range(n)]

    down_parts = [reduce(p) for p in share(dot(act, cot, 0, 0), 1)]
    gate_parts = [reduce(p) for p in share(dot(xn_two, dgate, 0, 0), 0)]
    up_parts = [reduce(p) for p in share(dot(xn_two, dup, 0, 0), 0)]
    d_two = scatter(dot(dgate, wg, 1, 1) + dot(dup, wu, 1, 1))
    out_half = (hidden + scatter(dot(act, wd, 1, 0))).astype(BF)
    output = join(out_half, swap(out_half))
    gain_two_grad = jnp.sum(d_two * hat_two, 0)
    e_two = d_two * gain_two
    d_hidden = mine(cotangent[0], t).astype(F32) + scale_two * (e_two - hat_two * row_mean(e_two * hat_two))
    dhb = gather(d_hidden.astype(BF))
    out_parts = [reduce(p) for p in share(dot(attended_low, dhb, 0, 0), 1)]

    d_att = dot(dhb, wo, 1, 1).astype(BF).reshape(n, tokens, heads, HD)
    delta = jnp.einsum("nthd,nthd->nht", d_att.astype(F32), attended)
    d_weights = jnp.einsum("nthd,nsd->nhts", d_att, values, preferred_element_type=F32)
    d_scores = (weights * (d_weights - delta[..., None])).astype(BF)
    dv = jnp.einsum("nhts,nthd->nsd", weights_low, d_att, preferred_element_type=F32)
    dk = jnp.einsum("nhts,nthd->nsd", d_scores, query, preferred_element_type=F32) * factor
    dq = jnp.einsum("nhts,nsd->nthd", d_scores, keys, preferred_element_type=F32) * factor
    d_kv = jnp.concatenate([dk, dv], -1).reshape(n, m, tokens, 2 * HD)
    d_low = d_kv.astype(BF)
    d_kv_own = d_kv[:, 0]
    for k in range(1, m):
        d_kv_own = d_kv_own + column(d_low[:, k], k).astype(F32)
    d_kv_own = d_kv_own.reshape(n * tokens, 2 * HD)
    dq = rotate(dq.reshape(n * tokens, heads, HD), cosine, -sine).reshape(n * tokens, cols)
    dk = rotate(d_kv_own[:, None, :HD], cosine, -sine)[:, 0, :]
    d_qkv = jnp.concatenate([dq, dk, d_kv_own[:, HD:]], 1).astype(BF)
    w_here = jnp.concatenate([w_qkv[:, :cols], pick(w_qkv[:, cols : cols + kw]), pick(w_qkv[:, cols + kw :])], 1)
    d_one = scatter(dot(d_qkv, w_here, 1, 1))
    qkv_parts = share(dot(xn_one, d_qkv, 0, 0), 0)
    key_parts, value_parts = [0.0] * kv_heads, [0.0] * kv_heads
    for k in range(n):
        owner = (heads * (f ^ k)) // ((w_query.shape[1] // HD) // kv_heads)
        piece = qkv_parts[k].astype(F32)
        for g in range(kv_heads):
            key_parts[g] = key_parts[g] + jnp.where(owner == g, piece[:, cols : cols + HD], 0.0)
            value_parts[g] = value_parts[g] + jnp.where(owner == g, piece[:, cols + HD :], 0.0)
    small = reduce(jnp.concatenate(key_parts + value_parts, 1).astype(BF)).astype(F32)
    query_parts = [reduce(p[:, :cols]) for p in qkv_parts]
    gain_one_grad = jnp.sum(d_one * hat_one, 0)
    e_one = d_one * gain_one
    in_half = d_hidden + scale_one * (e_one - hat_one * row_mean(e_one * hat_one))
    input_grad = join(in_half, swap(in_half))
    gain_grads = jnp.stack([gain_one_grad, gain_two_grad])
    nothing = jnp.zeros_like(gain_grads)
    gain_grads = jnp.where(t == 0, jnp.concatenate([gain_grads, nothing], 1), jnp.concatenate([nothing, gain_grads], 1))
    gain_grads = part(lax.psum(gain_grads, ("fsdp", "ctx", "tp")), f, 1)

    def settle(pieces, axis):
        return place(pieces, axis).astype(F32)

    return (
        output[None],
        input_grad[None],
        gain_grads[0],
        settle(query_parts, 1),
        small[:, :kw],
        small[:, kw:],
        settle(out_parts, 0),
        gain_grads[1],
        settle(gate_parts, 1),
        settle(up_parts, 1),
        settle(down_parts, 0),
    )


T, W, H, TILE = 256, 2048, 1024, 128
MAIN, WIN = 640, 768
GRADS = (("d", 2816, 512), ("g", 512, 2816), ("u", 512, 2816), ("o", 1024, 512), ("q", 512, 1024), ("k", 512, 256))
PART = 384


PARTS = {"dA": (0, 128), "dB": (128, 256), "dC": (PART, PART)}
PARTS |= {name + which: (0 if which == "A" else PART, PART) for name in "gu" for which in "AB"}
LAST = ("dC", "gB", "uB")
GROUPS = tuple(PARTS) + ("o", "q", "k")


def chunk_list():
    chunks = []
    for group, (_, size) in PARTS.items():
        for j in range(4):
            part = MAIN - PART if group in LAST and j % 2 else size
            chunks.append((group, group[0], j, j) + ((part, 512) if group[0] == "d" else (512, part)))
    chunks += [("o", "o", r, 0, 256, 512) for r in range(0, 1024, 256)]
    chunks += [("q", "q", 0, c, 512, 256) for c in range(0, 1024, 256)]
    return chunks + [("k", "k", r, 0, 256, 256) for r in (0, 256)]


CHUNKS = chunk_list()
DEPTH = 4
ORDER = (
    "dA", "+", "feed_back", 1, 1, 1, "dB", 1, "gate_A", 1, 1, "d2_first", 1, "d2_own", "dC", 1, "relay", 1, "gate_B", "gA", 1, 1, 1,
    "norm_two_back", 1, "gB", "up_A", 1, 1, "dh_take", "+", "out_grads", 1, "attend0", 1, "attend1", 1, "uA", "+", "up_B", 1, "attend2", 1,
    "attend3", "pair_send", 1, "-", "pair_sum", "uB", "+", 1, "o", "d_kv_take", 1, "qkv_grads", 1, "d1_first", 1, "d1_own", 1, "q", 1, "relay", 1,
    "kv_ready", 1, 1, "norm_one_back", 1, "out_first", 1, "out_own", 1, "relay", 1, "-", "gains_column", "-", "out_end", "gains_end",
)
MESH = pl.DeviceIdType.MESH


def nn(a, b):
    return lax.dot_general(a, b, (((1,), (0,)), ((), ())), preferred_element_type=F32)


def nt(a, b):
    return lax.dot_general(a, b, (((1,), (1,)), ((), ())), preferred_element_type=F32)


def tn(a, b):
    return lax.dot_general(a, b, (((0,), (0,)), ((), ())), preferred_element_type=F32)


def flip(a, k):
    return (a % 2 + k % 2) % 2 + 2 * ((a // 2 + k // 2) % 2)


def layer_kernel(*refs):
    names = iter(refs)

    def take(count):
        return [next(names) for _ in range(count)]

    x_in, place_in, block_in, gain_in_one, gain_in_two, cot_in, wq, wk, wv, wo, wg, wu, wd = take(13)
    out_ref, in_grad_ref, gain_ref = take(3)
    first, left, cross, total = ({name: next(names) for name, _, _ in GRADS} for _ in range(4))
    (x1, x2, ct, dh, w_qkv, w_o, w_g, w_u, w_d, act, dg, du, q_buf, kv_all, ob) = take(15)
    (ps, pr, rr, rd, yo, hid, d_hid, xv, tb, ga, ids, r1s, r2s, ss_own, ss_other, lse, bias) = take(17)
    (gs_d, line, waves, d_kv, d_kv_recv, out_s, g_sum, g_plane, g_column, g_whole) = take(10)
    send_sem, recv_sem, local_sem, credit = take(4)
    f, z, t = lax.axis_index("fsdp"), lax.axis_index("ctx"), lax.axis_index("tp")
    sems = iter(range(10**6))
    drains = []

    def al(v, by):
        return pl.multiple_of(v, by)

    def plane(k):
        return (flip(f, k), z, t)

    def column(k):
        return (f, flip(z, k), t)

    core = (f, z, 1 - t)
    rows_f = pl.ds(al(f * T, T), T)
    half = pl.ds(al(t * H, H), H)
    rest = pl.ds(al((1 - t) * H, H), H)

    def rows_of(b):
        return pl.ds(al(b * T, T), T)

    def remote(src, dst, s, device):
        return pltpu.make_async_remote_copy(src_ref=src, dst_ref=dst, send_sem=send_sem.at[s], recv_sem=recv_sem.at[s], device_id=device, device_id_type=MESH)

    def here(src, dst, s):
        return pltpu.make_async_copy(src, dst, local_sem.at[s])

    local_count = iter(range(10**6))

    lx = here(x_in.at[0], xv, next(local_count))
    lx.start()
    lc = here(cot_in.at[0], ct.at[rows_f, :], next(local_count))
    lc.start()
    lh = here(cot_in.at[0, :, half], out_s, next(local_count))
    lh.start()
    own_gain = ga.at[:, pl.ds(al(f * 512, 512), 512)]
    own_gain[0:1, :] = gain_in_one[...].astype(F32).reshape(1, 512)
    own_gain[1:2, :] = gain_in_two[...].astype(F32).reshape(1, 512)
    tb[f, 0:1, :] = place_in[...].astype(F32)
    tb[f, 1:2, :] = block_in[...].astype(F32)

    def starts(r):
        return (11 * r + 1 - t) // 2

    def full(r):
        return (r + t) % 2 == 0

    def weight_moves(k, taking):
        r = flip(f, k)
        sender, taker = (r, f) if taking else (f, r)
        rows = pl.ds(al(sender * 512, 512), 512)
        row_part = pl.ds(al(sender * 512 + z * TILE, TILE), TILE)
        own_part = pl.ds(al(z * TILE, TILE), TILE)
        begin = al(starts(taker) * TILE, TILE)
        tail = al(begin + MAIN, TILE)
        col = al(taker * T, T)
        moves = {
            "o": [(wo.at[pl.ds(col, T), :], w_o.at[:, rows])],
            "g": [(wg.at[:, pl.ds(begin, MAIN)], w_g.at[rows, pl.ds(0, MAIN)])],
            "g+": [(wg.at[:, pl.ds(tail, TILE)], w_g.at[rows, pl.ds(MAIN, TILE)])],
        }
        from_rows, to_rows = pl.ds(0, 512), rows
        if k:
            from_rows, to_rows = pl.ds(al(z % 2 * T, T), T), pl.ds(al(sender * 512 + z % 2 * T, T), T)
        moves["qkv"] = [
            (wq.at[from_rows, pl.ds(col, T)], w_qkv.at[to_rows, pl.ds(0, T)]),
            (wk.at[from_rows, :], w_qkv.at[to_rows, pl.ds(T, TILE)]),
            (wv.at[from_rows, :], w_qkv.at[to_rows, pl.ds(T + TILE, TILE)]),
        ]
        if k == 0:
            moves["u"] = [(wu.at[:, pl.ds(begin, MAIN)], w_u.at[rows, pl.ds(0, MAIN)])]
            moves["u+"] = [(wu.at[:, pl.ds(tail, TILE)], w_u.at[rows, pl.ds(MAIN, TILE)])]
            moves["d"] = [(wd.at[pl.ds(begin, MAIN), :], w_d.at[pl.ds(0, MAIN), rows])]
            moves["d+"] = [(wd.at[pl.ds(tail, TILE), :], w_d.at[pl.ds(MAIN, TILE), rows])]
        else:
            moves["u"] = [(wu.at[own_part, pl.ds(begin, MAIN)], w_u.at[row_part, pl.ds(0, MAIN)])]
            moves["u+"] = [(wu.at[own_part, pl.ds(tail, TILE)], w_u.at[row_part, pl.ds(MAIN, TILE)])]
            moves["d"] = [(wd.at[pl.ds(begin, MAIN), own_part], w_d.at[pl.ds(0, MAIN), row_part])]
            moves["d+"] = [(wd.at[pl.ds(tail, TILE), own_part], w_d.at[pl.ds(MAIN, TILE), row_part])]
        return moves

    w_counts = (("qkv", 3), ("o", 1), ("g", 1), ("g+", 1), ("u", 1), ("u+", 1), ("d", 1), ("d+", 1))
    w_sem = {(key, k, i): next(sems) for key, c in w_counts for k in (1, 2, 3) for i in range(c)}
    w_local = {(key, i): next(local_count) for key, c in w_counts for i in range(c)}

    def weights_each(key, taking, run):
        for k in (1, 2, 3):
            moves = weight_moves(k, taking)
            for i, (src, dst) in enumerate(moves[key]):
                run(remote(src, dst, w_sem[key, k, i], plane(k)))
            if key + "+" in moves:

                @pl.when(full(f if taking else flip(f, k)))
                def _():
                    (src, dst), = moves[key + "+"]
                    run(remote(src, dst, w_sem[key + "+", k, 0], plane(k)))

    def weights_start(key):
        weights_each(key, False, lambda cp: cp.start())

    def weights_wait(key):
        weights_each(key, True, lambda cp: cp.wait_recv())

    def weights_drain():
        for key in ("qkv", "o", "g", "u", "d"):
            weights_each(key, False, lambda cp: cp.wait_send())

    def weights_own(keys, wait):
        moves = weight_moves(0, False)

        def run(key):
            for i, (src, dst) in enumerate(moves[key]):
                cp = here(src, dst, w_local[key, i])
                cp.wait() if wait else cp.start()

        for key in keys:
            run(key)
            if key + "+" in moves:
                pl.when(full(f))(functools.partial(run, key + "+"))

    y_sem = {(key, k, j): next(sems) for key in ("qkv", "u", "d") for k in (1, 2, 3) for j in (1, 2, 3) if key != "qkv" or j == 1}

    def column_each(key, taking, run):
        for k in (1, 2, 3):
            for j in (1, 2, 3):
                from_z = flip(z, j) if taking else z
                part = pl.ds(al(flip(f, k) * 512 + from_z * TILE, TILE), TILE)

                def move(size):
                    ref = w_u.at[part, pl.ds(0, size)] if key == "u" else w_d.at[pl.ds(0, size), part]
                    run(remote(ref, ref, y_sem[key, k, j], column(j)))

                if key == "qkv":
                    if j == 1:
                        ref = w_qkv.at[pl.ds(al(flip(f, k) * 512 + from_z % 2 * T, T), T), :]
                        run(remote(ref, ref, y_sem[key, k, j], column(j)))
                    continue
                pl.when(full(f))(functools.partial(move, WIN))
                pl.when(full(f + 1))(functools.partial(move, MAIN))

    g_sem = [[next(sems) for _ in range(4)] for _ in range(4)]
    f_sem = [[next(sems) for _ in range(4)] for _ in range(4)]
    quarters = (pl.ds(al(t * H, 512), 512), pl.ds(al(t * H + 512, 512), 512))

    def gather_direct(g):
        return (1, 2, 3) if g == 3 else (1, 2)

    def gather_start(g, buf, with_own, src=None):
        block = buf.at[rows_f, half]
        for k in gather_direct(g):
            remote(block if src is None else src, block, g_sem[g][k - 1], plane(k)).start()
        if with_own:
            remote(block, block, f_sem[g][3], core).start()

    def gather_hand(g, buf, k):
        block = buf.at[rows_of(flip(f, k)), half]
        return remote(block, block, f_sem[g][k - 1], core)

    def gather_relay(g, buf, k):
        part = buf.at[rows_of(flip(f, k)), quarters[k - 1]]
        return remote(part, part, g_sem[g][4 - k], plane(3 - k))

    def gather_forward(g, buf):
        for k in gather_direct(g):
            block = buf.at[rows_of(flip(f, k)), half]
            remote(block, block, g_sem[g][k - 1], plane(k)).wait_recv()
            if g != 3:
                gather_relay(g, buf, k).start()
            gather_hand(g, buf, k).start()

    def gather_diagonal(g, buf):
        for k in (1, 2):
            part = buf.at[rows_of(flip(f, 3)), quarters[k - 1]]
            remote(part, part, g_sem[g][4 - k], plane(3 - k)).wait_recv()
        gather_hand(g, buf, 3).start()

    def gather_take(g, buf, k):
        if k == 0:
            block = buf.at[rows_f, rest]
            remote(block, block, f_sem[g][3], core).wait_recv()
        else:
            block = buf.at[rows_of(flip(f, k)), rest]
            remote(block, block, f_sem[g][k - 1], core).wait_recv()

    def gather_drain(g, buf, with_own, src=None):
        block = buf.at[rows_f, half]
        for k in gather_direct(g):
            remote(block if src is None else src, block, g_sem[g][k - 1], plane(k)).wait_send()
        for k in (1, 2, 3):
            gather_hand(g, buf, k).wait_send()
            if g != 3 and k != 3:
                gather_relay(g, buf, k).wait_send()
        if with_own:
            remote(block, block, f_sem[g][3], core).wait_send()

    t_sem = [next(sems) for _ in range(3)]
    a_sem = [next(sems) for _ in range(3)]
    barrier = pltpu.get_barrier_semaphore()
    for k in (1, 2, 3):
        pl.semaphore_signal(barrier, inc=1, device_id=plane(k), device_id_type=MESH)
        pl.semaphore_signal(barrier, inc=1, device_id=column(k), device_id_type=MESH)
    pl.semaphore_signal(barrier, inc=1, device_id=core, device_id_type=MESH)
    pl.semaphore_wait(barrier, 7)

    for k in (1, 2, 3):
        remote(own_gain, own_gain, a_sem[k - 1], plane(k)).start()
        remote(tb.at[f], tb.at[f], t_sem[k - 1], plane(k)).start()
    weights_start("qkv")
    weights_own(("qkv",), False)

    @pl.when(full(f + 1))
    def _():
        w_g[:, MAIN:WIN] = jnp.zeros((W, TILE), BF)
        w_u[:, MAIN:WIN] = jnp.zeros((W, TILE), BF)
        w_d[MAIN:WIN, :] = jnp.zeros((TILE, W), BF)

    lx.wait()
    for k in (1, 2, 3):
        dst = ga.at[:, pl.ds(al(flip(f, k) * 512, 512), 512)]
        remote(dst, dst, a_sem[k - 1], plane(k)).wait_recv()

    STEP = 32

    def sub(i):
        return pl.ds(al(i * STEP, STEP), STEP)

    @pl.loop(0, T // STEP)
    def _(i):
        xs = xv[sub(i), :].astype(F32)
        scale = lax.rsqrt(jnp.mean(xs * xs, axis=-1, keepdims=True) + EPSILON)
        r1s[sub(i), :] = jnp.broadcast_to(scale, (STEP, TILE))
        x1[pl.ds(al(f * T + i * STEP, STEP), STEP), :] = (xs * scale * ga[0:1, :]).astype(BF)

    weights_wait("qkv")
    column_each("qkv", False, lambda cp: cp.start())
    gather_start(0, x1, False)
    gather_forward(0, x1)
    for key in "oudg":
        weights_start(key)
    weights_own("oudg", False)
    gather_diagonal(0, x1)
    for k in (1, 2, 3):
        dst = tb.at[flip(f, k)]
        remote(dst, dst, t_sem[k - 1], plane(k)).wait_recv()
    weights_own(("qkv",), True)
    column_each("qkv", True, lambda cp: cp.wait_recv())

    lane = lax.broadcasted_iota(jnp.int32, (T, TILE), 1)
    low_lane = lane < HD
    first_half = lane % HD < HD // 2
    kv_head = f // 2

    def make_turns(b):
        exponent = lax.broadcasted_iota(jnp.int32, (HD // 2, T), 0).astype(F32) * (-2.0 * math.log(10000.0) / HD)
        turned = jnp.exp(exponent) * tb[b, 0:1, :]
        cosine, sine = jnp.cos(turned), jnp.sin(turned)
        waves[b, 0, :, :] = jnp.transpose(jnp.concatenate([cosine] * 4, 0))
        waves[b, 1, :, :] = jnp.transpose(jnp.concatenate([-sine, sine, -sine, sine], 0))

    def turns(b):
        return waves[b, 0, :, :], waves[b, 1, :, :]

    def turn(v, c, s):
        swapped = jnp.where(first_half, pltpu.roll(v, TILE - 32, 1), pltpu.roll(v, 32, 1))
        return v * c + swapped * s

    def qkv_block(k):
        b = flip(f, k)
        qkv = nn(x1[rows_of(b), :], w_qkv[...])
        make_turns(b)
        c, s = turns(b)
        for i in range(2):
            q = turn(qkv[:, i * TILE : (i + 1) * TILE], c, s) * 0.125
            q_buf[rows_of(b), i * TILE : (i + 1) * TILE] = q.astype(BF)
        key = turn(qkv[:, 2 * TILE : 3 * TILE], c, s)
        value = qkv[:, 3 * TILE :]
        key = jnp.where(kv_head == 0, key, pltpu.roll(key, HD, 1))
        value = jnp.where(kv_head == 1, value, pltpu.roll(value, HD, 1))
        kv_all[z, b, :, :] = jnp.where(low_lane, key, value).astype(BF)
        ids[z, pl.ds(b, 1), :] = tb[b, 1:2, :]

    qkv_block(0)
    for k in (1, 2, 3):
        gather_take(0, x1, k)

    @pl.loop(1, 4)
    def _(k):
        qkv_block(k)

    z_sem = [[next(sems) for _ in range(2)] for _ in range(3)]
    for k in (1, 2, 3):
        remote(kv_all.at[z], kv_all.at[z], z_sem[k - 1][0], column(k)).start()
        remote(ids.at[z], ids.at[z], z_sem[k - 1][1], column(k)).start()
    for k in (1, 2, 3):
        zz = flip(z, k)
        remote(kv_all.at[zz], kv_all.at[zz], z_sem[k - 1][0], column(k)).wait_recv()
        remote(ids.at[zz], ids.at[zz], z_sem[k - 1][1], column(k)).wait_recv()
    lc.wait()
    weights_wait("u")
    column_each("u", False, lambda cp: cp.start())

    low_keys = lax.broadcasted_iota(jnp.int32, (4 * T, TILE), 1) < HD

    def bias_of(s):
        query_id = ids[z, pl.ds(s, 1), :]
        for j in range(4):
            key_id = jnp.transpose(jnp.broadcast_to(ids[j, pl.ds(s, 1), :], (8, T)))[:, 0:1]
            bias[j * T : (j + 1) * T, :] = jnp.where(key_id <= query_id, 0.0, NEGATIVE).astype(BF)

    def kv_of(s):
        kv = jnp.concatenate([kv_all[j, s, :, :] for j in range(4)], 0).astype(F32)
        turned = pltpu.roll(kv, HD, 1)
        keys = jnp.where(low_keys, kv, turned).astype(BF)
        values = jnp.where(low_keys, turned, kv).astype(BF)
        return kv, keys, values

    def only(v, parity):
        return jnp.where(low_lane if parity == 0 else ~low_lane, v.astype(F32), 0.0).astype(BF)

    @pl.loop(0, 4)
    def _(s):
        bias_of(s)
        kv, keys, _ = kv_of(s)
        values_t = jnp.transpose(kv)[HD:, :].astype(BF)

        for i in range(2):
            mixed = []
            for parity in range(2):
                q = only(q_buf[rows_of(s), i * TILE : (i + 1) * TILE], parity)
                scores = nt(keys, q) + bias[...].astype(F32)
                top = jnp.max(scores, axis=0, keepdims=True)
                raw = jnp.exp(scores - top)
                norm = jnp.sum(raw, axis=0, keepdims=True)
                lse[s, 2 * i + parity : 2 * i + parity + 1, :] = top + jnp.log(norm)
                mixed.append(nn(values_t, raw.astype(BF)) * (1.0 / norm))
            ob[rows_of(s), i * TILE : (i + 1) * TILE] = jnp.transpose(jnp.concatenate(mixed, 0)).astype(BF)

    p_sem = [next(sems) for _ in range(4)][0]
    s_sem = [next(sems) for _ in range(6)]
    COLS = 256
    lows, highs = pl.ds(0, 512), pl.ds(512, 512)

    def pass_first(k):
        return remote(ps.at[3, :, (lows, highs)[k - 1]], rd.at[k - 1], s_sem[k - 1], plane(k))

    def pass_second(k, added):
        cols = (lows, highs)[k - 1 if not added else 2 - k]
        return remote(ps.at[k, :, cols], rr.at[k - 1, :, cols], s_sem[2 * k + added], plane(k))

    def tiles(run):
        @pl.loop(0, H // COLS)
        def _(j):
            run(pl.ds(al(j * COLS, COLS), COLS), j * COLS)

    def core_move(k):
        return remote(ps.at[k], pr.at[k], p_sem + k, core)

    def scatter_first(product):
        @pl.loop(0, 4)
        def _(i):
            k = (7 - i) % 4

            def run(cols, c):
                ps[k, :, cols] = product(flip(f, k), (1 - t) * H + c).astype(BF)

            tiles(run)
            core_move(k).start()

    def scatter_own(product):
        @pl.loop(0, 3)
        def _(i):
            k = (i + 2) % 3 + 1
            core_move(k).wait()

            def run(cols, c):
                ps[k, :, cols] = (product(flip(f, k), t * H + c) + pr[k, :, cols].astype(F32)).astype(BF)

            tiles(run)

            @pl.when(k == 3)
            def _():
                pass_first(1).start()
                pass_first(2).start()

        pass_second(1, 0).start()
        pass_second(2, 0).start()
        core_move(0).wait()

        def run(cols, c):
            yo[:, cols] = product(f, t * H + c) + pr[0, :, cols].astype(F32)

        tiles(run)

    def scatter_steps(product):
        return functools.partial(scatter_first, product), functools.partial(scatter_own, product)

    def scatter_relay():
        for k in (1, 2):
            pass_first(3 - k).wait()
            c = (512, 0)[k - 1]

            @pl.loop(0, T // STEP)
            def _(i):
                ps[k, sub(i), c : c + 512] = (ps[k, sub(i), c : c + 512].astype(F32) + rd[2 - k, sub(i), :].astype(F32)).astype(BF)

            pass_second(k, 1).start()

    def scatter_wait():
        for k in (1, 2):
            for added in (0, 1):
                pass_second(k, added).wait()

    def scattered(i):
        return yo[sub(i), :] + rr[0, sub(i), :].astype(F32) + rr[1, sub(i), :].astype(F32)

    n_sem = [next(sems) for _ in range(3)]

    def core_sums(u):
        remote(ss_own.at[u], ss_other.at[u], n_sem[u], core).start()
        remote(ss_own.at[u], ss_other.at[u], n_sem[u], core).wait()

    weights_wait("o")
    weights_own("o", True)
    for step in scatter_steps(lambda b, c: nn(ob[rows_of(b), :], w_o[:, pl.ds(al(c, COLS), COLS)])):
        step()
    scatter_relay()
    scatter_wait()
    weights_wait("d")
    column_each("d", False, lambda cp: cp.start())

    @pl.loop(0, T // STEP)
    def _(i):
        rows = xv[sub(i), half].astype(F32) + scattered(i)
        hid[sub(i), :] = rows
        ss_own[0, sub(i), :] = jnp.broadcast_to(jnp.sum(rows * rows, axis=-1, keepdims=True), (STEP, TILE))

    core_sums(0)
    gain_one, gain_two = ga[0:1, half], ga[1:2, half]

    @pl.loop(0, T // STEP)
    def _(i):
        scale = lax.rsqrt((ss_own[0, sub(i), 0:1] + ss_other[0, sub(i), 0:1]) * (1.0 / W) + EPSILON)
        r2s[sub(i), :] = jnp.broadcast_to(scale, (STEP, TILE))
        x2[pl.ds(al(f * T + i * STEP, STEP), STEP), half] = (hid[sub(i), :] * scale * gain_two).astype(BF)

    gather_start(2, x2, True)
    gather_forward(2, x2)
    gather_start(1, ct, False, cot_in.at[0, :, half])
    weights_wait("g")
    weights_own("ugd", True)
    column_each("u", True, lambda cp: cp.wait_recv())

    UNITS = 256

    def feed_block(k):
        b = flip(f, k)

        @pl.loop(0, WIN // UNITS)
        def _(j):
            cols = pl.ds(al(j * UNITS, UNITS), UNITS)
            gate = nn(x2[rows_of(b), :], w_g[:, cols])
            up = nn(x2[rows_of(b), :], w_u[:, cols])
            sigma = jax.nn.sigmoid(gate)
            silu = gate * sigma
            act[rows_of(b), cols] = (silu * up).astype(BF)
            dg[rows_of(b), cols] = (up * sigma * (1.0 + gate * (1.0 - sigma))).astype(BF)
            du[rows_of(b), cols] = silu.astype(BF)

    for k in (0, 1, 2):
        gather_take(2, x2, k)

    @pl.loop(0, 3)
    def _(k):
        feed_block(k)

    gather_diagonal(2, x2)
    gather_take(2, x2, 3)
    feed_block(3)
    gather_forward(1, ct)
    gather_diagonal(1, ct)
    for k in (1, 2, 3):
        gather_take(1, ct, k)

    e_sem = {(name, i): [next(sems) for _ in range(3)][0] for name in GROUPS for i in range(2 if name in LAST else 1)}
    e_local = {(name, i): next(local_count) for name in GROUPS for i in range(2 if name in LAST else 1)}

    def kv_place(k):
        return w_u.at[pl.ds(al((k - 1) * 512, 512), 512), pl.ds(0, T)]

    def stage(name, k):
        if name == "d":
            return gs_d.at[pl.ds(al(k * WIN, WIN), WIN), :]
        if name in "gu":
            return ct.at[pl.ds(al((k // 2) * 512, 512), 512), pl.ds(al((k % 2) * H, H), WIN)]
        if name == "o":
            return gs_d.at[pl.ds(al(k * WIN, WIN), T), :]
        return x2.at[pl.ds(al((k // 2) * 512, 512), 512), pl.ds(al((k % 2) * 512 + (0 if name == "q" else T), T), T)]

    def grad_moves(group, k, sender):
        name = group[0]
        buf, begin = stage(name, k), al(starts(sender) * TILE, TILE)
        if name in "dgu":
            parts = [(PART, MAIN - PART), (MAIN, TILE)] if group in LAST else [PARTS[group]]
            if name == "d":
                return [(buf.at[pl.ds(c, size), :], first["d"].at[pl.ds(al(begin + c, TILE), size), :]) for c, size in parts]
            return [(buf.at[:, pl.ds(c, size)], first[name].at[:, pl.ds(al(begin + c, TILE), size)]) for c, size in parts]
        if name == "o":
            return [(buf, first["o"].at[rows_of(sender), :])]
        if name == "q":
            return [(buf, first["q"].at[:, rows_of(sender)])]
        return [(buf, kv_place(k))]

    def grad_send(group, k, act_on):
        for i, (src, dst) in enumerate(grad_moves(group, k, f)):

            def run(i=i, src=src, dst=dst):
                if isinstance(k, int) and k == 0:
                    cp = here(src, dst, e_local[group, i])
                    cp.wait() if act_on == "wait" else cp.start()
                else:
                    cp = remote(src, dst, e_sem[group, i] + k - 1, plane(k))
                    cp.wait_send() if act_on == "wait" else cp.start()

            if i == 0:
                run()
            else:
                pl.when(full(f))(run)

    def grad_take(group):
        for k in (1, 2, 3):
            sender = flip(f, k)
            for i, (src, dst) in enumerate(grad_moves(group, k, sender)):

                def run(i=i, src=src, dst=dst):
                    remote(src, dst, e_sem[group, i] + k - 1, plane(k)).wait_recv()

                if i == 0:
                    run()
                else:
                    pl.when(full(sender))(run)

    def sent(*groups):
        for group in groups:
            for k in (1, 2, 3):
                grad_send(group, k, "wait")

    def block_cols(k):
        return pl.ds(al(flip(f, k) * 512, 512), 512)

    def each_owner(product, *groups):
        @pl.loop(0, 4)
        def _(i):
            k = (i + 1) % 4
            product(k)

            @pl.when(k != 0)
            def _():
                for group in groups:
                    grad_send(group, k, "start")

            @pl.when(k == 0)
            def _():
                for group in groups:
                    if group != "k":
                        grad_send(group, 0, "start")

    def down_grads(group):
        c, size = PARTS[group]

        def product(k):
            stage("d", k)[c : c + size, :] = tn(act[:, c : c + size], ct[:, block_cols(k)]).astype(BF)

        each_owner(product, group)

    def feed_grads(name, which, right):
        c = 0 if which == "A" else PART

        def product(k):
            @pl.loop(0, 2)
            def _(i):
                xs = x2[:, pl.ds(al(flip(f, k) * 512 + i * T, T), T)]
                stage(name, k)[pl.ds(al(i * T, T), T), c : c + PART] = tn(xs, right[:, c : c + PART]).astype(BF)

        each_owner(product, name + which)

    for group in ("dA", "dB", "dC"):
        down_grads(group)

    def feed_back():
        column_each("d", True, lambda cp: cp.wait_recv())

        @pl.loop(0, 4)
        def _(b):
            @pl.loop(0, WIN // UNITS)
            def _(j):
                cols = pl.ds(al(j * UNITS, UNITS), UNITS)
                back = nt(ct[rows_of(b), :], w_d[cols, :])
                dg[rows_of(b), cols] = (back * dg[rows_of(b), cols].astype(F32)).astype(BF)
                du[rows_of(b), cols] = (back * du[rows_of(b), cols].astype(F32)).astype(BF)

    def gate_A():
        gather_drain(1, ct, False, cot_in.at[0, :, half])
        feed_grads("g", "A", dg)

    d2_first, d2_own = scatter_steps(
        lambda b, c: nt(dg[rows_of(b), :], w_g[pl.ds(al(c, COLS), COLS), :]) + nt(du[rows_of(b), :], w_u[pl.ds(al(c, COLS), COLS), :])
    )

    end = (z == 0) | (z == 3)
    middle = (z == 1) | (z == 2)
    next_in = (f, jnp.where(z < 2, 1, 2), t)
    next_out = (f, jnp.where(z < 2, 0, 3), t)
    facing = (f, 3 - z, t)
    across = [next(sems) for _ in range(2 * DEPTH)]
    l_sem = [[s, across[i % (2 * DEPTH)], s] for i, s in enumerate([next(sems) for _ in CHUNKS])]
    v_sem = [next(local_count) for _ in range(2)]
    o_sem = [next(local_count) for _ in range(4)]

    la, lb, *rest_of_line = (line.at[i] for i in range(8))
    tt, ring = rest_of_line[:2], rest_of_line[2:]

    kept, given = (w_g.at[:, pl.ds(512 + j * TILE, TILE)] for j in range(2))
    even = f % 2 == 0

    def pair_rows(pair, j):
        return pl.ds(j * 512 + pair * T, T)


    def window(arrays, i):
        group, name, r, c, rows, cols = CHUNKS[i]
        if name in "dgu":
            j = flip(r, t) if group in LAST else r
            at = al(starts(j) * TILE + PARTS[group][0], TILE)
            r, c = (at, 0) if name == "d" else (0, at)
        return arrays[name].at[pl.ds(r, rows), pl.ds(c, cols)]

    def line_send(group):
        @pl.when(end)
        def _():
            for i, chunk in enumerate(CHUNKS):
                if chunk[0] == group:
                    remote(window(first, i), window(left, i), l_sem[i][0], next_in).start()

    def add_into(dst, a, b, rows, cols):
        @pl.loop(0, rows // STEP)
        def _(i):
            at = sub(i)
            dst[at, pl.ds(0, cols)] = (a[at, pl.ds(0, cols)].astype(F32) + b[at, pl.ds(0, cols)].astype(F32)).astype(BF)

    def line_one(i):
        _, name, r, c, rows, cols = CHUNKS[i]
        part = (pl.ds(0, rows), pl.ds(0, cols))
        a, b, keep = la.at[part], lb.at[part], ring[i % DEPTH]

        @pl.when(middle)
        def _():
            get_a = here(window(first, i), a, v_sem[0])
            get_a.start()
            remote(window(first, i), window(left, i), l_sem[i][0], next_in).wait_recv()
            get_b = here(window(left, i), b, v_sem[1])
            get_b.start()
            get_a.wait()
            get_b.wait()
            add_into(keep, la, lb, rows, cols)
            remote(keep.at[part], window(cross, i), l_sem[i][1], facing).start()

    def line_two(i):
        _, name, r, c, rows, cols = CHUNKS[i]
        part = (pl.ds(0, rows), pl.ds(0, cols))
        keep, done = ring[i % DEPTH], tt[i % 2]

        @pl.when(middle)
        def _():
            remote(keep.at[part], window(cross, i), l_sem[i][1], facing).wait()
            get = here(window(cross, i), lb.at[part], v_sem[1])
            get.start()
            if i >= 2:
                line_out(i - 2)
            get.wait()
            add_into(done, keep, lb, rows, cols)
            remote(done.at[part], window(total, i), l_sem[i][2], next_out).start()
            here(done.at[part], window(total, i), o_sem[i % 4]).start()

    def line_out(i):
        _, name, r, c, rows, cols = CHUNKS[i]
        done = tt[i % 2].at[pl.ds(0, rows), pl.ds(0, cols)]
        remote(done, window(total, i), l_sem[i][2], next_out).wait_send()
        here(done, window(total, i), o_sem[i % 4]).wait()

    pumped, ready = [0, 0], set()

    def ahead():
        i = pumped[0]
        assert CHUNKS[i][0] in ready and i < pumped[1] + DEPTH
        line_one(i)
        pumped[0] += 1

    def behind():
        i = pumped[1]
        assert i < pumped[0]
        line_two(i)
        pumped[1] += 1

    def grad_ready(group):
        grad_take(group)
        grad_send(group, 0, "wait")
        line_send(group)
        ready.add(group)

    g_sum[...] = jnp.zeros((8, H), F32)
    k_sem = [next(sems) for _ in range(3)]
    q_sem = [[next(sems) for _ in range(3)] for _ in range(2)]
    d_ob, d_qkv = ob, dg
    here_half = (lane // HD) == kv_head
    out_local = here(out_s, out_ref.at[:, half], next(local_count))
    out_remote = remote(out_s, out_ref.at[:, half], next(sems), core)
    in_local = here(d_hid, in_grad_ref.at[:, half], next(local_count))
    in_remote = remote(d_hid, in_grad_ref.at[:, half], next(sems), core)
    kv_copy = here(x2.at[pl.ds(0, 512), pl.ds(T, T)], first["k"], next(local_count))
    whole_move = remote(g_whole.at[:, half], g_whole.at[:, half], next(sems), core)
    gain_move = here(g_whole.at[:, pl.ds(al(f * 512, 512), 512)], gain_ref, next(local_count))

    def norm_two_back():
        lh.wait()
        scatter_wait()

        def rows_back(i, carry):
            rows = scattered(i)
            yo[sub(i), :] = rows
            hat = hid[sub(i), :] * r2s[sub(i), 0:1]
            ss_own[1, sub(i), :] = jnp.broadcast_to(jnp.sum(rows * gain_two * hat, axis=-1, keepdims=True), (STEP, TILE))
            return carry + jnp.sum(rows * hat, axis=0, keepdims=True)

        g_sum[1:2, :] = lax.fori_loop(0, T // STEP, rows_back, jnp.zeros((1, H), F32))
        core_sums(1)

        @pl.loop(0, T // STEP)
        def _(i):
            scale = r2s[sub(i), 0:1]
            hat = hid[sub(i), :] * scale
            mean = (ss_own[1, sub(i), 0:1] + ss_other[1, sub(i), 0:1]) * (1.0 / W)
            rows = out_s[sub(i), :].astype(F32) + scale * (yo[sub(i), :] * gain_two - hat * mean)
            d_hid[sub(i), :] = rows
            dh[pl.ds(al(f * T + i * STEP, STEP), STEP), half] = rows.astype(BF)

        column_each("u", False, lambda cp: cp.wait_send())
        gather_start(3, dh, True)

    def dh_take():
        gather_forward(3, dh)
        for k in range(4):
            gather_take(3, dh, k)

    def out_grads():
        sent("dA", "dB", "dC")

        def product(k):
            stage("o", k)[...] = tn(ob[...], dh[:, block_cols(k)]).astype(BF)

        each_owner(product, "o")

        @pl.loop(0, 4)
        def _(b):
            ob[rows_of(b), :] = nt(dh[rows_of(b), :], w_o[...]).astype(BF)

    def attend_back(pair, i_seq):
        s = 2 * pair + i_seq
        bias_of(s)
        kv, keys, values = kv_of(s)
        keys_t = jnp.transpose(kv)[:HD, :].astype(BF)
        c, sn = turns(s)
        d_key = jnp.zeros((4 * T, TILE), F32)
        d_value = jnp.zeros((4 * T, TILE), F32)
        for i in range(2):
            d_query = []
            for parity in range(2):
                q = only(q_buf[rows_of(s), i * TILE : (i + 1) * TILE], parity)
                do = only(d_ob[rows_of(s), i * TILE : (i + 1) * TILE], parity)
                weights = jnp.exp(nt(keys, q) + bias[...].astype(F32) - lse[s, 2 * i + parity : 2 * i + parity + 1, :])
                d_weights = nt(values, do)
                delta = jnp.sum(weights * d_weights, axis=0, keepdims=True)
                d_scores = (weights * (d_weights - delta)).astype(BF)
                d_value = d_value + nn(weights.astype(BF), do)
                d_key = d_key + nn(d_scores, q)
                d_query.append(nn(keys_t, d_scores))
            d_query = jnp.transpose(jnp.concatenate(d_query, 0)) * 0.125
            d_qkv[rows_of(s), i * TILE : (i + 1) * TILE] = turn(d_query, c, -sn).astype(BF)
        d_key = d_key + pltpu.roll(d_key, HD, 1)
        d_value = d_value + pltpu.roll(d_value, HD, 1)
        keep, give = jnp.where(even, d_key, d_value), jnp.where(even, d_value, d_key)
        mine_here = lane // HD == i_seq
        for j in range(4):
            for place, values in ((kept, keep), (given, give)):
                at = pair_rows(pair, j)
                place[at, :] = jnp.where(mine_here, values[j * T : (j + 1) * T, :], place[at, :].astype(F32)).astype(BF)

    d_kv_pair = w_u.at[:, pl.ds(T, TILE)]
    pair_move = remote(given, d_kv_pair, next(sems), plane(1))

    def pair_sum():
        pair_move.wait()

        @pl.loop(0, W // STEP)
        def _(i):
            rows = kept[sub(i), :].astype(F32) + d_kv_pair[sub(i), :].astype(F32)
            kept[sub(i), :] = rows.astype(BF)

            @pl.when(i // (512 // STEP) == z)
            def _():
                d_kv[pl.ds(al(i % (512 // STEP) * STEP, STEP), STEP), :] = rows

        for move in d_kv_moves():
            move.start()

    def d_kv_moves():
        return [remote(kept.at[pl.ds(al(flip(z, k) * 512, 512), 512), :], d_kv_recv.at[k - 1], k_sem[k - 1], column(k)) for k in (1, 2, 3)]

    def up_A():
        sent("gA", "gB")
        feed_grads("u", "A", du)

    def d_kv_take():
        for move in d_kv_moves():
            move.wait()

        for s in range(4):
            c, sn = turns(s)
            rows = pl.ds(s // 2 * T, T)
            whole = d_kv[rows, :]
            for k in range(3):
                whole = whole + d_kv_recv[k, rows, :].astype(F32)
            turned = pltpu.roll(whole, HD, 1)
            whole = jnp.where(low_lane, whole, turned) if s % 2 == 0 else jnp.where(low_lane, turned, whole)
            d_qkv[rows_of(s), 2 * TILE : 3 * TILE] = jnp.where(here_half & even, turn(whole, c, -sn), 0.0).astype(BF)
            d_qkv[rows_of(s), 3 * TILE : 4 * TILE] = jnp.where(here_half & ~even, whole, 0.0).astype(BF)

    def qkv_grads():
        gather_drain(2, x2, True)

        def product(k):
            @pl.loop(0, 2)
            def _(i):
                xs = x1[:, pl.ds(al(flip(f, k) * 512 + i * T, T), T)]
                grads = tn(xs, d_qkv[:, 0:512]).astype(BF)
                stage("q", k)[pl.ds(al(i * T, T), T), :] = grads[:, 0:T]
                stage("k", k)[pl.ds(al(i * T, T), T), :] = grads[:, T:]

        each_owner(product, "q", "k")

    d1_first, d1_own = scatter_steps(lambda b, c: nt(d_qkv[rows_of(b), 0:512], w_qkv[pl.ds(al(c, COLS), COLS), :]))
    out_first, out_own = scatter_steps(lambda b, c: nn(act[rows_of(b), :], w_d[:, pl.ds(al(c, COLS), COLS)]))

    def kv_ready():
        grad_take("k")

        @pl.loop(0, 512 // STEP)
        def _(i):
            rows = x2[sub(i), T : 2 * T].astype(F32)
            for k in (1, 2, 3):
                rows = rows + kv_place(k)[sub(i), :].astype(F32)
            x2[sub(i), T : 2 * T] = rows.astype(BF)

        kv_copy.start()
        kv_copy.wait()
        line_send("k")
        ready.add("k")

    def norm_one_back():
        scatter_wait()

        def rows_back(i, carry):
            rows = scattered(i)
            yo[sub(i), :] = rows
            hat = xv[sub(i), half].astype(F32) * r1s[sub(i), 0:1]
            ss_own[2, sub(i), :] = jnp.broadcast_to(jnp.sum(rows * gain_one * hat, axis=-1, keepdims=True), (STEP, TILE))
            return carry + jnp.sum(rows * hat, axis=0, keepdims=True)

        g_sum[0:1, :] = lax.fori_loop(0, T // STEP, rows_back, jnp.zeros((1, H), F32))
        for k in (1, 2, 3):
            pl.semaphore_signal(credit, inc=1, device_id=plane(k), device_id_type=MESH)
        pl.semaphore_signal(credit, inc=1, device_id=core, device_id_type=MESH)
        core_sums(2)
        g_plane[f, :, :] = g_sum[...]
        for k in (1, 2, 3):
            remote(g_sum, g_plane.at[f], q_sem[0][k - 1], plane(k)).start()

        @pl.loop(0, T // STEP)
        def _(i):
            scale = r1s[sub(i), 0:1]
            hat = xv[sub(i), half].astype(F32) * scale
            mean = (ss_own[2, sub(i), 0:1] + ss_other[2, sub(i), 0:1]) * (1.0 / W)
            d_hid[sub(i), :] = d_hid[sub(i), :] + scale * (yo[sub(i), :] * gain_one - hat * mean)

        in_local.start()
        in_remote.start()

    def out_begin():
        pl.semaphore_wait(credit, 4)
        out_first()

    def out_end():
        scatter_wait()

        @pl.loop(0, T // STEP)
        def _(i):
            out_s[sub(i), :] = (hid[sub(i), :] + scattered(i)).astype(BF)

        out_local.start()
        out_remote.start()

    def gains_column():
        for k in (1, 2, 3):
            remote(g_sum, g_plane.at[flip(f, k)], q_sem[0][k - 1], plane(k)).wait_recv()
        g_column[z, :, :] = ((g_plane[0, :, :] + g_plane[1, :, :]) + g_plane[2, :, :]) + g_plane[3, :, :]
        for k in (1, 2, 3):
            remote(g_column.at[z], g_column.at[z], q_sem[1][k - 1], column(k)).start()

    def gains_end():
        for k in (1, 2, 3):
            remote(g_column.at[z], g_column.at[flip(z, k)], q_sem[1][k - 1], column(k)).wait_recv()
        g_whole[:, half] = ((g_column[0, :, :] + g_column[1, :, :]) + g_column[2, :, :]) + g_column[3, :, :]
        whole_move.start()
        whole_move.wait()
        gain_move.start()

    steps = {
        "feed_back": feed_back,
        "gate_A": gate_A,
        "d2_first": d2_first,
        "d2_own": d2_own,
        "gate_B": lambda: feed_grads("g", "B", dg),
        "up_A": up_A,
        "up_B": lambda: feed_grads("u", "B", du),
        "relay": scatter_relay,
        "norm_two_back": norm_two_back,
        "dh_take": dh_take,
        "out_grads": out_grads,
        "pair_send": lambda: pair_move.start(),
        "pair_sum": pair_sum,
        "d_kv_take": d_kv_take,
        "qkv_grads": qkv_grads,
        "d1_first": d1_first,
        "d1_own": d1_own,
        "kv_ready": kv_ready,
        "norm_one_back": norm_one_back,
        "out_first": out_begin,
        "out_own": out_own,
        "out_end": out_end,
        "gains_column": gains_column,
        "gains_end": gains_end,
    }
    for step in ORDER:
        if step == "+":
            ahead()
        elif step == "-":
            behind()
        elif step == 1:
            ahead()
            behind()
        elif step in GROUPS:
            grad_ready(step)
        elif step[:6] == "attend":
            attend_back(int(step[6]) // 2, int(step[6]) % 2)
        else:
            steps[step]()
    while pumped[0] < len(CHUNKS):
        ahead()
        behind()
    while pumped[1] < len(CHUNKS):
        behind()

    @pl.when(middle)
    def _():
        line_out(len(CHUNKS) - 2)
        line_out(len(CHUNKS) - 1)

    @pl.when(end)
    def _():
        for i in range(len(CHUNKS)):
            remote(window(first, i), window(left, i), l_sem[i][0], next_in).wait_send()
            remote(window(total, i), window(total, i), l_sem[i][2], next_in).wait_recv()

    gain_move.wait()
    out_local.wait()
    out_remote.wait()
    in_local.wait()
    in_remote.wait()
    weights_drain()
    column_each("d", False, lambda cp: cp.wait_send())
    column_each("qkv", False, lambda cp: cp.wait_send())
    gather_drain(0, x1, False)
    gather_drain(3, dh, True)
    for k in (1, 2, 3):
        remote(own_gain, own_gain, a_sem[k - 1], plane(k)).wait_send()
        remote(tb.at[f], tb.at[f], t_sem[k - 1], plane(k)).wait_send()
        remote(kv_all.at[z], kv_all.at[z], z_sem[k - 1][0], column(k)).wait_send()
        remote(ids.at[z], ids.at[z], z_sem[k - 1][1], column(k)).wait_send()
        remote(g_sum, g_plane.at[f], q_sem[0][k - 1], plane(k)).wait_send()
        remote(g_column.at[z], g_column.at[z], q_sem[1][k - 1], column(k)).wait_send()
        for name in ("uA", "uB", "o", "q", "k"):
            grad_send(name, k, "wait")
    assert (next(sems), next(local_count)) == (REMOTE_SEMS, LOCAL_SEMS)


REMOTE_SEMS, LOCAL_SEMS = 206, 36


def layer_call(inputs, positions, blocks, cotangent, attn_gain, w_query, w_key, w_value, w_out, mlp_gain, w_gate, w_up, w_down):
    shape = jax.ShapeDtypeStruct
    grads = [shape((rows, cols), BF) for _, rows, cols in GRADS]
    any_spec = pl.BlockSpec(memory_space=pl.ANY)
    v = pltpu.VMEM
    results = pl.pallas_call(
        layer_kernel,
        out_shape=[shape((T, W), BF), shape((T, W), F32), shape((8, 512), F32)] + grads * 4,
        in_specs=[any_spec] + [pl.BlockSpec(memory_space=pltpu.VMEM)] * 4 + [any_spec] * 8,
        out_specs=[any_spec] * 27,
        scratch_shapes=[
            v((4 * T, W), BF), v((4 * T, W), BF), v((4 * T, W), BF), v((4 * T, W), BF),
            v((W, 512), BF), v((T, W), BF), v((W, WIN), BF), v((W, WIN), BF), v((WIN, W), BF),
            v((4 * T, WIN), BF), v((4 * T, WIN), BF), v((4 * T, WIN), BF),
            v((4 * T, T), BF), v((4, 4, T, TILE), BF), v((4 * T, T), BF),
            v((4, T, H), BF), v((4, T, H), BF), v((2, T, H), BF), v((2, T, 512), BF), v((T, H), F32), v((T, H), F32), v((T, H), F32), v((T, W), BF),
            v((4, 8, T), F32), v((8, W), F32), v((4, 8, T), F32), v((T, TILE), F32), v((T, TILE), F32),
            v((3, T, TILE), F32), v((3, T, TILE), F32), v((4, 8, T), F32), v((4 * T, T), BF),
            v((4 * WIN, 512), BF), v((8, 512, 512), BF), v((4, 2, T, TILE), F32),
            v((512, TILE), F32), v((3, 512, TILE), BF),
            v((T, H), BF), v((8, H), F32), v((4, 8, H), F32), v((4, 8, H), F32), v((8, W), F32),
            pltpu.SemaphoreType.DMA((REMOTE_SEMS,)), pltpu.SemaphoreType.DMA((REMOTE_SEMS,)),
            pltpu.SemaphoreType.DMA((LOCAL_SEMS,)), pltpu.SemaphoreType.REGULAR,
        ],
        compiler_params=pltpu.CompilerParams(collective_id=0, has_side_effects=True, vmem_limit_bytes=62 << 20),
    )(inputs, positions, blocks, attn_gain, mlp_gain, cotangent, w_query, w_key, w_value, w_out, w_gate, w_up, w_down)
    return finish(*results[:3], *results[-6:])


def finish_kernel(*refs):
    output, input_grad, gains, down, gate, up, out, query, kv = refs[:9]
    targets = refs[9:]
    for source, target in zip((output, input_grad), targets):
        target[0] = source[...]
    attn_target, q_target, k_target, v_target, o_target, mlp_target, g_target, u_target, d_target = targets[2:]
    attn_target[...] = gains[0:1, :]
    mlp_target[...] = gains[1:2, :]
    k_target[...] = kv[:, :TILE].astype(F32)
    v_target[...] = kv[:, TILE:].astype(F32)
    for source, target in ((query, q_target), (out, o_target), (gate, g_target), (up, u_target), (down, d_target)):
        target[...] = source[...].astype(F32)


def finish(output, input_grad, gains, down, gate, up, out, query, kv):
    parts = 2
    shape = jax.ShapeDtypeStruct

    def rows(count, cols):
        return pl.BlockSpec((count // parts, cols), lambda i: (i, 0))

    def page(count, cols):
        return pl.BlockSpec((1, count // parts, cols), lambda i: (0, i, 0))

    line = pl.BlockSpec((1, 512), lambda i: (0, 0))
    results = pl.pallas_call(
        finish_kernel,
        grid=(parts,),
        in_specs=[rows(T, W), rows(T, W), pl.BlockSpec((8, 512), lambda i: (0, 0))] + [rows(*a.shape) for a in (down, gate, up, out, query, kv)],
        out_specs=[page(T, W), page(T, W), line, rows(512, 1024), rows(512, TILE), rows(512, TILE), rows(1024, 512), line, rows(512, 2816), rows(512, 2816), rows(2816, 512)],
        out_shape=[shape((1, T, W), BF), shape((1, T, W), F32), shape((1, 512), F32)]
        + [shape(a, F32) for a in ((512, 1024), (512, TILE), (512, TILE), (1024, 512), (1, 512), (512, 2816), (512, 2816), (2816, 512))],
        compiler_params=pltpu.CompilerParams(dimension_semantics=("arbitrary",)),
    )(output, input_grad, gains, down, gate, up, out, query, kv)
    results = list(results)
    results[2], results[7] = results[2][0], results[7][0]
    return tuple(results)


def solution(mesh):
    n, m = mesh.shape["fsdp"], mesh.shape["ctx"]

    def step(*args):
        return layer_call(*args) if n == m == 4 else local(n, m, *args)

    return jax.shard_map(
        step,
        mesh=mesh,
        in_specs=(
            P("fsdp", "ctx", None),
            P("fsdp", "ctx"),
            P("fsdp", "ctx"),
            P("fsdp", "ctx", None),
            P("fsdp"),
            P("fsdp", "tp"),
            P("fsdp", "tp"),
            P("fsdp", "tp"),
            P("tp", "fsdp"),
            P("fsdp"),
            P("fsdp", "tp"),
            P("fsdp", "tp"),
            P("tp", "fsdp"),
        ),
        out_specs=(
            P("fsdp", "ctx", None),
            P("fsdp", "ctx", None),
            P("fsdp"),
            P("fsdp", "tp"),
            P("fsdp", "tp"),
            P("fsdp", "tp"),
            P("tp", "fsdp"),
            P("fsdp"),
            P("fsdp", "tp"),
            P("fsdp", "tp"),
            P("tp", "fsdp"),
        ),
        check_vma=False,
    )
```
